32 devices in a mesh: ctx: 8 (over z, x), fsdp: 4 (over y, core).
Axes of the slice: x: 2, y: 2, z: 4, core: 2. Of those that a mesh axis runs over, the one named last changes fastest.
Arguments:
- hidden: bfloat16 [4, 1024, 768], P('fsdp', 'ctx'), may hold values from -6 to 6
- neighbours: bfloat16 [4, 16, 256, 768], P('fsdp', 'ctx'), may hold values from -6 to 6
- cotangent: bfloat16 [4, 1024, 768], P('fsdp', 'ctx'), may hold values from -6 to 6
- stretch_deal: int32 [4, 16], P('fsdp'), may hold values from 0 to 15, as said below
- seq_lengths: int32 [4, 3], P('fsdp'), may hold values from 1 to 8, 16 in all within a row
- norm_gains: bfloat16 [3, 768], P(None, 'fsdp'), may hold values from 0.5 to 1.5
- attn_qkv: bfloat16 [768, 2304], P('fsdp'), may hold values from -0.21875 to 0.21875
- attn_out: bfloat16 [768, 768], P('fsdp'), may hold values from -1.5 to 1.5
- cross_q: bfloat16 [768, 768], P('fsdp'), may hold values from -0.21875 to 0.21875
- cross_kv: bfloat16 [768, 1536], P('fsdp'), may hold values from -0.21875 to 0.21875
- cross_out: bfloat16 [768, 768], P('fsdp'), may hold values from -0.875 to 0.875
- mlp_in: bfloat16 [768, 3072], P('fsdp'), may hold values from -0.21875 to 0.21875
- mlp_out: bfloat16 [3072, 768], P('fsdp'), may hold values from -0.109375 to 0.109375
Outputs:
- layer_out: float32 [4, 1024, 768], P('fsdp', 'ctx')
- grad_hidden: float32 [4, 1024, 768], P('fsdp', 'ctx')
- grad_neighbours: float32 [4, 16, 256, 768], P('fsdp', 'ctx')
- grad_norm_gains: float32 [3, 768], P(None, 'fsdp')
- grad_attn_qkv: float32 [768, 2304], P('fsdp')
- grad_attn_out: float32 [768, 768], P('fsdp')
- grad_cross_q: float32 [768, 768], P('fsdp')
- grad_cross_kv: float32 [768, 1536], P('fsdp')
- grad_cross_out: float32 [768, 768], P('fsdp')
- grad_mlp_in: float32 [768, 3072], P('fsdp')
- grad_mlp_out: float32 [3072, 768], P('fsdp')
The draws below stay inside these ranges and needn't reach their ends.
Inputs may be any that keep to these rules, and one draw needn't show every extreme that they name: `stretch_deal`: each row is a permutation of the 16 stretches of a group; the 2 slots of one device hold a block of 1 given stretches in a row, then the mirror block counted from the group's end. `seq_lengths`: A row holds the lengths of a group's sequences, which fill its 16 stretches in given order.
All inputs are finite; a program needn't handle non-finite values.
Results may differ from the reference program's by a relative error of at most 0.025.
Values may be sent and summed in bfloat16 or wider, within the bound.
No kernel may reach another device: no remote copies, remote signals or barrier semaphores. Data moves between devices by JAX's collectives and lax.ppermute only.
A program may use at most 256 MiB of HBM per device.

```python
import math
import jax
import jax.numpy as jnp
import numpy as np
from jax import lax

D = 768
H = 12
HD = 64
FF = 3072
STRETCH = 64
CH_DEV = 2
MAXCH = 64
GROUPS = 4
GROUP_CH = 16
GROUP_TOK = 1024
NKEYS = 256
MOST = 8
SEQS = 3


def draw_stretch_deal(key, part):
    device_count = GROUP_CH // CH_DEV
    half_slots = CH_DEV // 2
    slot_ids = jnp.arange(CH_DEV, dtype=jnp.int32)
    deal_rows = []
    for group_index in range(GROUPS):
        device_order = jax.random.permutation(jax.random.fold_in(key, 17 + group_index), device_count).astype(jnp.int32)
        block_ids = jnp.where(slot_ids[None, :] < half_slots, device_order[:, None], 2 * device_count - 1 - device_order[:, None])
        deal_rows.append((block_ids * half_slots + slot_ids[None, :] % half_slots).reshape(GROUP_CH))
    return jnp.stack(deal_rows).astype(jnp.int32)


def levels(stream_key, extent, shards, smallest, top_value):
    level, own = 1.0, jax.random.fold_in(stream_key, 6)
    for dim, parts in shards:
        draws = jnp.exp(jax.random.uniform(jax.random.fold_in(own, dim), (parts,), jnp.float32, smallest / len(shards), top_value / len(shards)))
        level = level * jnp.repeat(draws, extent[dim] // parts).reshape([-1 if axis == dim else 1 for axis in range(len(extent))])
    return level


def length_profile(number_of, total, most, slope):
    loads = [(1 << 20) // math.isqrt(grade ** slope) + 1 for grade in range(2, number_of + 1)]
    rest, holding = total - most - (number_of - 1), [1] * (number_of - 1)
    while rest > 0:
        candidates = [i for i in range(number_of - 1) if holding[i] < most]
        whole, budget = sum([loads[i] for i in candidates]), rest
        for i in candidates:
            addition = min(most - holding[i], max(1, budget * loads[i] // whole), rest)
            holding[i] = holding[i] + addition
            rest = rest - addition
    return np.array([most] + holding)


def uneven(stream_key, count, total, bound, lean):
    if count == 2:
        one = jax.random.randint(stream_key, (), max(1, total - bound), min(bound, total - 1) + 1)
        return jnp.stack([one, total - one])
    sizes = jnp.asarray(length_profile(count, total, bound, lean), jnp.int32)
    couples = (count - 1) // 2
    giver, taker = sizes[1:1 + 2 * couples:2], sizes[2:2 + 2 * couples:2]
    room = jnp.minimum(giver - 1, bound - taker)
    passed = jax.random.randint(jax.random.fold_in(stream_key, 1), (couples,), 0, 1 << 20) % (room + 1)
    sizes = sizes.at[1:1 + 2 * couples:2].set(giver - passed).at[2:2 + 2 * couples:2].set(taker + passed)
    return sizes[jax.random.permutation(jax.random.fold_in(stream_key, 2), count)]


def noise(own_key, shape, deviation, reach, split=(), kind=jnp.bfloat16):
    entries = jax.random.normal(own_key, shape, jnp.float32) * deviation
    if len(split) > 0:
        entries = levels(own_key, shape, split, -0.22, 0.18) * entries
    return jnp.clip(entries, min=-reach, max=reach).astype(kind)


def setup_inputs(seed: int = 0) -> dict:
    keys = jax.random.split(jax.random.key(seed), 14)
    hidden = noise(keys[0], (GROUPS, GROUP_TOK, D), 1.0, 6.0, ((0, 4), (1, 8)))
    neighbours = noise(keys[1], (GROUPS, GROUP_CH, NKEYS, D), 1.0, 6.0, ((0, 4), (1, 8)))
    cotangent = noise(keys[2], (GROUPS, GROUP_TOK, D), 1.0, 6.0, ((0, 4), (1, 8)))
    stretch_deal = draw_stretch_deal(jax.random.fold_in(keys[13], 71), 0)
    seq_lengths = jax.vmap(lambda own: uneven(own, SEQS, GROUP_CH, MOST, 2))(jax.random.split(keys[4], GROUPS)).reshape((GROUPS, SEQS)).astype(jnp.int32)
    norm_gains = jnp.clip(1.0 + 0.1 * jax.random.normal(keys[5], (3, D), jnp.float32), 0.5, 1.5).astype(jnp.bfloat16)
    attn_qkv = noise(keys[6], (D, 3 * D), D ** -0.5, 0.21875, ((0, 4),))
    attn_out = noise(keys[7], (D, D), (D // 48) ** -0.5, 1.5, ((0, 4),))
    cross_q = noise(keys[8], (D, D), D ** -0.5, 0.21875, ((0, 4),))
    cross_kv = noise(keys[9], (D, 2 * D), D ** -0.5, 0.21875, ((0, 4),))
    cross_out = noise(keys[10], (D, D), (D // 16) ** -0.5, 0.875, ((0, 4),))
    mlp_in = noise(keys[11], (D, FF), D ** -0.5, 0.21875, ((0, 4),))
    mlp_out = noise(keys[12], (FF, D), FF ** -0.5, 0.109375, ((0, 4),))
    return {"hidden": hidden, "neighbours": neighbours, "cotangent": cotangent, "stretch_deal": stretch_deal, "seq_lengths": seq_lengths, "norm_gains": norm_gains, "attn_qkv": attn_qkv, "attn_out": attn_out, "cross_q": cross_q, "cross_kv": cross_kv, "cross_out": cross_out, "mlp_in": mlp_in, "mlp_out": mlp_out}


NORM_EPS = 1e-06
MASKED_SCORE = -1e+30
HIGHEST_PRECISION = lax.Precision.HIGHEST

@jax.custom_vjp
def low(v):
    return lax.optimization_barrier(v.astype(jnp.bfloat16)).astype(jnp.float32)

@jax.custom_vjp
def low_back(v):
    return v

def low_keep(v):
    return (low(v), None)

def low_pass(kept, grad):
    return (grad,)

def back_keep(v):
    return (v, None)

def back_low(kept, grad):
    return (low(grad),)
low.defvjp(low_keep, low_pass)
low_back.defvjp(back_keep, back_low)

def rms_norm(values, norm_gain):
    return values * lax.rsqrt(lax.optimization_barrier(jnp.mean(values * values, axis=-1, keepdims=True)) + NORM_EPS) * norm_gain

def matmul(left, right):
    return jnp.dot(left, right, preferred_element_type=jnp.float32, precision=HIGHEST_PRECISION)

def self_block(query_rows, keys_pad, values_pad, seq_rows, seq_pad, block_index):
    block_rows = 8 * STRETCH
    key_span = MAXCH * STRETCH + block_rows
    row_start = block_index * block_rows
    query_heads = lax.dynamic_slice_in_dim(query_rows, row_start, block_rows).reshape(block_rows, H, HD)
    key_heads = lax.dynamic_slice_in_dim(keys_pad, row_start, key_span).reshape(key_span, H, HD)
    value_heads = lax.dynamic_slice_in_dim(values_pad, row_start, key_span).reshape(key_span, H, HD)
    query_seq = lax.dynamic_slice_in_dim(seq_rows, row_start, block_rows)
    key_seq = lax.dynamic_slice_in_dim(seq_pad, row_start, key_span)
    query_pos = row_start + jnp.arange(block_rows, dtype=jnp.int32)
    key_pos = row_start - MAXCH * STRETCH + jnp.arange(key_span, dtype=jnp.int32)
    visible = (query_seq[:, None] == key_seq[None, :]) & (key_pos[None, :] <= query_pos[:, None])
    scores = low_back(jnp.einsum('qhd,khd->hqk', query_heads, key_heads, precision=HIGHEST_PRECISION) * HD ** (-0.5))
    scores = jnp.where(visible[None], scores, MASKED_SCORE)
    attn_probs = low(jax.nn.softmax(scores, axis=-1))
    return jnp.einsum('hqk,khd->qhd', attn_probs, value_heads, precision=HIGHEST_PRECISION).reshape(block_rows, H * HD)

def cross_block(query_block, enc_block, w_kv):
    stretch_count = query_block.shape[0]
    projected = low(low_back(matmul(enc_block.reshape(-1, D), w_kv)))
    key_heads = projected[:, :D].reshape(stretch_count, NKEYS, H, HD)
    value_heads = projected[:, D:].reshape(stretch_count, NKEYS, H, HD)
    query_heads = query_block.reshape(stretch_count, STRETCH, H, HD)
    scores = low_back(jnp.einsum('cqhd,ckhd->chqk', query_heads, key_heads, precision=HIGHEST_PRECISION) * HD ** (-0.5))
    attn_probs = low(jax.nn.softmax(scores, axis=-1))
    return jnp.einsum('chqk,ckhd->cqhd', attn_probs, value_heads, precision=HIGHEST_PRECISION).reshape(stretch_count, STRETCH, H * HD)

def reference(hidden, neighbours, cotangent, stretch_deal, seq_lengths, norm_gains, attn_qkv, attn_out, cross_q, cross_kv, cross_out, mlp_in, mlp_out):
    total_ch = GROUPS * GROUP_CH
    total_tok = total_ch * STRETCH
    group_base = (jnp.arange(GROUPS, dtype=jnp.int32) * GROUP_CH)[:, None]
    given_at_slot = (stretch_deal.astype(jnp.int32) + group_base).reshape(total_ch)
    slot_of_given = jnp.zeros((total_ch,), jnp.int32).at[given_at_slot].set(jnp.arange(total_ch, dtype=jnp.int32))
    seq_ends = jnp.cumsum(seq_lengths.astype(jnp.int32), axis=1)
    seq_starts = seq_ends - seq_lengths.astype(jnp.int32)
    local_stretch = jnp.arange(GROUP_CH, dtype=jnp.int32)
    seq_local = lax.optimization_barrier(jnp.sum((seq_ends[:, None, :] <= local_stretch[None, :, None]).astype(jnp.int32), axis=2))
    seq_stretch = (seq_local + jnp.arange(GROUPS, dtype=jnp.int32)[:, None] * SEQS).reshape(total_ch)
    first_stretch = jnp.any(seq_starts[:, None, :] == local_stretch[None, :, None], axis=2).reshape(total_ch)
    keep_stretch = 1.0 - first_stretch.astype(jnp.float32)
    seq_rows = jnp.repeat(seq_stretch, STRETCH)
    keep_rows = jnp.repeat(keep_stretch, STRETCH)[:, None]
    self_count = total_tok // (8 * STRETCH)
    cross_count = total_ch // 8
    seq_pad = jnp.concatenate([jnp.full((MAXCH * STRETCH,), -1, jnp.int32), seq_rows])
    self_fn = jax.checkpoint(self_block)
    cross_fn = jax.checkpoint(cross_block)

    def layer(hidden_in, enc_in, gain_rows, w_qkv, w_out, w_cq, w_ckv, w_cout, w_in, w_down):
        given_rows = hidden_in.reshape(total_ch, STRETCH, D)[slot_of_given].reshape(total_tok, D)
        given_enc = enc_in.reshape(total_ch, NKEYS, D)[slot_of_given]
        norm_one = low(rms_norm(given_rows, gain_rows[0]))
        projected = low(low_back(matmul(norm_one, w_qkv)))
        front_pad = jnp.zeros((MAXCH * STRETCH, D), jnp.float32)
        keys_pad = jnp.concatenate([front_pad, projected[:, D:2 * D]], axis=0)
        values_pad = jnp.concatenate([front_pad, projected[:, 2 * D:]], axis=0)
        query_rows = projected[:, :D]
        attended = lax.map(lambda block_index: self_fn(query_rows, keys_pad, values_pad, seq_rows, seq_pad, block_index), jnp.arange(self_count, dtype=jnp.int32))
        attended = low(low_back(attended.reshape(total_tok, D)))
        after_attn = given_rows + low_back(matmul(attended, w_out))
        norm_two = low(rms_norm(after_attn, gain_rows[1]))
        cross_query = low(low_back(matmul(norm_two, w_cq)))
        block_pairs = (cross_query.reshape(cross_count, 8, STRETCH, D), given_enc.reshape(cross_count, 8, NKEYS, D))
        cross_rows = lax.map(lambda block_pair: cross_fn(block_pair[0], block_pair[1], w_ckv), block_pairs)
        cross_rows = low(low_back(cross_rows.reshape(total_tok, D)))
        after_cross = after_attn + keep_rows * low_back(matmul(cross_rows, w_cout))
        norm_three = low(rms_norm(after_cross, gain_rows[2]))
        inner_rows = low_back(matmul(norm_three, w_in))
        activation = low(jax.nn.gelu(inner_rows, approximate=False))
        layer_out = after_cross + low_back(matmul(activation, w_down))
        return layer_out.reshape(total_ch, STRETCH, D)[given_at_slot].reshape(GROUPS, GROUP_TOK, D)
    float_args = [arg.astype(jnp.float32) for arg in (hidden, neighbours, norm_gains, attn_qkv, attn_out, cross_q, cross_kv, cross_out, mlp_in, mlp_out)]
    layer_out, pullback = jax.vjp(layer, *float_args)
    gradients = pullback(cotangent.astype(jnp.float32))
    return (layer_out, gradients[0], gradients[1], gradients[2], gradients[3], gradients[4], gradients[5], gradients[6], gradients[7], gradients[8], gradients[9])
```

```python
import functools

import jax
import jax.numpy as jnp
from jax import lax
from jax.experimental import pallas as pl
from jax.experimental.pallas import tpu as pltpu
from jax.sharding import PartitionSpec as P

H = 12
STRETCH = 64


NORM_EPS = 1e-06
MASKED_SCORE = -1e30
KEY_BLOCK = 1024


def to_low(values):
    return values.astype(jnp.bfloat16)


def matmul(left, right):
    return jnp.dot(left, right, preferred_element_type=jnp.float32)


def left_product(left, right):
    return lax.dot_general(left, right, (((0,), (0,)), ((), ())), preferred_element_type=jnp.float32)


def right_product(left, right):
    return lax.dot_general(left, right, (((1,), (1,)), ((), ())), preferred_element_type=jnp.float32)


def inverse_rms(values):
    return lax.rsqrt(jnp.mean(values * values, axis=-1, keepdims=True) + NORM_EPS)


def rms_back(values, scale, gain, grad):
    gained = gain * grad
    along = jnp.mean(gained * values, axis=-1, keepdims=True)
    return scale * gained - values * (scale * scale * scale) * along


def head_rows(rows, head_size):
    wide = rows.astype(jnp.float32)
    lane = lax.broadcasted_iota(jnp.int32, wide.shape, 1)
    first = jnp.where(lane < head_size, wide, 0.0)
    second = jnp.where(lane >= head_size, wide, 0.0)
    return to_low(jnp.concatenate([first, second], axis=0))


def join_heads(columns, head_size):
    tok_count = columns.shape[1] // 2
    return jnp.concatenate(
        [columns[:head_size, :tok_count], columns[head_size:, tok_count:]], axis=0
    ).T


def self_scores(query, key, key_pos, low_pos, high_pos, score_scale):
    scores = right_product(key, query) * score_scale
    return jnp.where((key_pos >= low_pos) & (key_pos <= high_pos), scores, MASKED_SCORE)


def self_forward_kernel(
    head_size, blocks, q_ref, k_ref, v_ref, pos_ref, low_ref, high_ref, o_ref, lse_ref
):
    score_scale = head_size ** (-0.5)
    query = head_rows(q_ref[...], head_size)
    low_pos, high_pos = low_ref[...], high_ref[...]
    rows = k_ref.shape[0] // blocks

    def scores_of(index):
        span = pl.ds(pl.multiple_of(index * rows, rows), rows)
        return self_scores(query, k_ref[span, :], pos_ref[span, :], low_pos, high_pos, score_scale)

    def values_of(index):
        return v_ref[pl.ds(pl.multiple_of(index * rows, rows), rows), :]

    if blocks == 1:
        scores = scores_of(0)
        peak = jnp.max(scores, axis=0, keepdims=True)
        weights = jnp.exp(scores - peak)
        total = jnp.sum(weights, axis=0, keepdims=True)
        running = left_product(values_of(0), to_low(weights))
    else:
        peak = lax.fori_loop(
            0,
            blocks,
            lambda i, top: jnp.maximum(top, jnp.max(scores_of(i), axis=0, keepdims=True)),
            jnp.full((1, query.shape[0]), MASKED_SCORE, jnp.float32),
        )

        def add(index, state):
            total, running = state
            weights = jnp.exp(scores_of(index) - peak)
            return (
                total + jnp.sum(weights, axis=0, keepdims=True),
                running + left_product(values_of(index), to_low(weights)),
            )

        total, running = lax.fori_loop(
            0,
            blocks,
            add,
            (
                jnp.zeros((1, query.shape[0]), jnp.float32),
                jnp.zeros((2 * head_size, query.shape[0]), jnp.float32),
            ),
        )
    o_ref[...] = to_low(join_heads(running / total, head_size))
    lse_ref[0] = peak + jnp.log(total)


def self_backward_kernel(
    head_size,
    blocks,
    q_ref,
    k_ref,
    v_ref,
    do_ref,
    pos_ref,
    low_ref,
    high_ref,
    lse_ref,
    dq_ref,
    dkv_ref,
):
    score_scale = head_size ** (-0.5)
    query = head_rows(q_ref[...], head_size)
    grad = head_rows(do_ref[...], head_size)
    low_pos, high_pos = low_ref[...], high_ref[...]
    log_total = lse_ref[0]
    rows = k_ref.shape[0] // blocks

    def span_of(index):
        return pl.ds(pl.multiple_of(index * rows, rows), rows)

    def pair_of(index):
        span = span_of(index)
        scores = self_scores(
            query, k_ref[span, :], pos_ref[span, :], low_pos, high_pos, score_scale
        )
        return jnp.exp(scores - log_total), right_product(v_ref[span, :], grad)

    def finish(index, probs, dprobs, delta):
        span = span_of(index)
        dscores = to_low(probs * (dprobs - delta))
        dkv_ref[0, span, :] = to_low(score_scale * matmul(dscores, query))
        dkv_ref[1, span, :] = to_low(matmul(to_low(probs), grad))
        return left_product(k_ref[span, :], dscores)

    if blocks == 1:
        probs, dprobs = pair_of(0)
        delta = jnp.sum(probs * dprobs, axis=0, keepdims=True)
        columns = finish(0, probs, dprobs, delta)
    else:

        def add_delta(index, delta):
            probs, dprobs = pair_of(index)
            return delta + jnp.sum(probs * dprobs, axis=0, keepdims=True)

        delta = lax.fori_loop(
            0, blocks, add_delta, jnp.zeros((1, query.shape[0]), jnp.float32)
        )

        def add_query(index, columns):
            probs, dprobs = pair_of(index)
            return columns + finish(index, probs, dprobs, delta)

        columns = lax.fori_loop(
            0, blocks, add_query, jnp.zeros((2 * head_size, query.shape[0]), jnp.float32)
        )
    dq_ref[...] = to_low(score_scale * join_heads(columns, head_size))


def self_specs(tok_count, key_count, pairs):
    wide = 128
    return (
        pl.BlockSpec((tok_count, wide), lambda i: (0, i)),
        pl.BlockSpec((key_count, wide), lambda i: (0, i)),
        pl.BlockSpec((key_count, wide), lambda i: (0, pairs + i)),
        pl.BlockSpec((key_count, 1), lambda i: (0, 0)),
        pl.BlockSpec((1, 2 * tok_count), lambda i: (0, 0)),
        pl.BlockSpec((1, 1, 2 * tok_count), lambda i: (i, 0, 0)),
    )


def self_forward(query, key_value, key_pos, low_pos, high_pos):
    tok_count, feature_width = query.shape
    key_count = key_value.shape[0]
    head_size = feature_width // H
    pairs = H // 2
    blocks = max(1, key_count // KEY_BLOCK)
    rows, keys, values, pos, edge, lse = self_specs(tok_count, key_count, pairs)
    return pl.pallas_call(
        functools.partial(self_forward_kernel, head_size, blocks),
        grid=(pairs,),
        in_specs=[rows, keys, values, pos, edge, edge],
        out_specs=[rows, lse],
        out_shape=[
            jax.ShapeDtypeStruct((tok_count, feature_width), jnp.bfloat16),
            jax.ShapeDtypeStruct((pairs, 1, 2 * tok_count), jnp.float32),
        ],
        cost_estimate=pl.CostEstimate(
            flops=8 * tok_count * key_count * feature_width,
            bytes_accessed=4 * key_count * feature_width,
            transcendentals=H * tok_count * key_count,
        ),
        name="self_forward",
    )(query, key_value, key_value, key_pos, low_pos, high_pos)


def self_backward(query, key_value, grad, key_pos, low_pos, high_pos, log_total):
    tok_count, feature_width = query.shape
    key_count = key_value.shape[0]
    head_size = feature_width // H
    pairs = H // 2
    blocks = max(1, key_count // KEY_BLOCK)
    rows, keys, values, pos, edge, lse = self_specs(tok_count, key_count, pairs)
    return pl.pallas_call(
        functools.partial(self_backward_kernel, head_size, blocks),
        grid=(pairs,),
        in_specs=[rows, keys, values, rows, pos, edge, edge, lse],
        out_specs=[rows, pl.BlockSpec((2, key_count, 128), lambda i: (0, 0, i))],
        out_shape=[
            jax.ShapeDtypeStruct((tok_count, feature_width), jnp.bfloat16),
            jax.ShapeDtypeStruct((2, key_count, feature_width), jnp.bfloat16),
        ],
        cost_estimate=pl.CostEstimate(
            flops=20 * tok_count * key_count * feature_width,
            bytes_accessed=8 * key_count * feature_width,
            transcendentals=H * tok_count * key_count,
        ),
        name="self_backward",
    )(query, key_value, key_value, grad, key_pos, low_pos, high_pos, log_total)


def cross_forward_kernel(head_size, stretches, q_ref, k_ref, v_ref, o_ref):
    score_scale = head_size ** (-0.5)
    keys = k_ref.shape[0] // stretches
    for s in range(stretches):
        rows = pl.ds(s * STRETCH, STRETCH)
        span = pl.ds(s * keys, keys)
        query = head_rows(q_ref[rows, :], head_size)
        scores = right_product(k_ref[span, :], query) * score_scale
        weights = jnp.exp(scores - jnp.max(scores, axis=0, keepdims=True))
        probs = to_low(weights / jnp.sum(weights, axis=0, keepdims=True))
        o_ref[rows, :] = to_low(join_heads(left_product(v_ref[span, :], probs), head_size))


def cross_backward_kernel(head_size, stretches, q_ref, k_ref, v_ref, do_ref, dq_ref, dkv_ref):
    score_scale = head_size ** (-0.5)
    keys = k_ref.shape[0] // stretches
    for s in range(stretches):
        rows = pl.ds(s * STRETCH, STRETCH)
        span = pl.ds(s * keys, keys)
        query = head_rows(q_ref[rows, :], head_size)
        grad = head_rows(do_ref[rows, :], head_size)
        scores = right_product(k_ref[span, :], query) * score_scale
        weights = jnp.exp(scores - jnp.max(scores, axis=0, keepdims=True))
        probs = weights / jnp.sum(weights, axis=0, keepdims=True)
        dprobs = right_product(v_ref[span, :], grad)
        delta = jnp.sum(probs * dprobs, axis=0, keepdims=True)
        dscores = to_low(probs * (dprobs - delta))
        dkv_ref[0, span, :] = to_low(score_scale * matmul(dscores, query))
        dkv_ref[1, span, :] = to_low(matmul(to_low(probs), grad))
        columns = left_product(k_ref[span, :], dscores)
        dq_ref[rows, :] = to_low(score_scale * join_heads(columns, head_size))


def cross_forward(query, key_value, stretches):
    tok_count, feature_width = query.shape
    key_count = key_value.shape[0]
    pairs = H // 2
    rows, keys, values, _, _, _ = self_specs(tok_count, key_count, pairs)
    return pl.pallas_call(
        functools.partial(cross_forward_kernel, feature_width // H, stretches),
        grid=(pairs,),
        in_specs=[rows, keys, values],
        out_specs=rows,
        out_shape=jax.ShapeDtypeStruct((tok_count, feature_width), jnp.bfloat16),
        cost_estimate=pl.CostEstimate(
            flops=8 * tok_count * key_count * feature_width,
            bytes_accessed=4 * key_count * feature_width,
            transcendentals=H * tok_count * key_count,
        ),
        name="cross_forward",
    )(query, key_value, key_value)


def cross_backward(query, key_value, grad, stretches):
    tok_count, feature_width = query.shape
    key_count = key_value.shape[0]
    pairs = H // 2
    rows, keys, values, _, _, _ = self_specs(tok_count, key_count, pairs)
    return pl.pallas_call(
        functools.partial(cross_backward_kernel, feature_width // H, stretches),
        grid=(pairs,),
        in_specs=[rows, keys, values, rows],
        out_specs=[rows, pl.BlockSpec((2, key_count, 128), lambda i: (0, 0, i))],
        out_shape=[
            jax.ShapeDtypeStruct((tok_count, feature_width), jnp.bfloat16),
            jax.ShapeDtypeStruct((2, key_count, feature_width), jnp.bfloat16),
        ],
        cost_estimate=pl.CostEstimate(
            flops=20 * tok_count * key_count * feature_width,
            bytes_accessed=8 * key_count * feature_width,
            transcendentals=H * tok_count * key_count,
        ),
        name="cross_backward",
    )(query, key_value, key_value, grad)


def swap(values, axis, bit):
    count = lax.axis_size(axis)
    return lax.ppermute(values, axis, [(i, i ^ bit) for i in range(count)])


def assemble_kernel(index_ref, *refs):
    pieces, out_ref = refs[:-1], refs[-1]
    rows = pieces[0].shape[0]
    for j, piece in enumerate(pieces):
        place = (index_ref[0] ^ j) * rows
        out_ref[pl.ds(pl.multiple_of(place, rows), rows), :] = piece[...]


def assemble(index, pieces):
    rows, width = pieces[0].shape
    count = len(pieces)
    tile = width
    for size in (768, 512, 256):
        if width % size == 0:
            tile = size
            break
    return pl.pallas_call(
        assemble_kernel,
        grid_spec=pltpu.PrefetchScalarGridSpec(
            num_scalar_prefetch=1,
            grid=(width // tile,),
            in_specs=[pl.BlockSpec((rows, tile), lambda i, _: (0, i))] * count,
            out_specs=pl.BlockSpec((rows * count, tile), lambda i, _: (0, i)),
        ),
        out_shape=jax.ShapeDtypeStruct((rows * count, width), pieces[0].dtype),
        cost_estimate=pl.CostEstimate(
            flops=0, bytes_accessed=4 * rows * count * width, transcendentals=0
        ),
        name="assemble",
    )(index, *pieces)


def gather_weight(index, share):
    sibling = swap(share, "fsdp", 1)
    across = swap(share, "fsdp", 2)
    across_sibling = swap(across, "fsdp", 1)
    return assemble(index, [share, sibling, across, across_sibling])


def column_blocks(values, index, count):
    width = values.shape[1] // count
    cut = [
        lax.dynamic_slice_in_dim(values, (index ^ j) * width, width, axis=1) for j in (0, 2, 1, 3)
    ]
    return cut[0], cut[1], jnp.concatenate(cut[2:], axis=1)


def share_of_product(index, terms, count):
    cut = [(column_blocks(left, index, count), right) for left, right in terms]

    def total(which):
        return sum(left_product(blocks[which], right) for blocks, right in cut)

    received = swap(to_low(total(2)), "fsdp", 1)
    rows = received.shape[0] // 2
    across = swap(to_low(total(1) + received[rows:].astype(jnp.float32)), "fsdp", 2)
    return to_low(
        total(0) + received[:rows].astype(jnp.float32) + across.astype(jnp.float32)
    )


def reduce_over_ctx(share):
    part = lax.psum_scatter(share, "ctx", scatter_dimension=0, tiled=True)
    return lax.all_gather(part, "ctx", axis=0, tiled=True)


def local(
    hidden,
    neighbours,
    cotangent,
    stretch_deal,
    seq_lengths,
    norm_gains,
    attn_qkv,
    attn_out,
    cross_q,
    cross_kv,
    cross_out,
    mlp_in,
    mlp_out,
):
    shares = lax.axis_size("fsdp")
    fsdp_index = lax.axis_index("fsdp")
    ctx_index = lax.axis_index("ctx")
    place = fsdp_index.astype(jnp.int32).reshape(1)
    hidden_all = lax.all_gather(hidden[0], "ctx", axis=0, tiled=True)
    w_qkv = gather_weight(place, attn_qkv)
    w_ckv = gather_weight(place, cross_kv)
    w_out = gather_weight(place, attn_out)
    w_cq = gather_weight(place, cross_q)
    w_cout = gather_weight(place, cross_out)
    w_in = gather_weight(place, mlp_in)
    w_down = gather_weight(place, mlp_out)
    gain_rows = lax.all_gather(norm_gains, "fsdp", axis=1, tiled=True).astype(jnp.float32)

    tok_count, feature_width = hidden.shape[1:]
    stretch_count = tok_count // STRETCH
    deal_row = stretch_deal[0]
    lengths_row = seq_lengths[0]
    group_tok = deal_row.shape[0] * STRETCH
    seq_ends = jnp.cumsum(lengths_row)
    seq_starts = seq_ends - lengths_row
    slot_start = jnp.max(
        jnp.where(seq_starts[None, :] <= deal_row[:, None], seq_starts[None, :], 0), axis=1
    )
    offsets = jnp.arange(STRETCH, dtype=jnp.int32)
    token_pos = (deal_row[:, None] * STRETCH + offsets[None, :]).reshape(group_tok)
    own_deal = lax.dynamic_slice_in_dim(deal_row, ctx_index * stretch_count, stretch_count)
    own_start = lax.dynamic_slice_in_dim(slot_start, ctx_index * stretch_count, stretch_count)
    keep_rows = jnp.repeat((own_deal != own_start).astype(jnp.float32), STRETCH)[:, None]
    high_pos = jnp.tile((own_deal[:, None] * STRETCH + offsets[None, :]).reshape(1, tok_count), (1, 2))
    low_pos = jnp.tile(jnp.repeat(own_start * STRETCH, STRETCH).reshape(1, tok_count), (1, 2))
    key_pos = token_pos.reshape(group_tok, 1)

    rows_all = hidden_all.astype(jnp.float32)
    scale_all = inverse_rms(rows_all)
    norm_all = to_low(rows_all * scale_all * gain_rows[0])
    key_value = to_low(matmul(norm_all, w_qkv[:, feature_width:]))
    input_rows = hidden[0].astype(jnp.float32)
    scale_one = inverse_rms(input_rows)
    norm_one = to_low(input_rows * scale_one * gain_rows[0])
    query = to_low(matmul(norm_one, w_qkv[:, :feature_width]))
    attended, log_total = self_forward(query, key_value, key_pos, low_pos, high_pos)
    after_attn = input_rows + matmul(attended, w_out)
    scale_two = inverse_rms(after_attn)
    norm_two = to_low(after_attn * scale_two * gain_rows[1])
    cross_query = to_low(matmul(norm_two, w_cq))
    enc_rows = neighbours[0].reshape(-1, feature_width)
    cross_key_value = to_low(matmul(enc_rows, w_ckv))
    cross_rows = cross_forward(cross_query, cross_key_value, stretch_count)
    after_cross = after_attn + keep_rows * matmul(cross_rows, w_cout)
    scale_three = inverse_rms(after_cross)
    norm_three = to_low(after_cross * scale_three * gain_rows[2])
    inner_rows = matmul(norm_three, w_in)
    share_below = 0.5 * (1.0 + lax.erf(inner_rows * (2.0 ** -0.5)))
    activation = to_low(inner_rows * share_below)
    slope = share_below + inner_rows * jnp.exp(-0.5 * inner_rows * inner_rows) * (
        (2.0 * jnp.pi) ** -0.5
    )
    layer_out = after_cross + matmul(activation, w_down)

    grad_out = cotangent[0].astype(jnp.float32)
    grad_inner = to_low(right_product(cotangent[0], w_down) * slope)
    grad_norm3 = right_product(grad_inner, w_in)
    grad_gain3 = jnp.sum(grad_norm3 * after_cross * scale_three, axis=0)
    grad_after_cross = grad_out + rms_back(after_cross, scale_three, gain_rows[2], grad_norm3)
    grad_cross_branch = to_low(keep_rows * grad_after_cross)
    grad_cross_rows = to_low(right_product(grad_cross_branch, w_cout))
    grad_cross_query, grad_cross_pair = cross_backward(
        cross_query, cross_key_value, grad_cross_rows, stretch_count
    )
    grad_norm2 = right_product(grad_cross_query, w_cq)
    grad_gain2 = jnp.sum(grad_norm2 * after_attn * scale_two, axis=0)
    grad_after_attn = grad_after_cross + rms_back(
        after_attn, scale_two, gain_rows[1], grad_norm2
    )
    grad_attn_branch = to_low(grad_after_attn)
    grad_attended = to_low(right_product(grad_attn_branch, w_out))
    grad_query, grad_pair = self_backward(
        query, key_value, grad_attended, key_pos, low_pos, high_pos, log_total
    )
    grad_norm1_all = right_product(
        grad_pair[0], w_qkv[:, feature_width : 2 * feature_width]
    ) + right_product(grad_pair[1], w_qkv[:, 2 * feature_width :])
    grad_norm1_query = right_product(grad_query, w_qkv[:, :feature_width])
    grad_norm1 = (
        lax.psum_scatter(to_low(grad_norm1_all), "ctx", scatter_dimension=0, tiled=True).astype(
            jnp.float32
        )
        + grad_norm1_query
    )
    grad_input = grad_after_attn + rms_back(input_rows, scale_one, gain_rows[0], grad_norm1)
    grad_gain1 = jnp.sum(grad_norm1_all * rows_all * scale_all, axis=0) + jnp.sum(
        grad_norm1_query * input_rows * scale_one, axis=0
    )
    grad_enc = right_product(grad_cross_pair[0], w_ckv[:, :feature_width]) + right_product(
        grad_cross_pair[1], w_ckv[:, feature_width:]
    )

    product = functools.partial(share_of_product, fsdp_index, count=shares)
    part_down = product([(activation, cotangent[0])])
    part_in = product([(norm_three, grad_inner)])
    part_cout = product([(cross_rows, grad_cross_branch)])
    part_cq = product([(norm_two, grad_cross_query)])
    part_ck = product([(enc_rows, grad_cross_pair[0])])
    part_cv = product([(enc_rows, grad_cross_pair[1])])
    part_out = product([(attended, grad_attn_branch)])
    part_q = product([(norm_one, grad_query)])
    part_k = product([(norm_all, grad_pair[0])])
    part_v = product([(norm_all, grad_pair[1])])
    share_rows = feature_width // shares
    total_mlp = reduce_over_ctx(
        jnp.concatenate([part_in, part_down.reshape(share_rows, -1)], axis=1)
    ).astype(jnp.float32)
    total_cross = reduce_over_ctx(
        jnp.concatenate([part_cout, part_cq, part_ck, part_cv], axis=1)
    ).astype(jnp.float32)
    total_attn = reduce_over_ctx(
        jnp.concatenate([part_out, part_q, part_k, part_v], axis=1)
    ).astype(jnp.float32)
    grad_gains = lax.psum(jnp.stack([grad_gain1, grad_gain2, grad_gain3]), ("ctx", "fsdp"))
    grad_gains = lax.dynamic_slice_in_dim(grad_gains, fsdp_index * share_rows, share_rows, axis=1)
    inner_width = mlp_in.shape[1]
    return (
        layer_out[None],
        grad_input[None],
        grad_enc.reshape(neighbours.shape),
        grad_gains,
        total_attn[:, feature_width:],
        total_attn[:, :feature_width],
        total_cross[:, feature_width : 2 * feature_width],
        total_cross[:, 2 * feature_width :],
        total_cross[:, :feature_width],
        total_mlp[:, :inner_width],
        total_mlp[:, inner_width:].reshape(mlp_out.shape),
    )


def solution(mesh):
    return jax.shard_map(
        local,
        mesh=mesh,
        in_specs=(
            P("fsdp", "ctx", None),
            P("fsdp", "ctx", None, None),
            P("fsdp", "ctx", None),
            P("fsdp", None),
            P("fsdp", None),
            P(None, "fsdp"),
            P("fsdp", None),
            P("fsdp", None),
            P("fsdp", None),
            P("fsdp", None),
            P("fsdp", None),
            P("fsdp", None),
            P("fsdp", None),
        ),
        out_specs=(
            P("fsdp", "ctx", None),
            P("fsdp", "ctx", None),
            P("fsdp", "ctx", None, None),
            P(None, "fsdp"),
            P("fsdp", None),
            P("fsdp", None),
            P("fsdp", None),
            P("fsdp", None),
            P("fsdp", None),
            P("fsdp", None),
            P("fsdp", None),
        ),
        check_vma=False,
    )
```

```python
import functools

import jax
import jax.numpy as jnp
from jax import lax
from jax.experimental import pallas as pl
from jax.experimental.pallas import tpu as pltpu
from jax.sharding import PartitionSpec as P

H = 12
STRETCH = 64


NORM_EPS = 1e-06
MASKED_SCORE = -1e30
KEY_BLOCK = 1024


def to_low(values):
    return values.astype(jnp.bfloat16)


def matmul(left, right):
    return jnp.dot(left, right, preferred_element_type=jnp.float32)


def left_product(left, right):
    return lax.dot_general(left, right, (((0,), (0,)), ((), ())), preferred_element_type=jnp.float32)


def right_product(left, right):
    return lax.dot_general(left, right, (((1,), (1,)), ((), ())), preferred_element_type=jnp.float32)


def inverse_rms(values):
    return lax.rsqrt(jnp.mean(values * values, axis=-1, keepdims=True) + NORM_EPS)


def rms_back(values, scale, gain, grad):
    gained = gain * grad
    along = jnp.mean(gained * values, axis=-1, keepdims=True)
    return scale * gained - values * (scale * scale * scale) * along


def head_rows(rows, head_size):
    wide = rows.astype(jnp.float32)
    lane = lax.broadcasted_iota(jnp.int32, wide.shape, 1)
    first = jnp.where(lane < head_size, wide, 0.0)
    second = jnp.where(lane >= head_size, wide, 0.0)
    return to_low(jnp.concatenate([first, second], axis=0))


def join_heads(columns, head_size):
    tok_count = columns.shape[1] // 2
    return jnp.concatenate(
        [columns[:head_size, :tok_count], columns[head_size:, tok_count:]], axis=0
    ).T


def self_scores(query, key, key_pos, low_pos, high_pos, score_scale):
    scores = right_product(key, query) * score_scale
    return jnp.where((key_pos >= low_pos) & (key_pos <= high_pos), scores, MASKED_SCORE)


def self_forward_kernel(
    head_size, blocks, q_ref, k_ref, v_ref, pos_ref, low_ref, high_ref, o_ref, lse_ref
):
    score_scale = head_size ** (-0.5)
    query = head_rows(q_ref[...], head_size)
    low_pos, high_pos = low_ref[...], high_ref[...]
    rows = k_ref.shape[0] // blocks

    def scores_of(index):
        span = pl.ds(pl.multiple_of(index * rows, rows), rows)
        return self_scores(query, k_ref[span, :], pos_ref[span, :], low_pos, high_pos, score_scale)

    def values_of(index):
        return v_ref[pl.ds(pl.multiple_of(index * rows, rows), rows), :]

    if blocks == 1:
        scores = scores_of(0)
        peak = jnp.max(scores, axis=0, keepdims=True)
        weights = jnp.exp(scores - peak)
        total = jnp.sum(weights, axis=0, keepdims=True)
        running = left_product(values_of(0), to_low(weights))
    else:
        peak = lax.fori_loop(
            0,
            blocks,
            lambda i, top: jnp.maximum(top, jnp.max(scores_of(i), axis=0, keepdims=True)),
            jnp.full((1, query.shape[0]), MASKED_SCORE, jnp.float32),
        )

        def add(index, state):
            total, running = state
            weights = jnp.exp(scores_of(index) - peak)
            return (
                total + jnp.sum(weights, axis=0, keepdims=True),
                running + left_product(values_of(index), to_low(weights)),
            )

        total, running = lax.fori_loop(
            0,
            blocks,
            add,
            (
                jnp.zeros((1, query.shape[0]), jnp.float32),
                jnp.zeros((2 * head_size, query.shape[0]), jnp.float32),
            ),
        )
    o_ref[...] = to_low(join_heads(running / total, head_size))
    lse_ref[0] = peak + jnp.log(total)


def self_backward_kernel(
    head_size,
    blocks,
    q_ref,
    k_ref,
    v_ref,
    do_ref,
    pos_ref,
    low_ref,
    high_ref,
    lse_ref,
    dq_ref,
    dkv_ref,
):
    score_scale = head_size ** (-0.5)
    query = head_rows(q_ref[...], head_size)
    grad = head_rows(do_ref[...], head_size)
    low_pos, high_pos = low_ref[...], high_ref[...]
    log_total = lse_ref[0]
    rows = k_ref.shape[0] // blocks

    def span_of(index):
        return pl.ds(pl.multiple_of(index * rows, rows), rows)

    def pair_of(index):
        span = span_of(index)
        scores = self_scores(
            query, k_ref[span, :], pos_ref[span, :], low_pos, high_pos, score_scale
        )
        return jnp.exp(scores - log_total), right_product(v_ref[span, :], grad)

    def finish(index, probs, dprobs, delta):
        span = span_of(index)
        dscores = to_low(probs * (dprobs - delta))
        dkv_ref[0, span, :] = to_low(score_scale * matmul(dscores, query))
        dkv_ref[1, span, :] = to_low(matmul(to_low(probs), grad))
        return left_product(k_ref[span, :], dscores)

    if blocks == 1:
        probs, dprobs = pair_of(0)
        delta = jnp.sum(probs * dprobs, axis=0, keepdims=True)
        columns = finish(0, probs, dprobs, delta)
    else:

        def add_delta(index, delta):
            probs, dprobs = pair_of(index)
            return delta + jnp.sum(probs * dprobs, axis=0, keepdims=True)

        delta = lax.fori_loop(
            0, blocks, add_delta, jnp.zeros((1, query.shape[0]), jnp.float32)
        )

        def add_query(index, columns):
            probs, dprobs = pair_of(index)
            return columns + finish(index, probs, dprobs, delta)

        columns = lax.fori_loop(
            0, blocks, add_query, jnp.zeros((2 * head_size, query.shape[0]), jnp.float32)
        )
    dq_ref[...] = to_low(score_scale * join_heads(columns, head_size))


def self_specs(tok_count, key_count, pairs):
    wide = 128
    return (
        pl.BlockSpec((tok_count, wide), lambda i: (0, i)),
        pl.BlockSpec((key_count, wide), lambda i: (0, i)),
        pl.BlockSpec((key_count, wide), lambda i: (0, pairs + i)),
        pl.BlockSpec((key_count, 1), lambda i: (0, 0)),
        pl.BlockSpec((1, 2 * tok_count), lambda i: (0, 0)),
        pl.BlockSpec((1, 1, 2 * tok_count), lambda i: (i, 0, 0)),
    )


def self_forward(query, key_value, key_pos, low_pos, high_pos):
    tok_count, feature_width = query.shape
    key_count = key_value.shape[0]
    head_size = feature_width // H
    pairs = H // 2
    blocks = max(1, key_count // KEY_BLOCK)
    rows, keys, values, pos, edge, lse = self_specs(tok_count, key_count, pairs)
    return pl.pallas_call(
        functools.partial(self_forward_kernel, head_size, blocks),
        grid=(pairs,),
        in_specs=[rows, keys, values, pos, edge, edge],
        out_specs=[rows, lse],
        out_shape=[
            jax.ShapeDtypeStruct((tok_count, feature_width), jnp.bfloat16),
            jax.ShapeDtypeStruct((pairs, 1, 2 * tok_count), jnp.float32),
        ],
        cost_estimate=pl.CostEstimate(
            flops=8 * tok_count * key_count * feature_width,
            bytes_accessed=4 * key_count * feature_width,
            transcendentals=H * tok_count * key_count,
        ),
        name="self_forward",
    )(query, key_value, key_value, key_pos, low_pos, high_pos)


def self_backward(query, key_value, grad, key_pos, low_pos, high_pos, log_total):
    tok_count, feature_width = query.shape
    key_count = key_value.shape[0]
    head_size = feature_width // H
    pairs = H // 2
    blocks = max(1, key_count // KEY_BLOCK)
    rows, keys, values, pos, edge, lse = self_specs(tok_count, key_count, pairs)
    return pl.pallas_call(
        functools.partial(self_backward_kernel, head_size, blocks),
        grid=(pairs,),
        in_specs=[rows, keys, values, rows, pos, edge, edge, lse],
        out_specs=[rows, pl.BlockSpec((2, key_count, 128), lambda i: (0, 0, i))],
        out_shape=[
            jax.ShapeDtypeStruct((tok_count, feature_width), jnp.bfloat16),
            jax.ShapeDtypeStruct((2, key_count, feature_width), jnp.bfloat16),
        ],
        cost_estimate=pl.CostEstimate(
            flops=20 * tok_count * key_count * feature_width,
            bytes_accessed=8 * key_count * feature_width,
            transcendentals=H * tok_count * key_count,
        ),
        name="self_backward",
    )(query, key_value, key_value, grad, key_pos, low_pos, high_pos, log_total)


def cross_forward_kernel(head_size, stretches, q_ref, k_ref, v_ref, o_ref):
    score_scale = head_size ** (-0.5)
    keys = k_ref.shape[0] // stretches
    for s in range(stretches):
        rows = pl.ds(s * STRETCH, STRETCH)
        span = pl.ds(s * keys, keys)
        query = head_rows(q_ref[rows, :], head_size)
        scores = right_product(k_ref[span, :], query) * score_scale
        weights = jnp.exp(scores - jnp.max(scores, axis=0, keepdims=True))
        probs = to_low(weights / jnp.sum(weights, axis=0, keepdims=True))
        o_ref[rows, :] = to_low(join_heads(left_product(v_ref[span, :], probs), head_size))


def cross_backward_kernel(head_size, stretches, q_ref, k_ref, v_ref, do_ref, dq_ref, dkv_ref):
    score_scale = head_size ** (-0.5)
    keys = k_ref.shape[0] // stretches
    for s in range(stretches):
        rows = pl.ds(s * STRETCH, STRETCH)
        span = pl.ds(s * keys, keys)
        query = head_rows(q_ref[rows, :], head_size)
        grad = head_rows(do_ref[rows, :], head_size)
        scores = right_product(k_ref[span, :], query) * score_scale
        weights = jnp.exp(scores - jnp.max(scores, axis=0, keepdims=True))
        probs = weights / jnp.sum(weights, axis=0, keepdims=True)
        dprobs = right_product(v_ref[span, :], grad)
        delta = jnp.sum(probs * dprobs, axis=0, keepdims=True)
        dscores = to_low(probs * (dprobs - delta))
        dkv_ref[0, span, :] = to_low(score_scale * matmul(dscores, query))
        dkv_ref[1, span, :] = to_low(matmul(to_low(probs), grad))
        columns = left_product(k_ref[span, :], dscores)
        dq_ref[rows, :] = to_low(score_scale * join_heads(columns, head_size))


def cross_forward(query, key_value, stretches):
    tok_count, feature_width = query.shape
    key_count = key_value.shape[0]
    pairs = H // 2
    rows, keys, values, _, _, _ = self_specs(tok_count, key_count, pairs)
    return pl.pallas_call(
        functools.partial(cross_forward_kernel, feature_width // H, stretches),
        grid=(pairs,),
        in_specs=[rows, keys, values],
        out_specs=rows,
        out_shape=jax.ShapeDtypeStruct((tok_count, feature_width), jnp.bfloat16),
        cost_estimate=pl.CostEstimate(
            flops=8 * tok_count * key_count * feature_width,
            bytes_accessed=4 * key_count * feature_width,
            transcendentals=H * tok_count * key_count,
        ),
        name="cross_forward",
    )(query, key_value, key_value)


def cross_backward(query, key_value, grad, stretches):
    tok_count, feature_width = query.shape
    key_count = key_value.shape[0]
    pairs = H // 2
    rows, keys, values, _, _, _ = self_specs(tok_count, key_count, pairs)
    return pl.pallas_call(
        functools.partial(cross_backward_kernel, feature_width // H, stretches),
        grid=(pairs,),
        in_specs=[rows, keys, values, rows],
        out_specs=[rows, pl.BlockSpec((2, key_count, 128), lambda i: (0, 0, i))],
        out_shape=[
            jax.ShapeDtypeStruct((tok_count, feature_width), jnp.bfloat16),
            jax.ShapeDtypeStruct((2, key_count, feature_width), jnp.bfloat16),
        ],
        cost_estimate=pl.CostEstimate(
            flops=20 * tok_count * key_count * feature_width,
            bytes_accessed=8 * key_count * feature_width,
            transcendentals=H * tok_count * key_count,
        ),
        name="cross_backward",
    )(query, key_value, key_value, grad)


def swap(values, axis, bit):
    count = lax.axis_size(axis)
    return lax.ppermute(values, axis, [(i, i ^ bit) for i in range(count)])


def assemble_kernel(index_ref, *refs):
    pieces, out_ref = refs[:-1], refs[-1]
    rows = pieces[0].shape[0]
    for j, piece in enumerate(pieces):
        place = (index_ref[0] ^ j) * rows
        out_ref[pl.ds(pl.multiple_of(place, rows), rows), :] = piece[...]


def assemble(index, pieces):
    rows, width = pieces[0].shape
    count = len(pieces)
    tile = width
    for size in (768, 512, 256):
        if width % size == 0:
            tile = size
            break
    return pl.pallas_call(
        assemble_kernel,
        grid_spec=pltpu.PrefetchScalarGridSpec(
            num_scalar_prefetch=1,
            grid=(width // tile,),
            in_specs=[pl.BlockSpec((rows, tile), lambda i, _: (0, i))] * count,
            out_specs=pl.BlockSpec((rows * count, tile), lambda i, _: (0, i)),
        ),
        out_shape=jax.ShapeDtypeStruct((rows * count, width), pieces[0].dtype),
        cost_estimate=pl.CostEstimate(
            flops=0, bytes_accessed=4 * rows * count * width, transcendentals=0
        ),
        name="assemble",
    )(index, *pieces)


def gather_weight(index, share):
    sibling = swap(share, "fsdp", 1)
    across = swap(share, "fsdp", 2)
    across_sibling = swap(across, "fsdp", 1)
    return assemble(index, [share, sibling, across, across_sibling])


def mirrored(position, count):
    out = 0
    for _ in range(count.bit_length() - 1):
        out, position = 2 * out + position % 2, position // 2
    return out


def chunk_count(rows):
    count = lax.axis_size("ctx")
    return count if count & (count - 1) == 0 and rows % (8 * count) == 0 else 1


def store_chunks(out_ref, start, held_ref, base, rows, ctx_index, chunks):
    size = rows // chunks
    for p in range(chunks):
        place = base + (ctx_index ^ mirrored(p, chunks)) * size
        part = held_ref[pl.ds(pl.multiple_of(place, 8), size), :]
        out_ref[pl.ds(start + p * size, size), :] = part.astype(out_ref.dtype)


def products_kernel(tiles, rows, chunks, index_ref, *refs):
    count = len(tiles)
    inputs, (keep_ref, send_ref, held_ref) = refs[:-3], refs[-3:]
    fsdp_index, ctx_index = index_ref[0], index_ref[1]
    width = held_ref.shape[1]
    for t, (left, right, column) in enumerate(tiles):

        @pl.when(pl.program_id(0) == t)
        def _(left=left, right=right, column=column):
            grads = inputs[right][:, pl.ds(column * width, width)]
            held_ref[...] = left_product(inputs[left][...], grads)

    for out_ref, order in ((keep_ref, (0, 2)), (send_ref, (1, 3))):
        for k, j in enumerate(order):
            store_chunks(
                out_ref, k * rows, held_ref, (fsdp_index ^ j) * rows, rows, ctx_index, chunks
            )


def wide_products(index, terms):
    shares = lax.axis_size("fsdp")
    inputs, tiles = [], []
    width = terms[0][0].shape[1]
    for left, right, plane in terms:
        if not inputs or all(left is not value for value, _ in inputs):
            inputs.append((left, None))
        first = next(i for i, (value, _) in enumerate(inputs) if value is left)
        inputs.append((right, plane))
        for column in range(right.shape[-1] // width):
            tiles.append((first, len(inputs) - 1, column))
    rows = width // shares
    chunks = chunk_count(rows)
    specs = []
    for value, plane in inputs:
        if value.ndim == 2:
            specs.append(pl.BlockSpec(value.shape, lambda i, _: (0, 0)))
        else:
            specs.append(
                pl.BlockSpec((None,) + value.shape[1:], lambda i, _, plane=plane: (plane, 0, 0))
            )
    total = len(tiles) * width
    out = jax.ShapeDtypeStruct((2 * rows, total), jnp.bfloat16)
    out_spec = pl.BlockSpec((2 * rows, width), lambda i, _: (0, i))
    tokens = sum(left.shape[0] * right.shape[-1] for left, right, _ in terms)
    return pl.pallas_call(
        functools.partial(products_kernel, tiles, rows, chunks),
        grid_spec=pltpu.PrefetchScalarGridSpec(
            num_scalar_prefetch=1,
            grid=(len(tiles),),
            in_specs=specs,
            out_specs=[out_spec, out_spec],
            scratch_shapes=[pltpu.VMEM((width, width), jnp.float32)],
        ),
        out_shape=[out, out],
        cost_estimate=pl.CostEstimate(
            flops=2 * width * tokens, bytes_accessed=8 * rows * total, transcendentals=0
        ),
        name="wide_products",
    )(index, *[value for value, _ in inputs])


def tall_kernel(rows, chunks, index_ref, left_ref, right_ref, keep_ref, send_ref, held_ref):
    held_ref[...] = left_product(left_ref[...], right_ref[...])
    for out_ref, steps in ((keep_ref, (0, 1)), (send_ref, (2, 3))):

        @pl.when((pl.program_id(0) == steps[0]) | (pl.program_id(0) == steps[1]))
        def _(out_ref=out_ref):
            store_chunks(out_ref, 0, held_ref, 0, rows, index_ref[1], chunks)


def tall_products(index, left, right):
    shares = lax.axis_size("fsdp")
    tokens, depth = left.shape
    width = right.shape[1]
    rows = depth // shares
    chunks = chunk_count(rows)
    out = jax.ShapeDtypeStruct((2 * rows, width), jnp.bfloat16)

    def share_of(i, index_ref):
        return (0, index_ref[0] ^ (2 * (i % 2) + i // 2))

    return pl.pallas_call(
        functools.partial(tall_kernel, rows, chunks),
        grid_spec=pltpu.PrefetchScalarGridSpec(
            num_scalar_prefetch=1,
            grid=(shares,),
            in_specs=[
                pl.BlockSpec((tokens, rows), share_of),
                pl.BlockSpec((tokens, width), lambda i, _: (0, 0)),
            ],
            out_specs=[
                pl.BlockSpec((rows, width), lambda i, _: (jnp.minimum(i, 1), 0)),
                pl.BlockSpec((rows, width), lambda i, _: (jnp.maximum(i - 2, 0), 0)),
            ],
            scratch_shapes=[pltpu.VMEM((rows, width), jnp.float32)],
        ),
        out_shape=[out, out],
        cost_estimate=pl.CostEstimate(
            flops=2 * tokens * depth * width, bytes_accessed=4 * depth * width, transcendentals=0
        ),
        name="tall_products",
    )(index, left, right)


def add_low(*parts):
    return to_low(sum(part.astype(jnp.float32) for part in parts))


def reduce_products(keep, send):
    rows = keep.shape[0] // 2
    received = swap(send, "fsdp", 1)
    across = swap(add_low(keep[rows:], received[rows:]), "fsdp", 2)
    chunks = chunk_count(rows)
    if chunks == 1:
        share = lax.psum(add_low(keep[:rows], received[:rows], across), "ctx")
        return share[: rows // 2], share[rows // 2 :]
    parts = (keep[:rows], received[:rows], across)
    half = rows // 2
    bit = 1
    while bit < chunks:
        sent = add_low(*[part[half:] for part in parts])
        held = add_low(*[part[:half] for part in parts])
        parts = (held, swap(sent, "ctx", bit))
        half, bit = half // 2, 2 * bit
    gathered = add_low(*parts)
    while bit > 2:
        bit = bit // 2
        gathered = jnp.concatenate([gathered, swap(gathered, "ctx", bit)], axis=0)
    return gathered, swap(gathered, "ctx", 1)


def place_kernel(chunks, index_ref, low_ref, high_ref, out_ref):
    size = out_ref.shape[0] // chunks
    per_half = max(1, chunks // 2)
    if chunks == 1:
        half = out_ref.shape[0] // 2
        out_ref[pl.ds(0, half), :] = low_ref[...].astype(jnp.float32)
        out_ref[pl.ds(half, half), :] = high_ref[...].astype(jnp.float32)
        return
    for p in range(chunks):
        source = low_ref if p < per_half else high_ref
        part = source[pl.ds((p % per_half) * size, size), :].astype(jnp.float32)
        place = (index_ref[1] ^ mirrored(p, chunks)) * size
        out_ref[pl.ds(pl.multiple_of(place, 8), size), :] = part


def place_share(index, halves, offset, width):
    low, high = halves
    rows = 2 * low.shape[0]
    tile = 768 if width % 768 == 0 and offset % 768 == 0 else width
    start = offset // tile
    spec = pl.BlockSpec((rows // 2, tile), lambda i, _: (0, start + i))
    return pl.pallas_call(
        functools.partial(place_kernel, chunk_count(rows)),
        grid_spec=pltpu.PrefetchScalarGridSpec(
            num_scalar_prefetch=1,
            grid=(width // tile,),
            in_specs=[spec, spec],
            out_specs=pl.BlockSpec((rows, tile), lambda i, _: (0, i)),
        ),
        out_shape=jax.ShapeDtypeStruct((rows, width), jnp.float32),
        cost_estimate=pl.CostEstimate(
            flops=0, bytes_accessed=6 * rows * width, transcendentals=0
        ),
        name="place_share",
    )(index, low, high)


def gain_gradient(weight, grad, gain):
    return jnp.sum(weight.astype(jnp.float32) * grad, axis=1) / gain.astype(jnp.float32)


def local(
    hidden,
    neighbours,
    cotangent,
    stretch_deal,
    seq_lengths,
    norm_gains,
    attn_qkv,
    attn_out,
    cross_q,
    cross_kv,
    cross_out,
    mlp_in,
    mlp_out,
):
    shares = lax.axis_size("fsdp")
    fsdp_index = lax.axis_index("fsdp")
    ctx_index = lax.axis_index("ctx")
    place = jnp.stack([fsdp_index, ctx_index]).astype(jnp.int32)
    ctx_count = lax.axis_size("ctx")
    hidden_all = hidden[0]
    bit = ctx_count
    while bit > 1:
        bit = bit // 2
        hidden_all = jnp.concatenate([hidden_all, swap(hidden_all, "ctx", bit)], axis=0)
    w_qkv = gather_weight(place, attn_qkv)
    w_ckv = gather_weight(place, cross_kv)
    w_out = gather_weight(place, attn_out)
    w_cq = gather_weight(place, cross_q)
    w_cout = gather_weight(place, cross_out)
    w_in = gather_weight(place, mlp_in)
    w_down = gather_weight(place, mlp_out)
    gain_pair = jnp.stack([norm_gains, swap(norm_gains, "fsdp", 1)])
    gain_pieces = jnp.concatenate([gain_pair, swap(gain_pair, "fsdp", 2)])
    gain_rows = jnp.concatenate(
        [lax.dynamic_index_in_dim(gain_pieces, fsdp_index ^ j, 0, False) for j in range(shares)],
        axis=1,
    ).astype(jnp.float32)

    tok_count, feature_width = hidden.shape[1:]
    stretch_count = tok_count // STRETCH
    deal_row = stretch_deal[0]
    lengths_row = seq_lengths[0]
    group_tok = deal_row.shape[0] * STRETCH
    seq_ends = jnp.cumsum(lengths_row)
    seq_starts = seq_ends - lengths_row
    slot_start = jnp.max(
        jnp.where(seq_starts[None, :] <= deal_row[:, None], seq_starts[None, :], 0), axis=1
    )
    offsets = jnp.arange(STRETCH, dtype=jnp.int32)
    order = jnp.array([mirrored(p, ctx_count) for p in range(ctx_count)], jnp.int32) ^ ctx_index
    held_deal = deal_row.reshape(ctx_count, stretch_count)[order].reshape(-1)
    token_pos = (held_deal[:, None] * STRETCH + offsets[None, :]).reshape(group_tok)
    own_deal = lax.dynamic_slice_in_dim(deal_row, ctx_index * stretch_count, stretch_count)
    own_start = lax.dynamic_slice_in_dim(slot_start, ctx_index * stretch_count, stretch_count)
    keep_rows = jnp.repeat((own_deal != own_start).astype(jnp.float32), STRETCH)[:, None]
    high_pos = jnp.tile((own_deal[:, None] * STRETCH + offsets[None, :]).reshape(1, tok_count), (1, 2))
    low_pos = jnp.tile(jnp.repeat(own_start * STRETCH, STRETCH).reshape(1, tok_count), (1, 2))
    key_pos = token_pos.reshape(group_tok, 1)

    rows_all = hidden_all.astype(jnp.float32)
    scale_all = inverse_rms(rows_all)
    norm_all = to_low(rows_all * scale_all * gain_rows[0])
    key_value = to_low(matmul(norm_all, w_qkv[:, feature_width:]))
    input_rows = hidden[0].astype(jnp.float32)
    scale_one = inverse_rms(input_rows)
    norm_one = to_low(input_rows * scale_one * gain_rows[0])
    query = to_low(matmul(norm_one, w_qkv[:, :feature_width]))
    attended, log_total = self_forward(query, key_value, key_pos, low_pos, high_pos)
    after_attn = input_rows + matmul(attended, w_out)
    scale_two = inverse_rms(after_attn)
    norm_two = to_low(after_attn * scale_two * gain_rows[1])
    cross_query = to_low(matmul(norm_two, w_cq))
    enc_rows = neighbours[0].reshape(-1, feature_width)
    cross_key_value = to_low(matmul(enc_rows, w_ckv))
    cross_rows = cross_forward(cross_query, cross_key_value, stretch_count)
    after_cross = after_attn + keep_rows * matmul(cross_rows, w_cout)
    scale_three = inverse_rms(after_cross)
    norm_three = to_low(after_cross * scale_three * gain_rows[2])
    inner_rows = matmul(norm_three, w_in)
    share_below = 0.5 * (1.0 + lax.erf(inner_rows * (2.0 ** -0.5)))
    activation = to_low(inner_rows * share_below)
    slope = share_below + inner_rows * jnp.exp(-0.5 * inner_rows * inner_rows) * (
        (2.0 * jnp.pi) ** -0.5
    )
    layer_out = after_cross + matmul(activation, w_down)

    grad_out = cotangent[0].astype(jnp.float32)
    grad_inner = to_low(right_product(cotangent[0], w_down) * slope)
    grad_norm3 = right_product(grad_inner, w_in)
    grad_after_cross = grad_out + rms_back(after_cross, scale_three, gain_rows[2], grad_norm3)
    grad_cross_branch = to_low(keep_rows * grad_after_cross)
    grad_cross_rows = to_low(right_product(grad_cross_branch, w_cout))
    grad_cross_query, grad_cross_pair = cross_backward(
        cross_query, cross_key_value, grad_cross_rows, stretch_count
    )
    grad_norm2 = right_product(grad_cross_query, w_cq)
    grad_after_attn = grad_after_cross + rms_back(
        after_attn, scale_two, gain_rows[1], grad_norm2
    )
    grad_attn_branch = to_low(grad_after_attn)
    grad_attended = to_low(right_product(grad_attn_branch, w_out))
    grad_query, grad_pair = self_backward(
        query, key_value, grad_attended, key_pos, low_pos, high_pos, log_total
    )
    grad_norm1_all = right_product(
        grad_pair[0], w_qkv[:, feature_width : 2 * feature_width]
    ) + right_product(grad_pair[1], w_qkv[:, 2 * feature_width :])
    grad_norm1_query = right_product(grad_query, w_qkv[:, :feature_width])
    grad_norm1 = to_low(grad_norm1_all)
    bit = 1
    while bit < ctx_count:
        half = grad_norm1.shape[0] // 2
        grad_norm1 = add_low(grad_norm1[:half], swap(grad_norm1[half:], "ctx", bit))
        bit = 2 * bit
    grad_norm1 = grad_norm1.astype(jnp.float32) + grad_norm1_query
    grad_input = grad_after_attn + rms_back(input_rows, scale_one, gain_rows[0], grad_norm1)
    grad_enc = right_product(grad_cross_pair[0], w_ckv[:, :feature_width]) + right_product(
        grad_cross_pair[1], w_ckv[:, feature_width:]
    )

    halves_down = reduce_products(*tall_products(place, activation, cotangent[0]))
    halves_in = reduce_products(*wide_products(place, [(norm_three, grad_inner, None)]))
    halves_cross = reduce_products(
        *wide_products(
            place,
            [
                (cross_rows, grad_cross_branch, None),
                (norm_two, grad_cross_query, None),
                (enc_rows, grad_cross_pair, 0),
                (enc_rows, grad_cross_pair, 1),
                (attended, grad_attn_branch, None),
            ],
        )
    )
    halves_attn = reduce_products(
        *wide_products(
            place,
            [
                (norm_one, grad_query, None),
                (norm_all, grad_pair, 0),
                (norm_all, grad_pair, 1),
            ],
        )
    )
    d = feature_width
    total_down = place_share(place, halves_down, 0, d)
    total_in = place_share(place, halves_in, 0, mlp_in.shape[1])
    total_cout = place_share(place, halves_cross, 0, d)
    total_cq = place_share(place, halves_cross, d, d)
    total_ckv = place_share(place, halves_cross, 2 * d, 2 * d)
    total_out = place_share(place, halves_cross, 4 * d, d)
    total_qkv = place_share(place, halves_attn, 0, 3 * d)
    grad_gains = jnp.stack(
        [
            gain_gradient(attn_qkv, total_qkv, norm_gains[0]),
            gain_gradient(cross_q, total_cq, norm_gains[1]),
            gain_gradient(mlp_in, total_in, norm_gains[2]),
        ]
    )
    return (
        layer_out[None],
        grad_input[None],
        grad_enc.reshape(neighbours.shape),
        grad_gains,
        total_qkv,
        total_out,
        total_cq,
        total_ckv,
        total_cout,
        total_in,
        total_down,
    )


def solution(mesh):
    return jax.shard_map(
        local,
        mesh=mesh,
        in_specs=(
            P("fsdp", "ctx", None),
            P("fsdp", "ctx", None, None),
            P("fsdp", "ctx", None),
            P("fsdp", None),
            P("fsdp", None),
            P(None, "fsdp"),
            P("fsdp", None),
            P("fsdp", None),
            P("fsdp", None),
            P("fsdp", None),
            P("fsdp", None),
            P("fsdp", None),
            P("fsdp", None),
        ),
        out_specs=(
            P("fsdp", "ctx", None),
            P("fsdp", "ctx", None),
            P("fsdp", "ctx", None, None),
            P(None, "fsdp"),
            P("fsdp", None),
            P("fsdp", None),
            P("fsdp", None),
            P("fsdp", None),
            P("fsdp", None),
            P("fsdp", None),
            P("fsdp", None),
        ),
        check_vma=False,
    )
```

```python
import functools

import jax
import jax.numpy as jnp
from jax import lax
from jax.experimental import pallas as pl
from jax.experimental.pallas import tpu as pltpu
from jax.sharding import PartitionSpec as P

H = 12
STRETCH = 64


NORM_EPS = 1e-06
MASKED_SCORE = -1e30
KEY_BLOCK = 1024


def lasting(microseconds):
    return pl.CostEstimate(
        flops=int(microseconds * 1.15e10), bytes_accessed=int(microseconds * 1e6), transcendentals=0
    )


def to_low(values):
    return values.astype(jnp.bfloat16)


def matmul(left, right):
    return jnp.dot(left, right, preferred_element_type=jnp.float32)


def left_product(left, right):
    return lax.dot_general(left, right, (((0,), (0,)), ((), ())), preferred_element_type=jnp.float32)


def right_product(left, right):
    return lax.dot_general(left, right, (((1,), (1,)), ((), ())), preferred_element_type=jnp.float32)


def inverse_rms(values):
    return lax.rsqrt(jnp.mean(values * values, axis=-1, keepdims=True) + NORM_EPS)


def rms_back(values, scale, gain, grad):
    gained = gain * grad
    along = jnp.mean(gained * values, axis=-1, keepdims=True)
    return scale * gained - values * (scale * scale * scale) * along


def head_rows(rows, head_size):
    wide = rows.astype(jnp.float32)
    lane = lax.broadcasted_iota(jnp.int32, wide.shape, 1)
    first = jnp.where(lane < head_size, wide, 0.0)
    second = jnp.where(lane >= head_size, wide, 0.0)
    return to_low(jnp.concatenate([first, second], axis=0))


def join_heads(columns, head_size):
    tok_count = columns.shape[1] // 2
    return jnp.concatenate(
        [columns[:head_size, :tok_count], columns[head_size:, tok_count:]], axis=0
    ).T


def self_scores(query, key, key_pos, low_pos, high_pos, score_scale):
    scores = right_product(key, query) * score_scale
    return jnp.where((key_pos >= low_pos) & (key_pos <= high_pos), scores, MASKED_SCORE)


def self_forward_kernel(
    head_size, blocks, q_ref, k_ref, v_ref, pos_ref, low_ref, high_ref, o_ref, lse_ref
):
    score_scale = head_size ** (-0.5)
    query = head_rows(q_ref[...], head_size)
    low_pos, high_pos = low_ref[...], high_ref[...]
    rows = k_ref.shape[0] // blocks

    def scores_of(index):
        span = pl.ds(pl.multiple_of(index * rows, rows), rows)
        return self_scores(query, k_ref[span, :], pos_ref[span, :], low_pos, high_pos, score_scale)

    def values_of(index):
        return v_ref[pl.ds(pl.multiple_of(index * rows, rows), rows), :]

    if blocks == 1:
        scores = scores_of(0)
        peak = jnp.max(scores, axis=0, keepdims=True)
        weights = jnp.exp(scores - peak)
        total = jnp.sum(weights, axis=0, keepdims=True)
        running = left_product(values_of(0), to_low(weights))
    else:
        peak = lax.fori_loop(
            0,
            blocks,
            lambda i, top: jnp.maximum(top, jnp.max(scores_of(i), axis=0, keepdims=True)),
            jnp.full((1, query.shape[0]), MASKED_SCORE, jnp.float32),
        )

        def add(index, state):
            total, running = state
            weights = jnp.exp(scores_of(index) - peak)
            return (
                total + jnp.sum(weights, axis=0, keepdims=True),
                running + left_product(values_of(index), to_low(weights)),
            )

        total, running = lax.fori_loop(
            0,
            blocks,
            add,
            (
                jnp.zeros((1, query.shape[0]), jnp.float32),
                jnp.zeros((2 * head_size, query.shape[0]), jnp.float32),
            ),
        )
    o_ref[...] = to_low(join_heads(running / total, head_size))
    lse_ref[0] = peak + jnp.log(total)


def self_backward_kernel(
    head_size,
    blocks,
    q_ref,
    k_ref,
    v_ref,
    do_ref,
    pos_ref,
    low_ref,
    high_ref,
    lse_ref,
    dq_ref,
    dkv_ref,
):
    score_scale = head_size ** (-0.5)
    query = head_rows(q_ref[...], head_size)
    grad = head_rows(do_ref[...], head_size)
    low_pos, high_pos = low_ref[...], high_ref[...]
    log_total = lse_ref[0]
    rows = k_ref.shape[0] // blocks

    def span_of(index):
        return pl.ds(pl.multiple_of(index * rows, rows), rows)

    def pair_of(index):
        span = span_of(index)
        scores = self_scores(
            query, k_ref[span, :], pos_ref[span, :], low_pos, high_pos, score_scale
        )
        return jnp.exp(scores - log_total), right_product(v_ref[span, :], grad)

    def finish(index, probs, dprobs, delta):
        span = span_of(index)
        dscores = to_low(probs * (dprobs - delta))
        dkv_ref[0, span, :] = to_low(score_scale * matmul(dscores, query))
        dkv_ref[1, span, :] = to_low(matmul(to_low(probs), grad))
        return left_product(k_ref[span, :], dscores)

    if blocks == 1:
        probs, dprobs = pair_of(0)
        delta = jnp.sum(probs * dprobs, axis=0, keepdims=True)
        columns = finish(0, probs, dprobs, delta)
    else:

        def add_delta(index, delta):
            probs, dprobs = pair_of(index)
            return delta + jnp.sum(probs * dprobs, axis=0, keepdims=True)

        delta = lax.fori_loop(
            0, blocks, add_delta, jnp.zeros((1, query.shape[0]), jnp.float32)
        )

        def add_query(index, columns):
            probs, dprobs = pair_of(index)
            return columns + finish(index, probs, dprobs, delta)

        columns = lax.fori_loop(
            0, blocks, add_query, jnp.zeros((2 * head_size, query.shape[0]), jnp.float32)
        )
    dq_ref[...] = to_low(score_scale * join_heads(columns, head_size))


def self_specs(tok_count, key_count, pairs):
    wide = 128
    return (
        pl.BlockSpec((tok_count, wide), lambda i: (0, i)),
        pl.BlockSpec((key_count, wide), lambda i: (0, i)),
        pl.BlockSpec((key_count, wide), lambda i: (0, pairs + i)),
        pl.BlockSpec((key_count, 1), lambda i: (0, 0)),
        pl.BlockSpec((1, 2 * tok_count), lambda i: (0, 0)),
        pl.BlockSpec((1, 1, 2 * tok_count), lambda i: (i, 0, 0)),
    )


def self_forward(query, key_value, key_pos, low_pos, high_pos):
    tok_count, feature_width = query.shape
    key_count = key_value.shape[0]
    head_size = feature_width // H
    pairs = H // 2
    blocks = max(1, key_count // KEY_BLOCK)
    rows, keys, values, pos, edge, lse = self_specs(tok_count, key_count, pairs)
    return pl.pallas_call(
        functools.partial(self_forward_kernel, head_size, blocks),
        grid=(pairs,),
        in_specs=[rows, keys, values, pos, edge, edge],
        out_specs=[rows, lse],
        out_shape=[
            jax.ShapeDtypeStruct((tok_count, feature_width), jnp.bfloat16),
            jax.ShapeDtypeStruct((pairs, 1, 2 * tok_count), jnp.float32),
        ],
        cost_estimate=lasting(7.6),
        name="self_forward",
    )(query, key_value, key_value, key_pos, low_pos, high_pos)


def self_backward(query, key_value, grad, key_pos, low_pos, high_pos, log_total):
    tok_count, feature_width = query.shape
    key_count = key_value.shape[0]
    head_size = feature_width // H
    pairs = H // 2
    blocks = max(1, key_count // KEY_BLOCK)
    rows, keys, values, pos, edge, lse = self_specs(tok_count, key_count, pairs)
    return pl.pallas_call(
        functools.partial(self_backward_kernel, head_size, blocks),
        grid=(pairs,),
        in_specs=[rows, keys, values, rows, pos, edge, edge, lse],
        out_specs=[rows, pl.BlockSpec((2, key_count, 128), lambda i: (0, 0, i))],
        out_shape=[
            jax.ShapeDtypeStruct((tok_count, feature_width), jnp.bfloat16),
            jax.ShapeDtypeStruct((2, key_count, feature_width), jnp.bfloat16),
        ],
        cost_estimate=lasting(10.2),
        name="self_backward",
    )(query, key_value, key_value, grad, key_pos, low_pos, high_pos, log_total)


WHOLE = ((0, None), (1, None), (2, None), (3, None))
HALVES = ((0, None), (1, None), (2, 0), (2, 1), (3, 0), (3, 1))


def bases_of(pieces):
    return WHOLE if len(pieces) == len(WHOLE) else HALVES


def fill(out_ref, pieces, index_ref, columns=slice(None)):
    rows = pieces[0].shape[0]
    for piece, (j, half) in zip(pieces, bases_of(pieces)):
        place = (index_ref[0] ^ j) * rows
        if half is not None:
            place = place + ((index_ref[1] % 2) ^ half) * (rows // 2)
        part = piece[:, columns].astype(out_ref.dtype)
        out_ref[pl.ds(pl.multiple_of(place, 16), piece.shape[0]), :] = part


def whole(value):
    zeros = (0,) * value.ndim
    return pl.BlockSpec(value.shape, lambda *_: zeros)


def chain_call(kernel, name, grid, index, inputs, outputs, scratch, microseconds):
    return pl.pallas_call(
        kernel,
        grid_spec=pltpu.PrefetchScalarGridSpec(
            num_scalar_prefetch=1,
            grid=grid,
            in_specs=[spec for _, spec in inputs],
            out_specs=[spec for _, _, spec in outputs],
            scratch_shapes=scratch,
        ),
        out_shape=[jax.ShapeDtypeStruct(shape, dtype) for shape, dtype, _ in outputs],
        cost_estimate=lasting(microseconds),
        name=name,
    )(index, *[value for value, _ in inputs])


def const(shape):
    zeros = (0,) * len(shape)
    return pl.BlockSpec(shape, lambda *_: zeros)


def project_kernel(layout, tok, pieces, index_ref, *refs):
    row_refs, refs = refs[: len(layout)], refs[len(layout) :]
    piece_refs, refs = refs[:pieces], refs[pieces:]
    q_ref, kv_ref, norm_ref, w_ref, gain_ref, rows_ref, column_ref = refs
    width = q_ref.shape[1]
    step = pl.program_id(0)

    @pl.when(step == 0)
    def _():
        for row_ref, moves in zip(row_refs, layout):
            for start, place, count in moves:
                rows_ref[pl.ds(place, count), :] = row_ref[pl.ds(start, count), :]
        fill(w_ref, piece_refs, index_ref, slice(0, 3 * width))
        fill(column_ref, piece_refs, index_ref, slice(3 * width, 3 * width + 128))
        gain_ref[...] = column_ref[...].T[: gain_ref.shape[0], :]

    count = norm_ref.shape[0]
    values = rows_ref[pl.ds(pl.multiple_of(step * count, count), count), :].astype(jnp.float32)
    norm = to_low(values * inverse_rms(values) * gain_ref[0:1, :])
    norm_ref[...] = norm
    kv_ref[...] = to_low(matmul(norm, w_ref[:, width:]))

    @pl.when(step == 0)
    def _():
        q_ref[...] = to_low(matmul(norm_ref[pl.ds(0, tok), :], w_ref[:, :width]))


def project(index, row_pieces, layout, pieces, tok):
    width = row_pieces[0].shape[1]
    total = sum(piece.shape[0] for piece in row_pieces)
    block = min(512, total)
    inputs = [(value, whole(value)) for value in (*row_pieces, *pieces)]
    outputs = [
        ((tok, width), jnp.bfloat16, const((tok, width))),
        ((total, 2 * width), jnp.bfloat16, pl.BlockSpec((block, 2 * width), lambda i, _: (i, 0))),
        ((total, width), jnp.bfloat16, pl.BlockSpec((block, width), lambda i, _: (i, 0))),
        ((width, 3 * width), jnp.bfloat16, const((width, 3 * width))),
        ((8, width), jnp.float32, const((8, width))),
    ]
    scratch = [pltpu.VMEM((total, width), jnp.bfloat16), pltpu.VMEM((width, 128), jnp.float32)]
    return chain_call(
        functools.partial(project_kernel, layout, tok, len(pieces)),
        "project",
        (total // block,),
        index,
        inputs,
        outputs,
        scratch,
        9.6,
    )


def attend_out_kernel(pieces, index_ref, att_ref, own_ref, gain_ref, *refs):
    piece_refs, (after_ref, norm_ref, query_ref, w_ref) = refs[:pieces], refs[pieces:]
    width = att_ref.shape[1]
    fill(w_ref, piece_refs, index_ref)
    rows = own_ref[...].astype(jnp.float32) + matmul(att_ref[...], w_ref[:, :width])
    after_ref[...] = rows
    norm = to_low(rows * inverse_rms(rows) * gain_ref[1:2, :])
    norm_ref[...] = norm
    query_ref[...] = to_low(matmul(norm, w_ref[:, width:]))


def attend_out(index, attended, own, gain_rows, pieces):
    tok, width = attended.shape
    inputs = [(value, whole(value)) for value in (attended, own, gain_rows)]
    inputs += [
        (piece, pl.BlockSpec((piece.shape[0], 2 * width), lambda *_: (0, 0))) for piece in pieces
    ]
    outputs = [
        ((tok, width), jnp.float32, const((tok, width))),
        ((tok, width), jnp.bfloat16, const((tok, width))),
        ((tok, width), jnp.bfloat16, const((tok, width))),
        ((width, 2 * width), jnp.bfloat16, const((width, 2 * width))),
    ]
    return chain_call(
        functools.partial(attend_out_kernel, len(pieces)),
        "attend_out",
        (1,),
        index,
        inputs,
        outputs,
        [],
        4.4,
    )


def cross_forward_kernel(head_size, stretches, pieces, index_ref, *refs):
    q_ref, enc_ref, rows_ref, keep_ref, gain_ref = refs[:5]
    refs = refs[5:]
    key_refs, value_refs = refs[:pieces], refs[pieces : 2 * pieces]
    out_refs, refs = refs[2 * pieces : 3 * pieces], refs[3 * pieces :]
    kv_ref, cross_ref, after_ref, norm_ref, wkv_ref, wout_ref = refs
    score_scale = head_size ** (-0.5)
    pair = pl.program_id(0)
    wide = q_ref.shape[1]
    fill(wkv_ref.at[0], key_refs, index_ref)
    fill(wkv_ref.at[1], value_refs, index_ref)
    kv_ref[0] = to_low(matmul(enc_ref[...], wkv_ref[0]))
    kv_ref[1] = to_low(matmul(enc_ref[...], wkv_ref[1]))

    @pl.when(pair == 0)
    def _():
        fill(wout_ref, out_refs, index_ref)

    keys = enc_ref.shape[0] // stretches
    parts = []
    for s in range(stretches):
        span = pl.ds(s * keys, keys)
        query = head_rows(q_ref[pl.ds(s * STRETCH, STRETCH), :], head_size)
        scores = right_product(kv_ref[0, span, :], query) * score_scale
        weights = jnp.exp(scores - jnp.max(scores, axis=0, keepdims=True))
        probs = to_low(weights / jnp.sum(weights, axis=0, keepdims=True))
        parts.append(join_heads(left_product(kv_ref[1, span, :], probs), head_size))
    columns = pl.ds(pl.multiple_of(pair * wide, wide), wide)
    cross_ref[:, columns] = to_low(jnp.concatenate(parts, axis=0))

    @pl.when(pair == pl.num_programs(0) - 1)
    def _():
        rows = rows_ref[...] + keep_ref[...] * matmul(cross_ref[...], wout_ref[...])
        after_ref[...] = rows
        norm_ref[...] = to_low(rows * inverse_rms(rows) * gain_ref[2:3, :])


def cross_forward(index, query, enc_rows, after_attn, keep_rows, gain_rows, pieces, stretches):
    tok, width = query.shape
    pairs = H // 2
    keys = enc_rows.shape[0]
    inputs = [(query, pl.BlockSpec((tok, 128), lambda i, _: (0, i)))]
    inputs += [(value, whole(value)) for value in (enc_rows, after_attn, keep_rows, gain_rows)]
    for first in (0, pairs):
        inputs += [
            (piece, pl.BlockSpec((piece.shape[0], 128), lambda i, _, f=first: (0, f + i)))
            for piece in pieces
        ]
    inputs += [(piece, pl.BlockSpec((piece.shape[0], width), lambda i, _: (0, 2))) for piece in pieces]
    outputs = [
        ((2, keys, width), jnp.bfloat16, pl.BlockSpec((2, keys, 128), lambda i, _: (0, 0, i))),
        ((tok, width), jnp.bfloat16, const((tok, width))),
        ((tok, width), jnp.float32, const((tok, width))),
        ((tok, width), jnp.bfloat16, const((tok, width))),
        ((2, width, width), jnp.bfloat16, pl.BlockSpec((2, width, 128), lambda i, _: (0, 0, i))),
        ((width, width), jnp.bfloat16, const((width, width))),
    ]
    return chain_call(
        functools.partial(cross_forward_kernel, width // H, stretches, len(pieces)),
        "cross_forward",
        (pairs,),
        index,
        inputs,
        outputs,
        [],
        12.3,
    )


ERF_ABOVE = (
    -2.72614225801306e-10, 2.77068142495902e-08, -2.10102402082508e-06, -5.69250639462346e-05,
    -7.34990630326855e-04, -2.95459980854025e-03, -1.60960333262415e-02,
)
ERF_BELOW = (
    -1.45660718464996e-05, -2.13374055278905e-04, -1.68282697438203e-03, -7.37332916720468e-03,
    -1.42647390514189e-02,
)


def erf(values):
    values = jnp.clip(values, -4.0, 4.0)
    square = values * values
    above, below = ERF_ABOVE[0], ERF_BELOW[0]
    for factor in ERF_ABOVE[1:]:
        above = above * square + factor
    for factor in ERF_BELOW[1:]:
        below = below * square + factor
    return values * above / below


def mlp_kernel(tok, chunks, index_ref, *refs):
    norms, cots, pieces, (down_ref,) = refs[:4], refs[4:8], refs[8:12], refs[12:13]
    (
        grad_own_ref, grad_across_ref, grad_send_ref, out_own_ref, out_across_ref, out_send_ref,
        down_share_ref, keep_ref, send_ref, w_ref, held_ref, norm_all, cot_all, act_all, inner_all,
    ) = refs[13:]
    fill(w_ref, pieces, index_ref)
    for k in range(4):
        norm_all[pl.ds(k * tok, tok), :] = norms[k][...]
        cot_all[pl.ds(k * tok, tok), :] = cots[k][...]
    for k in range(2):
        rows = pl.ds(2 * k * tok, 2 * tok)
        inner = matmul(norm_all[rows, :], w_ref[...])
        share_below = 0.5 * (1.0 + erf(inner * (2.0**-0.5)))
        activation = to_low(inner * share_below)
        act_all[rows, :] = activation
        slope = share_below + inner * jnp.exp(-0.5 * inner * inner) * ((2.0 * jnp.pi) ** -0.5)
        grad_inner = to_low(right_product(cot_all[rows, :], down_ref[...]) * slope)
        inner_all[rows, :] = grad_inner
        grad = right_product(grad_inner, w_ref[...])
        out = matmul(activation, down_ref[...])
        for own_ref, across_ref, send_refs, value in (
            (grad_own_ref, grad_across_ref, grad_send_ref, grad),
            (out_own_ref, out_across_ref, out_send_ref, out),
        ):
            if k == 0:
                own_ref[...] = value[:tok]
            else:
                across_ref[...] = value[:tok]
            send_refs[k] = to_low(value[tok:])
    depth = down_ref.shape[0]
    held_ref[...] = left_product(act_all[...], cot_all[...])
    store_chunks(down_share_ref, 0, held_ref, 0, depth, index_ref[2], chunks[1])
    held_ref[...] = left_product(norm_all[...], inner_all[...])
    rows = depth // 4
    for out_ref, order in ((keep_ref, (0, 2)), (send_ref, (1, 3))):
        for k, j in enumerate(order):
            store_chunks(
                out_ref, k * rows, held_ref, (index_ref[0] ^ j) * rows, rows, index_ref[2], chunks[0]
            )


def mlp_share(index, norms, cots, pieces, w_down):
    depth, width = w_down.shape
    tok = norms[0][2]
    chunks = (chunk_count(width // len(WHOLE)), chunk_count(depth))
    inputs = []
    for value, start, count in (*norms, *cots, *pieces):
        inputs.append((value, pl.BlockSpec((count, depth), lambda *_, s=start // count: (s, 0))))
    inputs.append((w_down, whole(w_down)))
    token_f32 = ((tok, width), jnp.float32, const((tok, width)))
    token_send = ((2, tok, width), jnp.bfloat16, const((2, tok, width)))
    rows = ((width // 2, depth), jnp.bfloat16, const((width // 2, depth)))
    outputs = [token_f32, token_f32, token_send, token_f32, token_f32, token_send]
    outputs += [((depth, width), jnp.bfloat16, const((depth, width))), rows, rows]
    scratch = [pltpu.VMEM((width, depth), jnp.bfloat16), pltpu.VMEM((depth, depth), jnp.float32)]
    scratch += [pltpu.VMEM((4 * tok, depth), jnp.bfloat16)] * 4
    return chain_call(
        functools.partial(mlp_kernel, tok, chunks),
        "mlp_share",
        (1,),
        index,
        inputs,
        outputs,
        scratch,
        14.0,
    )


def inner_out_kernel(index_ref, own_ref, far_ref, weight_ref, gain_ref, out_ref, sum_ref):
    half = own_ref.shape[0]
    upper = index_ref[1] % 2
    own = own_ref[...].astype(jnp.float32)
    far = far_ref[...].astype(jnp.float32)
    out_ref[pl.ds(pl.multiple_of(upper * half, 8), half), :] = own
    out_ref[pl.ds(pl.multiple_of((1 - upper) * half, 8), half), :] = far
    part = jnp.sum(weight_ref[...].astype(jnp.float32) * out_ref[...], axis=1, keepdims=True)
    part = part / gain_ref[...]

    @pl.when(pl.program_id(0) == 0)
    def _():
        sum_ref[...] = part

    @pl.when(pl.program_id(0) > 0)
    def _():
        sum_ref[...] = sum_ref[...] + part


def inner_out(index, halves, weight, gain):
    own, far = halves
    rows, full = weight.shape
    depth = full // len(WHOLE)
    block = pl.BlockSpec((rows // 2, depth), lambda t, index_ref: (0, t ^ index_ref[0]))
    column = gain.astype(jnp.float32).reshape(rows, 1)
    inputs = [(own, block), (far, block)]
    inputs += [(weight, pl.BlockSpec((rows, depth), lambda t, _: (0, t))), (column, whole(column))]
    outputs = [
        ((rows, full), jnp.float32, pl.BlockSpec((rows, depth), lambda t, _: (0, t))),
        ((rows, 1), jnp.float32, const((rows, 1))),
    ]
    total, sums = chain_call(
        inner_out_kernel, "inner_out", (len(WHOLE),), index, inputs, outputs, [], 3.0
    )
    return total, sums.reshape(rows)


def cross_backward_kernel(head_size, stretches, index_ref, *refs):
    q_ref, kv_ref, cot_ref, part0, part1, part2, cross_ref, wout_ref, keep_ref = refs[:9]
    w_ref, rows_ref, gain_ref = refs[9:12]
    dq_ref, dkv_ref, out_ref, branch_ref, attended_ref, first_ref, grad_ref, do_ref = refs[12:]
    score_scale = head_size ** (-0.5)
    pair = pl.program_id(0)
    wide = q_ref.shape[1]
    keys = kv_ref.shape[1] // stretches
    columns = pl.ds(pl.multiple_of(pair * wide, wide), wide)

    @pl.when(pair == 0)
    def _():
        values = cross_ref[...]
        grad_norm = (
            part0[...] + part1[...].astype(jnp.float32) + part2[...].astype(jnp.float32)
        )
        grad = cot_ref[...].astype(jnp.float32) + rms_back(
            values, inverse_rms(values), gain_ref[2:3, :], grad_norm
        )
        grad_ref[...] = grad
        branch = to_low(keep_ref[...] * grad)
        first_ref[...] = branch
        do_ref[...] = to_low(right_product(branch, wout_ref[...]))

    parts = []
    for s in range(stretches):
        rows = pl.ds(s * STRETCH, STRETCH)
        span = pl.ds(s * keys, keys)
        query = head_rows(q_ref[rows, :], head_size)
        grad = head_rows(do_ref[rows, columns], head_size)
        scores = right_product(kv_ref[0, span, :], query) * score_scale
        weights = jnp.exp(scores - jnp.max(scores, axis=0, keepdims=True))
        probs = weights / jnp.sum(weights, axis=0, keepdims=True)
        dprobs = right_product(kv_ref[1, span, :], grad)
        delta = jnp.sum(probs * dprobs, axis=0, keepdims=True)
        dscores = to_low(probs * (dprobs - delta))
        dkv_ref[0, span, :] = to_low(score_scale * matmul(dscores, query))
        dkv_ref[1, span, :] = to_low(matmul(to_low(probs), grad))
        parts.append(join_heads(left_product(kv_ref[0, span, :], dscores), head_size))
    dq_ref[:, columns] = to_low(score_scale * jnp.concatenate(parts, axis=0))

    @pl.when(pair == pl.num_programs(0) - 1)
    def _():
        width = rows_ref.shape[1]
        values = rows_ref[...]
        grad_norm = right_product(dq_ref[...], w_ref[:, width:])
        total = grad_ref[...] + rms_back(
            values, inverse_rms(values), gain_ref[1:2, :], grad_norm
        )
        out_ref[...] = total
        branch = to_low(total)
        branch_ref[...] = branch
        attended_ref[...] = to_low(right_product(branch, w_ref[:, :width]))


def cross_backward(
    index, query, key_value, cotangent, terms, after_cross, w_cout, keep_rows, w_pair, after_attn,
    gain_rows, stretches,
):
    tok, width = query.shape
    keys = key_value.shape[1]
    block = pl.BlockSpec((tok, 128), lambda i, _: (0, i))
    planes = pl.BlockSpec((2, keys, 128), lambda i, _: (0, 0, i))
    inputs = [(query, block), (key_value, planes), (cotangent, whole(cotangent))]
    own, sibling, across = terms
    inputs += [
        (own, whole(own)),
        (sibling, pl.BlockSpec((None, tok, width), lambda *_: (0, 0, 0))),
        (across, whole(across)),
    ]
    inputs += [
        (value, whole(value))
        for value in (after_cross, w_cout, keep_rows, w_pair, after_attn, gain_rows)
    ]
    low = ((tok, width), jnp.bfloat16, const((tok, width)))
    outputs = [
        low,
        ((2, keys, width), jnp.bfloat16, planes),
        ((tok, width), jnp.float32, const((tok, width))),
        low,
        low,
        low,
    ]
    return chain_call(
        functools.partial(cross_backward_kernel, width // H, stretches),
        "cross_backward",
        (H // 2,),
        index,
        inputs,
        outputs,
        [pltpu.VMEM((tok, width), jnp.float32), pltpu.VMEM((tok, width), jnp.bfloat16)],
        13.0,
    )


def swap(values, axis, bit):
    count = lax.axis_size(axis)
    return lax.ppermute(values, axis, [(i, i ^ bit) for i in range(count)])


def after(value, *earlier):
    return lax.optimization_barrier((value,) + earlier)[0]


def mirrored(position, count):
    out = 0
    for _ in range(count.bit_length() - 1):
        out, position = 2 * out + position % 2, position // 2
    return out


def positions_kernel(
    stretches, index_ref, deal_ref, lengths_ref, pos_ref, low_ref, high_ref, keep_ref
):
    ctx_index = index_ref[1]
    held = pos_ref.shape[0] // STRETCH
    offset = lax.broadcasted_iota(jnp.int32, (STRETCH, 1), 0)
    for s in range(held):
        device = ctx_index ^ mirrored(s // stretches, held // stretches)
        given = deal_ref[device * stretches + s % stretches]
        pos_ref[pl.ds(s * STRETCH, STRETCH), :] = given * STRETCH + offset
    lane = lax.broadcasted_iota(jnp.int32, low_ref.shape, 1) % (stretches * STRETCH)
    low_pos = jnp.zeros(low_ref.shape, jnp.int32)
    high_pos = jnp.zeros(low_ref.shape, jnp.int32)
    for s in range(stretches):
        given = deal_ref[ctx_index * stretches + s]
        start, end = 0, 0
        for q in range(lengths_ref.shape[0]):
            start = jnp.where(end <= given, end, start)
            end = end + lengths_ref[q]
        here = lane // STRETCH == s
        low_pos = jnp.where(here, start * STRETCH, low_pos)
        high_pos = jnp.where(here, given * STRETCH + lane % STRETCH, high_pos)
        kept = jnp.where(given != start, 1.0, 0.0).astype(jnp.float32)
        keep_ref[pl.ds(s * STRETCH, STRETCH), :] = jnp.full((STRETCH, 1), kept, jnp.float32)
    low_ref[...] = low_pos
    high_ref[...] = high_pos


def positions(index, deal_row, lengths_row, stretches):
    tok_count = stretches * STRETCH
    smem = pl.BlockSpec(memory_space=pltpu.SMEM)
    vmem = pl.BlockSpec(memory_space=pltpu.VMEM)
    return pl.pallas_call(
        functools.partial(positions_kernel, stretches),
        in_specs=[smem] * 3,
        out_specs=[vmem] * 4,
        out_shape=[
            jax.ShapeDtypeStruct((deal_row.shape[0] * STRETCH, 1), jnp.int32),
            jax.ShapeDtypeStruct((1, 2 * tok_count), jnp.int32),
            jax.ShapeDtypeStruct((1, 2 * tok_count), jnp.int32),
            jax.ShapeDtypeStruct((tok_count, 1), jnp.float32),
        ],
        cost_estimate=lasting(1.5),
        name="positions",
    )(index, deal_row, lengths_row)


def chunk_count(rows):
    count = lax.axis_size("ctx")
    return count if count & (count - 1) == 0 and rows % (8 * count) == 0 else 1


def store_chunks(out_ref, start, held_ref, base, rows, own_chunk, chunks):
    size = rows // chunks
    for p in range(chunks):
        place = base + (own_chunk ^ p) * size
        part = held_ref[pl.ds(pl.multiple_of(place, 8), size), :]
        out_ref[pl.ds(start + p * size, size), :] = part.astype(out_ref.dtype)


def products_kernel(tiles, rows, chunks, index_ref, *refs):
    count = len(tiles)
    inputs, (keep_ref, send_ref, held_ref) = refs[:-3], refs[-3:]
    fsdp_index, own_chunk = index_ref[0], index_ref[2]
    width = held_ref.shape[1]
    for t, (left, right, column) in enumerate(tiles):

        @pl.when(pl.program_id(0) == t)
        def _(left=left, right=right, column=column):
            grads = inputs[right][:, pl.ds(column * width, width)]
            held_ref[...] = left_product(inputs[left][...], grads)

    for out_ref, order in ((keep_ref, (0, 2)), (send_ref, (1, 3))):
        for k, j in enumerate(order):
            store_chunks(
                out_ref, k * rows, held_ref, (fsdp_index ^ j) * rows, rows, own_chunk, chunks
            )


def wide_products(index, terms):
    shares = lax.axis_size("fsdp")
    inputs, tiles = [], []
    width = terms[0][0].shape[1]
    for left, right, plane in terms:
        if not inputs or all(left is not value for value, _ in inputs):
            inputs.append((left, None))
        first = next(i for i, (value, _) in enumerate(inputs) if value is left)
        inputs.append((right, plane))
        for column in range(right.shape[-1] // width):
            tiles.append((first, len(inputs) - 1, column))
    rows = width // shares
    chunks = chunk_count(rows)
    specs = []
    for value, plane in inputs:
        if value.ndim == 2:
            specs.append(pl.BlockSpec(value.shape, lambda i, _: (0, 0)))
        else:
            specs.append(
                pl.BlockSpec((None,) + value.shape[1:], lambda i, _, plane=plane: (plane, 0, 0))
            )
    total = len(tiles) * width
    out = jax.ShapeDtypeStruct((2 * rows, total), jnp.bfloat16)
    out_spec = pl.BlockSpec((2 * rows, width), lambda i, _: (0, i))
    return pl.pallas_call(
        functools.partial(products_kernel, tiles, rows, chunks),
        grid_spec=pltpu.PrefetchScalarGridSpec(
            num_scalar_prefetch=1,
            grid=(len(tiles),),
            in_specs=specs,
            out_specs=[out_spec, out_spec],
            scratch_shapes=[pltpu.VMEM((width, width), jnp.float32)],
        ),
        out_shape=[out, out],
        cost_estimate=lasting(8.2),
        name="wide_products",
    )(index, *[value for value, _ in inputs])


def add_low(*parts):
    return to_low(sum(part.astype(jnp.float32) for part in parts))


def reduction(keep, send):
    rows = keep.shape[0] // 2
    token = yield send
    received = after(swap(send, "fsdp", 1), *token)
    sent = add_low(keep[rows:], received[rows:])
    token = yield sent
    across = after(swap(sent, "fsdp", 2), *token)
    return (yield from ctx_reduction((keep[:rows], received[:rows], across)))


def in_order(index, bit, own, far):
    upper = (index & bit) != 0
    return jnp.concatenate([jnp.where(upper, far, own), jnp.where(upper, own, far)], axis=0)


def ctx_reduction(parts):
    index = lax.axis_index("ctx")
    half = parts[0].shape[0] // 2
    chunks = chunk_count(2 * half)
    if chunks == 1:
        share = lax.psum(add_low(*parts), "ctx")
        upper = (index & 1) != 0
        first, second = share[:half], share[half:]
        return jnp.where(upper, second, first), jnp.where(upper, first, second)
    bit = 1
    while bit < chunks:
        sent = add_low(*[part[half:] for part in parts])
        held = add_low(*[part[:half] for part in parts])
        token = yield sent
        parts = (held, after(swap(sent, "ctx", bit), *token))
        half, bit = half // 2, 2 * bit
    gathered = add_low(*parts)
    token = yield gathered
    while bit > 2:
        bit = bit // 2
        far = after(swap(gathered, "ctx", bit), *token)
        gathered = in_order(index, bit, gathered, far)
        token = yield gathered
    return gathered, after(swap(gathered, "ctx", 1), *token)


def finished(halves, offset, width):
    own, far = (half[:, offset : offset + width] for half in halves)
    return in_order(lax.axis_index("ctx"), 1, own, far).astype(jnp.float32)


def sum_to_owner(rows_sum):
    total = to_low(rows_sum)
    bit = 1
    while bit < lax.axis_size("ctx"):
        half = total.shape[0] // 2
        sent = total[half:]
        token = yield sent
        total = add_low(total[:half], after(swap(sent, "ctx", bit), *token))
        bit = 2 * bit
    return total


class Steps:
    def __init__(self, steps):
        self.steps = steps
        self.result = None
        self.advance(None)

    def advance(self, token):
        try:
            return self.steps.send(token)
        except StopIteration as stop:
            self.result = stop.value
            return stop.value[1] if isinstance(stop.value, tuple) else stop.value

    def move(self, *token):
        return token[0] if self.result is not None else self.advance(token)

    def finish(self, *token):
        sent = token[0]
        while self.result is None:
            sent = self.move(sent)
        return sent


def gain_gradient(weight, grad, gain):
    return jnp.sum(weight.astype(jnp.float32) * grad, axis=1) / gain.astype(jnp.float32)


def local(
    hidden,
    neighbours,
    cotangent,
    stretch_deal,
    seq_lengths,
    norm_gains,
    attn_qkv,
    attn_out,
    cross_q,
    cross_kv,
    cross_out,
    mlp_in,
    mlp_out,
):
    shares = lax.axis_size("fsdp")
    fsdp_index = lax.axis_index("fsdp")
    ctx_index = lax.axis_index("ctx")
    ctx_count = lax.axis_size("ctx")
    own_chunk, bit = 0 * ctx_index, 1
    while bit < ctx_count:
        own_chunk = 2 * own_chunk + (ctx_index & bit) // bit
        bit = 2 * bit
    place = jnp.stack([fsdp_index, ctx_index, own_chunk]).astype(jnp.int32)
    feature_width = hidden.shape[2]
    own = hidden[0]
    tok = own.shape[0]
    stretch_count = tok // STRETCH
    enc_rows = neighbours[0].reshape(-1, feature_width)
    cot = cotangent[0]

    key_pos, low_pos, high_pos, keep_rows = positions(
        place, stretch_deal[0], seq_lengths[0], stretch_count
    )

    first_share = jnp.concatenate(
        [attn_qkv, jnp.pad(norm_gains.T, ((0, 0), (0, 128 - norm_gains.shape[0])))], axis=1
    )
    own = after(own, first_share)
    across_qkv = swap(first_share, "fsdp", 2)
    if ctx_count == 8:
        far, last, near = swap(own, "ctx", 4), swap(own, "ctx", 6), swap(own, "ctx", 2)
        beside = swap(own, "ctx", 1)
        second = after(jnp.concatenate([far, near, last], axis=0), key_pos)
        row_pieces = [own, second, beside, swap(second, "ctx", 1)]
        layout = [((0, k * tok, piece.shape[0]),) for k, piece in zip((0, 1, 4, 5), row_pieces)]
        second = after(second, beside)
    else:
        first = own
        bit = ctx_count
        while bit > 2:
            bit = bit // 2
            first = jnp.concatenate([first, swap(first, "ctx", bit)], axis=0)
        row_pieces = [first, swap(first, "ctx", 1)]
        layout = [((0, k * first.shape[0], first.shape[0]),) for k in range(2)]
        second = first
    sibling_qkv = swap(after(first_share, second), "fsdp", 1)
    across_qkv = after(across_qkv, second)
    diagonal_qkv = swap(across_qkv, "fsdp", 1)
    pair_share = jnp.concatenate([attn_out, cross_q], axis=1)
    across_pair = swap(after(pair_share, second), "fsdp", 2)
    cross_share = jnp.concatenate([cross_kv, cross_out], axis=1)
    across_cross = swap(after(cross_share, across_qkv), "fsdp", 2)
    depth = mlp_out.shape[0]
    rows_in = mlp_in.shape[0]

    def block_of(j):
        return lax.dynamic_slice_in_dim(mlp_in, (fsdp_index ^ j) * depth, depth, axis=1)

    block_own = block_of(0)
    exchange_sibling = jnp.concatenate([block_of(1), cot], axis=0)
    exchange_across = jnp.concatenate([block_of(2), block_of(3), cot], axis=0)

    query, key_value, norm_all, w_qkv, gain_rows = project(
        place, row_pieces, layout, [first_share, sibling_qkv, across_qkv, diagonal_qkv], tok
    )
    across_pair = after(across_pair, query)
    diagonal_pair = swap(across_pair, "fsdp", 1)
    sibling_pair = swap(after(pair_share, query), "fsdp", 1)
    from_across = swap(after(exchange_across, across_pair), "fsdp", 2)
    attended, log_total = self_forward(query, key_value, key_pos, low_pos, high_pos)
    sibling_cross = swap(after(cross_share, attended), "fsdp", 1)
    after_attn, norm_two, cross_query, w_pair = attend_out(
        place, attended, own, gain_rows, [pair_share, sibling_pair, across_pair, diagonal_pair]
    )
    across_cross = after(across_cross, cross_query)
    diagonal_cross = swap(across_cross, "fsdp", 1)
    cross_key_value, cross_rows, after_cross, norm_three, w_ckv, w_cout = cross_forward(
        place,
        cross_query,
        enc_rows,
        after_attn,
        keep_rows,
        gain_rows,
        [cross_share, sibling_cross, across_cross, diagonal_cross],
        stretch_count,
    )
    from_sibling = swap(after(exchange_sibling, cross_query), "fsdp", 1)
    norm_across, norm_sibling = swap(norm_three, "fsdp", 2), swap(norm_three, "fsdp", 1)
    from_across = after(from_across, norm_three)
    from_diagonal = swap(from_across[rows_in:], "fsdp", 1)
    norm_diagonal = swap(norm_across, "fsdp", 1)
    cot_across = from_across[2 * rows_in :]
    (
        grad_own, grad_across, grad_send, out_own, out_across, out_send, share_down, keep_in, send_in,
    ) = mlp_share(
        place,
        [(value, 0, tok) for value in (norm_three, norm_sibling, norm_across, norm_diagonal)],
        [
            (value, 0, tok)
            for value in (cot, from_sibling[rows_in:], cot_across, from_diagonal[rows_in:])
        ],
        [
            (block_own, 0, rows_in),
            (from_sibling, 0, rows_in),
            (from_across, 0, rows_in),
            (from_diagonal, 0, rows_in),
        ],
        mlp_out,
    )

    from_sibling = swap(grad_send, "fsdp", 1)
    grad_far = swap(add_low(grad_across, from_sibling[1]), "fsdp", 2)
    down = Steps(ctx_reduction((share_down,)))
    received_in = swap(send_in, "fsdp", 1)
    (
        grad_cross_query, grad_cross_pair, grad_after_attn, grad_attn_branch, grad_attended,
        grad_cross_branch,
    ) = cross_backward(
        place,
        cross_query,
        cross_key_value,
        cot,
        (grad_own, from_sibling, grad_far),
        after_cross,
        w_cout,
        keep_rows,
        w_pair,
        after_attn,
        gain_rows,
        stretch_count,
    )
    received_in = after(received_in, grad_cross_query)
    across_in = swap(
        jnp.concatenate([keep_in[rows_in:], received_in[rows_in:]], axis=1), "fsdp", 2
    )
    ready = down.move(grad_cross_query)
    keep_cross, send_cross = wide_products(
        place,
        [
            (cross_rows, grad_cross_branch, None),
            (norm_two, grad_cross_query, None),
            (enc_rows, grad_cross_pair, 0),
            (enc_rows, grad_cross_pair, 1),
            (attended, grad_attn_branch, None),
        ],
    )
    cross = Steps(reduction(keep_cross, send_cross))
    grad_query, grad_pair = self_backward(
        query,
        key_value,
        after(grad_attended, keep_cross, ready),
        key_pos,
        low_pos,
        high_pos,
        log_total,
    )
    across_in = after(across_in, grad_query)
    inner = Steps(
        ctx_reduction(
            (jnp.concatenate([keep_in[:rows_in], received_in[:rows_in], across_in], axis=1),)
        )
    )
    ready = cross.move(down.move(grad_query))
    keep_attn, send_attn = wide_products(
        place,
        [
            (norm_all[:tok], after(grad_query, ready), None),
            (norm_all, grad_pair, 0),
            (norm_all, grad_pair, 1),
        ],
    )
    attn = Steps(reduction(keep_attn, send_attn))
    grad_pair, grad_query = lax.optimization_barrier((grad_pair, grad_query, keep_attn))[:2]
    grad_norm1_all = right_product(
        grad_pair[0], w_qkv[:, feature_width : 2 * feature_width]
    ) + right_product(grad_pair[1], w_qkv[:, 2 * feature_width :])
    norm1 = Steps(sum_to_owner(grad_norm1_all))
    out_sibling = swap(after(out_send, keep_attn), "fsdp", 1)
    grad_cross_pair = after(grad_cross_pair, grad_norm1_all)
    grad_enc = right_product(grad_cross_pair[0], w_ckv[0]) + right_product(
        grad_cross_pair[1], w_ckv[1]
    )
    out_sibling = after(out_sibling, grad_enc)
    out_far = swap(add_low(out_across, out_sibling[1]), "fsdp", 2)
    ready = grad_enc
    for step in (cross, attn, inner, down, norm1, inner, down, norm1, cross, attn):
        ready = step.move(ready)
    layer_out = after_cross + (
        out_own + out_sibling[0].astype(jnp.float32) + after(out_far, ready).astype(jnp.float32)
    )
    for step in (inner, down, norm1, cross, attn):
        ready = step.move(ready)
    ready = down.finish(ready)
    total_down = finished(down.result, 0, feature_width)
    input_rows = own.astype(jnp.float32)
    ready = norm1.finish(ready)
    grad_norm1 = (
        norm1.result.astype(jnp.float32)
        + right_product(after(grad_query, ready), w_qkv[:, :feature_width])
    )
    grad_input = grad_after_attn + rms_back(
        input_rows, inverse_rms(input_rows), gain_rows[0:1], grad_norm1
    )
    ready = after(ready, grad_input, total_down, layer_out)
    for step in (cross, attn, inner, cross, attn, inner, cross, attn):
        ready = step.move(ready)
    ready = inner.finish(ready)
    total_in, gain_three = inner_out(place, inner.result, mlp_in, norm_gains[2])
    ready = after(ready, total_in)
    while attn.result is None or cross.result is None:
        for step in (cross, attn):
            if step.result is None:
                ready = step.move(ready)
    halves_cross, halves_attn = cross.result, attn.result
    d = feature_width
    total_cout = finished(halves_cross, 0, d)
    total_cq = finished(halves_cross, d, d)
    total_ckv = finished(halves_cross, 2 * d, 2 * d)
    total_out = finished(halves_cross, 4 * d, d)
    total_qkv = finished(halves_attn, 0, 3 * d)
    grad_gains = jnp.stack(
        [
            gain_gradient(attn_qkv, total_qkv, norm_gains[0]),
            gain_gradient(cross_q, total_cq, norm_gains[1]),
            gain_three,
        ]
    )
    return (
        layer_out[None],
        grad_input[None],
        grad_enc.reshape(neighbours.shape),
        grad_gains,
        total_qkv,
        total_out,
        total_cq,
        total_ckv,
        total_cout,
        total_in,
        total_down,
    )


def solution(mesh):
    return jax.shard_map(
        local,
        mesh=mesh,
        in_specs=(
            P("fsdp", "ctx", None),
            P("fsdp", "ctx", None, None),
            P("fsdp", "ctx", None),
            P("fsdp", None),
            P("fsdp", None),
            P(None, "fsdp"),
            P("fsdp", None),
            P("fsdp", None),
            P("fsdp", None),
            P("fsdp", None),
            P("fsdp", None),
            P("fsdp", None),
            P("fsdp", None),
        ),
        out_specs=(
            P("fsdp", "ctx", None),
            P("fsdp", "ctx", None),
            P("fsdp", "ctx", None, None),
            P(None, "fsdp"),
            P("fsdp", None),
            P("fsdp", None),
            P("fsdp", None),
            P("fsdp", None),
            P("fsdp", None),
            P("fsdp", None),
            P("fsdp", None),
        ),
        check_vma=False,
    )
```

```python
import functools

import jax
import jax.numpy as jnp
from jax import lax
from jax.experimental import pallas as pl
from jax.experimental.pallas import tpu as pltpu
from jax.sharding import PartitionSpec as P

H = 12
STRETCH = 64


NORM_EPS = 1e-06
MASKED_SCORE = -1e30
KEY_BLOCK = 1024


def lasting(microseconds):
    return pl.CostEstimate(
        flops=int(microseconds * 1.15e10), bytes_accessed=int(microseconds * 1e6), transcendentals=0
    )


def to_low(values):
    return values.astype(jnp.bfloat16)


def matmul(left, right):
    return jnp.dot(left, right, preferred_element_type=jnp.float32)


def left_product(left, right):
    return lax.dot_general(left, right, (((0,), (0,)), ((), ())), preferred_element_type=jnp.float32)


def right_product(left, right):
    return lax.dot_general(left, right, (((1,), (1,)), ((), ())), preferred_element_type=jnp.float32)


def inverse_rms(values):
    return lax.rsqrt(jnp.mean(values * values, axis=-1, keepdims=True) + NORM_EPS)


def rms_back(values, scale, gain, grad):
    gained = gain * grad
    along = jnp.mean(gained * values, axis=-1, keepdims=True)
    return scale * gained - values * (scale * scale * scale) * along


def head_rows(rows, head_size):
    wide = rows.astype(jnp.float32)
    lane = lax.broadcasted_iota(jnp.int32, wide.shape, 1)
    first = jnp.where(lane < head_size, wide, 0.0)
    second = jnp.where(lane >= head_size, wide, 0.0)
    return to_low(jnp.concatenate([first, second], axis=0))


def join_heads(columns, head_size):
    tok_count = columns.shape[1] // 2
    return jnp.concatenate(
        [columns[:head_size, :tok_count], columns[head_size:, tok_count:]], axis=0
    ).T


def self_scores(query, key, key_pos, low_pos, high_pos, score_scale):
    scores = right_product(key, query) * score_scale
    return jnp.where((key_pos >= low_pos) & (key_pos <= high_pos), scores, MASKED_SCORE)


def self_forward_kernel(
    head_size, blocks, q_ref, k_ref, v_ref, pos_ref, low_ref, high_ref, o_ref, lse_ref
):
    score_scale = head_size ** (-0.5)
    query = head_rows(q_ref[...], head_size)
    low_pos, high_pos = low_ref[...], high_ref[...]
    rows = k_ref.shape[0] // blocks

    def scores_of(index):
        span = pl.ds(pl.multiple_of(index * rows, rows), rows)
        return self_scores(query, k_ref[span, :], pos_ref[span, :], low_pos, high_pos, score_scale)

    def values_of(index):
        return v_ref[pl.ds(pl.multiple_of(index * rows, rows), rows), :]

    if blocks == 1:
        scores = scores_of(0)
        peak = jnp.max(scores, axis=0, keepdims=True)
        weights = jnp.exp(scores - peak)
        total = jnp.sum(weights, axis=0, keepdims=True)
        running = left_product(values_of(0), to_low(weights))
    else:
        peak = lax.fori_loop(
            0,
            blocks,
            lambda i, top: jnp.maximum(top, jnp.max(scores_of(i), axis=0, keepdims=True)),
            jnp.full((1, query.shape[0]), MASKED_SCORE, jnp.float32),
        )

        def add(index, state):
            total, running = state
            weights = jnp.exp(scores_of(index) - peak)
            return (
                total + jnp.sum(weights, axis=0, keepdims=True),
                running + left_product(values_of(index), to_low(weights)),
            )

        total, running = lax.fori_loop(
            0,
            blocks,
            add,
            (
                jnp.zeros((1, query.shape[0]), jnp.float32),
                jnp.zeros((2 * head_size, query.shape[0]), jnp.float32),
            ),
        )
    o_ref[...] = to_low(join_heads(running / total, head_size))
    lse_ref[0] = peak + jnp.log(total)


def self_backward_kernel(
    head_size,
    blocks,
    q_ref,
    k_ref,
    v_ref,
    do_ref,
    pos_ref,
    low_ref,
    high_ref,
    lse_ref,
    dq_ref,
    dkv_ref,
):
    score_scale = head_size ** (-0.5)
    query = head_rows(q_ref[...], head_size)
    grad = head_rows(do_ref[...], head_size)
    low_pos, high_pos = low_ref[...], high_ref[...]
    log_total = lse_ref[0]
    rows = k_ref.shape[0] // blocks

    def span_of(index):
        return pl.ds(pl.multiple_of(index * rows, rows), rows)

    def pair_of(index):
        span = span_of(index)
        scores = self_scores(
            query, k_ref[span, :], pos_ref[span, :], low_pos, high_pos, score_scale
        )
        return jnp.exp(scores - log_total), right_product(v_ref[span, :], grad)

    def finish(index, probs, dprobs, delta):
        span = span_of(index)
        dscores = to_low(probs * (dprobs - delta))
        dkv_ref[0, span, :] = to_low(score_scale * matmul(dscores, query))
        dkv_ref[1, span, :] = to_low(matmul(to_low(probs), grad))
        return left_product(k_ref[span, :], dscores)

    if blocks == 1:
        probs, dprobs = pair_of(0)
        delta = jnp.sum(probs * dprobs, axis=0, keepdims=True)
        columns = finish(0, probs, dprobs, delta)
    else:

        def add_delta(index, delta):
            probs, dprobs = pair_of(index)
            return delta + jnp.sum(probs * dprobs, axis=0, keepdims=True)

        delta = lax.fori_loop(
            0, blocks, add_delta, jnp.zeros((1, query.shape[0]), jnp.float32)
        )

        def add_query(index, columns):
            probs, dprobs = pair_of(index)
            return columns + finish(index, probs, dprobs, delta)

        columns = lax.fori_loop(
            0, blocks, add_query, jnp.zeros((2 * head_size, query.shape[0]), jnp.float32)
        )
    dq_ref[...] = to_low(score_scale * join_heads(columns, head_size))


def self_specs(tok_count, key_count, pairs):
    wide = 128
    return (
        pl.BlockSpec((tok_count, wide), lambda i: (0, i)),
        pl.BlockSpec((key_count, wide), lambda i: (0, i)),
        pl.BlockSpec((key_count, wide), lambda i: (0, pairs + i)),
        pl.BlockSpec((key_count, 1), lambda i: (0, 0)),
        pl.BlockSpec((1, 2 * tok_count), lambda i: (0, 0)),
        pl.BlockSpec((1, 1, 2 * tok_count), lambda i: (i, 0, 0)),
    )


def self_forward(query, key_value, key_pos, low_pos, high_pos):
    tok_count, feature_width = query.shape
    key_count = key_value.shape[0]
    head_size = feature_width // H
    pairs = H // 2
    blocks = max(1, key_count // KEY_BLOCK)
    rows, keys, values, pos, edge, lse = self_specs(tok_count, key_count, pairs)
    return pl.pallas_call(
        functools.partial(self_forward_kernel, head_size, blocks),
        grid=(pairs,),
        in_specs=[rows, keys, values, pos, edge, edge],
        out_specs=[rows, lse],
        out_shape=[
            jax.ShapeDtypeStruct((tok_count, feature_width), jnp.bfloat16),
            jax.ShapeDtypeStruct((pairs, 1, 2 * tok_count), jnp.float32),
        ],
        cost_estimate=lasting(7.6),
        name="self_forward",
    )(query, key_value, key_value, key_pos, low_pos, high_pos)


def self_backward(query, key_value, grad, key_pos, low_pos, high_pos, log_total):
    tok_count, feature_width = query.shape
    key_count = key_value.shape[0]
    head_size = feature_width // H
    pairs = H // 2
    blocks = max(1, key_count // KEY_BLOCK)
    rows, keys, values, pos, edge, lse = self_specs(tok_count, key_count, pairs)
    return pl.pallas_call(
        functools.partial(self_backward_kernel, head_size, blocks),
        grid=(pairs,),
        in_specs=[rows, keys, values, rows, pos, edge, edge, lse],
        out_specs=[rows, pl.BlockSpec((2, key_count, 128), lambda i: (0, 0, i))],
        out_shape=[
            jax.ShapeDtypeStruct((tok_count, feature_width), jnp.bfloat16),
            jax.ShapeDtypeStruct((2, key_count, feature_width), jnp.bfloat16),
        ],
        cost_estimate=lasting(10.2),
        name="self_backward",
    )(query, key_value, key_value, grad, key_pos, low_pos, high_pos, log_total)


WHOLE = ((0, None), (1, None), (2, None), (3, None))
HALVES = ((0, None), (1, None), (2, 0), (2, 1), (3, 0), (3, 1))


def bases_of(pieces):
    return WHOLE if len(pieces) == len(WHOLE) else HALVES


def fill(out_ref, pieces, index_ref, columns=slice(None)):
    rows = pieces[0].shape[0]
    for piece, (j, half) in zip(pieces, bases_of(pieces)):
        place = (index_ref[0] ^ j) * rows
        if half is not None:
            place = place + ((index_ref[1] % 2) ^ half) * (rows // 2)
        part = piece[:, columns].astype(out_ref.dtype)
        out_ref[pl.ds(pl.multiple_of(place, 16), piece.shape[0]), :] = part


def whole(value):
    zeros = (0,) * value.ndim
    return pl.BlockSpec(value.shape, lambda *_: zeros)


def chain_call(kernel, name, grid, index, inputs, outputs, scratch, microseconds):
    return pl.pallas_call(
        kernel,
        grid_spec=pltpu.PrefetchScalarGridSpec(
            num_scalar_prefetch=1,
            grid=grid,
            in_specs=[spec for _, spec in inputs],
            out_specs=[spec for _, _, spec in outputs],
            scratch_shapes=scratch,
        ),
        out_shape=[jax.ShapeDtypeStruct(shape, dtype) for shape, dtype, _ in outputs],
        cost_estimate=lasting(microseconds),
        name=name,
    )(index, *[value for value, _ in inputs])


def const(shape):
    zeros = (0,) * len(shape)
    return pl.BlockSpec(shape, lambda *_: zeros)


def rows_kernel(layout, *refs):
    row_refs, (rows_ref, scale_ref) = refs[: len(layout)], refs[len(layout) :]
    for row_ref, places in zip(row_refs, layout):
        count = row_ref.shape[0] // len(places)
        for k, place in enumerate(places):
            rows = row_ref[pl.ds(k * count, count), :]
            rows_ref[pl.ds(place, count), :] = rows
            scale_ref[pl.ds(place, count), :] = inverse_rms(rows.astype(jnp.float32))


def held_rows(row_pieces, layout):
    total = sum(piece.shape[0] for piece in row_pieces)
    width = row_pieces[0].shape[1]
    return pl.pallas_call(
        functools.partial(rows_kernel, layout),
        out_shape=[
            jax.ShapeDtypeStruct((total, width), jnp.bfloat16),
            jax.ShapeDtypeStruct((total, 1), jnp.float32),
        ],
        cost_estimate=lasting(2.0),
        name="held_rows",
    )(*row_pieces)


def project_kernel(tok, pieces, index_ref, rows_ref, scale_ref, *refs):
    piece_refs, (q_ref, kv_ref, norm_ref, w_ref, gain_ref, column_ref) = (
        refs[:pieces],
        refs[pieces:],
    )
    width = q_ref.shape[1]
    step = pl.program_id(0)

    @pl.when(step == 0)
    def _():
        fill(w_ref, piece_refs, index_ref, slice(0, 3 * width))
        fill(column_ref, piece_refs, index_ref, slice(3 * width, 3 * width + 128))
        gain_ref[...] = column_ref[...].T[: gain_ref.shape[0], :]

    norm = to_low(rows_ref[...].astype(jnp.float32) * scale_ref[...] * gain_ref[0:1, :])
    norm_ref[...] = norm
    kv_ref[...] = to_low(matmul(norm, w_ref[:, width:]))

    @pl.when(step == 0)
    def _():
        q_ref[...] = to_low(matmul(norm_ref[pl.ds(0, tok), :], w_ref[:, :width]))


def project(index, rows, scale, pieces, tok):
    total, width = rows.shape
    block = min(512, total)

    def rows_of(columns):
        return pl.BlockSpec((block, columns), lambda i, _: (i, 0))

    inputs = [(rows, rows_of(width)), (scale, rows_of(1))]
    inputs += [(value, whole(value)) for value in pieces]
    outputs = [
        ((tok, width), jnp.bfloat16, const((tok, width))),
        ((total, 2 * width), jnp.bfloat16, rows_of(2 * width)),
        ((total, width), jnp.bfloat16, rows_of(width)),
        ((width, 3 * width), jnp.bfloat16, const((width, 3 * width))),
        ((8, width), jnp.float32, const((8, width))),
    ]
    return chain_call(
        functools.partial(project_kernel, tok, len(pieces)),
        "project",
        (total // block,),
        index,
        inputs,
        outputs,
        [pltpu.VMEM((width, 128), jnp.float32)],
        9.0,
    )


def enc_terms_kernel(index_ref, pair_ref, w_ref, out_ref):
    out_ref[...] = right_product(pair_ref[0], w_ref[0]) + right_product(pair_ref[1], w_ref[1])


def enc_terms(index, grad_pair, w_pair):
    _, total, width = grad_pair.shape
    block = min(256, total)
    inputs = [
        (grad_pair, pl.BlockSpec((2, block, width), lambda i, _: (0, i, 0))),
        (w_pair, whole(w_pair)),
    ]
    outputs = [((total, width), jnp.float32, pl.BlockSpec((block, width), lambda i, _: (i, 0)))]
    return chain_call(
        enc_terms_kernel, "enc_terms", (total // block,), index, inputs, outputs, [], 4.0
    )[0]


def norm_terms_kernel(index_ref, pair_ref, query_ref, w_ref, out_ref, own_ref):
    width = out_ref.shape[1]
    out_ref[...] = to_low(
        right_product(pair_ref[0], w_ref[:, width : 2 * width])
        + right_product(pair_ref[1], w_ref[:, 2 * width :])
    )

    @pl.when(pl.program_id(0) == 0)
    def _():
        own_ref[...] = right_product(query_ref[...], w_ref[:, :width])


def norm_terms(index, grad_pair, grad_query, w_qkv):
    _, total, width = grad_pair.shape
    tok = grad_query.shape[0]
    block = min(512, total)
    inputs = [
        (grad_pair, pl.BlockSpec((2, block, width), lambda i, _: (0, i, 0))),
        (grad_query, whole(grad_query)),
        (w_qkv, whole(w_qkv)),
    ]
    outputs = [
        ((total, width), jnp.bfloat16, pl.BlockSpec((block, width), lambda i, _: (i, 0))),
        ((tok, width), jnp.float32, const((tok, width))),
    ]
    return chain_call(
        norm_terms_kernel, "norm_terms", (total // block,), index, inputs, outputs, [], 0.01
    )


def attend_out_kernel(pieces, index_ref, att_ref, own_ref, gain_ref, *refs):
    piece_refs, (after_ref, norm_ref, query_ref, w_ref) = refs[:pieces], refs[pieces:]
    width = att_ref.shape[1]
    fill(w_ref, piece_refs, index_ref)
    rows = own_ref[...].astype(jnp.float32) + matmul(att_ref[...], w_ref[:, :width])
    after_ref[...] = rows
    norm = to_low(rows * inverse_rms(rows) * gain_ref[1:2, :])
    norm_ref[...] = norm
    query_ref[...] = to_low(matmul(norm, w_ref[:, width:]))


def attend_out(index, attended, own, gain_rows, pieces):
    tok, width = attended.shape
    inputs = [(value, whole(value)) for value in (attended, own, gain_rows)]
    inputs += [
        (piece, pl.BlockSpec((piece.shape[0], 2 * width), lambda *_: (0, 0))) for piece in pieces
    ]
    outputs = [
        ((tok, width), jnp.float32, const((tok, width))),
        ((tok, width), jnp.bfloat16, const((tok, width))),
        ((tok, width), jnp.bfloat16, const((tok, width))),
        ((width, 2 * width), jnp.bfloat16, const((width, 2 * width))),
    ]
    return chain_call(
        functools.partial(attend_out_kernel, len(pieces)),
        "attend_out",
        (1,),
        index,
        inputs,
        outputs,
        [],
        4.4,
    )


def cross_forward_kernel(head_size, stretches, pieces, index_ref, *refs):
    q_ref, enc_ref, rows_ref, keep_ref, gain_ref = refs[:5]
    refs = refs[5:]
    key_refs, value_refs = refs[:pieces], refs[pieces : 2 * pieces]
    out_refs, refs = refs[2 * pieces : 3 * pieces], refs[3 * pieces :]
    kv_ref, cross_ref, after_ref, norm_ref, wkv_ref, wout_ref = refs
    score_scale = head_size ** (-0.5)
    pair = pl.program_id(0)
    wide = q_ref.shape[1]
    fill(wkv_ref.at[0], key_refs, index_ref)
    fill(wkv_ref.at[1], value_refs, index_ref)
    kv_ref[0] = to_low(matmul(enc_ref[...], wkv_ref[0]))
    kv_ref[1] = to_low(matmul(enc_ref[...], wkv_ref[1]))

    @pl.when(pair == 0)
    def _():
        fill(wout_ref, out_refs, index_ref)

    keys = enc_ref.shape[0] // stretches
    parts = []
    for s in range(stretches):
        span = pl.ds(s * keys, keys)
        query = head_rows(q_ref[pl.ds(s * STRETCH, STRETCH), :], head_size)
        scores = right_product(kv_ref[0, span, :], query) * score_scale
        weights = jnp.exp(scores - jnp.max(scores, axis=0, keepdims=True))
        probs = to_low(weights / jnp.sum(weights, axis=0, keepdims=True))
        parts.append(join_heads(left_product(kv_ref[1, span, :], probs), head_size))
    columns = pl.ds(pl.multiple_of(pair * wide, wide), wide)
    cross_ref[:, columns] = to_low(jnp.concatenate(parts, axis=0))

    @pl.when(pair == pl.num_programs(0) - 1)
    def _():
        rows = rows_ref[...] + keep_ref[...] * matmul(cross_ref[...], wout_ref[...])
        after_ref[...] = rows
        norm_ref[...] = to_low(rows * inverse_rms(rows) * gain_ref[2:3, :])


def cross_forward(index, query, enc_rows, after_attn, keep_rows, gain_rows, pieces, stretches):
    tok, width = query.shape
    pairs = H // 2
    keys = enc_rows.shape[0]
    inputs = [(query, pl.BlockSpec((tok, 128), lambda i, _: (0, i)))]
    inputs += [(value, whole(value)) for value in (enc_rows, after_attn, keep_rows, gain_rows)]
    for first in (0, pairs):
        inputs += [
            (piece, pl.BlockSpec((piece.shape[0], 128), lambda i, _, f=first: (0, f + i)))
            for piece in pieces
        ]
    inputs += [(piece, pl.BlockSpec((piece.shape[0], width), lambda i, _: (0, 2))) for piece in pieces]
    outputs = [
        ((2, keys, width), jnp.bfloat16, pl.BlockSpec((2, keys, 128), lambda i, _: (0, 0, i))),
        ((tok, width), jnp.bfloat16, const((tok, width))),
        ((tok, width), jnp.float32, const((tok, width))),
        ((tok, width), jnp.bfloat16, const((tok, width))),
        ((2, width, width), jnp.bfloat16, pl.BlockSpec((2, width, 128), lambda i, _: (0, 0, i))),
        ((width, width), jnp.bfloat16, const((width, width))),
    ]
    return chain_call(
        functools.partial(cross_forward_kernel, width // H, stretches, len(pieces)),
        "cross_forward",
        (pairs,),
        index,
        inputs,
        outputs,
        [],
        12.3,
    )


ERF_ABOVE = (
    -2.72614225801306e-10, 2.77068142495902e-08, -2.10102402082508e-06, -5.69250639462346e-05,
    -7.34990630326855e-04, -2.95459980854025e-03, -1.60960333262415e-02,
)
ERF_BELOW = (
    -1.45660718464996e-05, -2.13374055278905e-04, -1.68282697438203e-03, -7.37332916720468e-03,
    -1.42647390514189e-02,
)


def erf(values):
    values = jnp.clip(values, -4.0, 4.0)
    square = values * values
    above, below = ERF_ABOVE[0], ERF_BELOW[0]
    for factor in ERF_ABOVE[1:]:
        above = above * square + factor
    for factor in ERF_BELOW[1:]:
        below = below * square + factor
    return values * above / below


def mlp_kernel(tok, chunks, index_ref, *refs):
    norms, cot_ref, block_ref, exchanged, down_ref = refs[:4], refs[4], refs[5], refs[6:9], refs[9]
    grad_refs, out_own_ref, out_across_ref, out_send_ref = refs[10:14], refs[14], refs[15], refs[16]
    down_share_ref, keep_ref, send_ref, w_ref, held_ref, norm_all, cot_all, act_all, inner_all = refs[
        17:
    ]
    rows_in = block_ref.shape[0]
    starts = (0, 0, rows_in)
    blocks = [ref.at[pl.ds(start, rows_in), :] for ref, start in zip(exchanged, starts)]
    fill(w_ref, [block_ref, *blocks], index_ref)
    cot_all[pl.ds(0, tok), :] = cot_ref[...]
    for k, ref in enumerate(exchanged):
        start = ref.shape[0] - tok
        cot_all[pl.ds((k + 1) * tok, tok), :] = ref[pl.ds(start, tok), :]
    for k in range(4):
        norm_all[pl.ds(k * tok, tok), :] = norms[k][...]
    for k in range(2):
        rows = pl.ds(2 * k * tok, 2 * tok)
        inner = matmul(norm_all[rows, :], w_ref[...])
        share_below = 0.5 * (1.0 + erf(inner * (2.0**-0.5)))
        activation = to_low(inner * share_below)
        act_all[rows, :] = activation
        slope = share_below + inner * jnp.exp(-0.5 * inner * inner) * ((2.0 * jnp.pi) ** -0.5)
        grad_inner = to_low(right_product(cot_all[rows, :], down_ref[...]) * slope)
        inner_all[rows, :] = grad_inner
        grad = right_product(grad_inner, w_ref[...])
        out = matmul(activation, down_ref[...])
        grad_refs[2 * k][...] = grad[:tok].astype(grad_refs[2 * k].dtype)
        grad_refs[2 * k + 1][...] = to_low(grad[tok:])
        if k == 0:
            out_own_ref[...] = out[:tok]
        else:
            out_across_ref[...] = out[:tok]
        out_send_ref[k] = to_low(out[tok:])
    depth = down_ref.shape[0]
    held_ref[...] = left_product(act_all[...], cot_all[...])
    store_chunks(down_share_ref, 0, held_ref, 0, depth, index_ref[2], chunks[1])
    held_ref[...] = left_product(norm_all[...], inner_all[...])
    rows = depth // 4
    for out_ref, order in ((keep_ref, (0, 2)), (send_ref, (1, 3))):
        for k, j in enumerate(order):
            store_chunks(
                out_ref, k * rows, held_ref, (index_ref[0] ^ j) * rows, rows, index_ref[2], chunks[0]
            )


def mlp_share(index, norms, cot, block_own, exchanged, w_down):
    depth, width = w_down.shape
    tok = cot.shape[0]
    chunks = (chunk_count(width // len(WHOLE)), chunk_count(depth))
    inputs = [(value, whole(value)) for value in (*norms, cot, block_own, *exchanged, w_down)]
    token_f32 = ((tok, width), jnp.float32, const((tok, width)))
    token_low = ((tok, width), jnp.bfloat16, const((tok, width)))
    token_send = ((2, tok, width), jnp.bfloat16, const((2, tok, width)))
    rows = ((width // 2, depth), jnp.bfloat16, const((width // 2, depth)))
    outputs = [token_f32, token_low, token_low, token_low, token_f32, token_f32, token_send]
    outputs += [((depth, width), jnp.bfloat16, const((depth, width))), rows, rows]
    scratch = [pltpu.VMEM((width, depth), jnp.bfloat16), pltpu.VMEM((depth, depth), jnp.float32)]
    scratch += [pltpu.VMEM((4 * tok, depth), jnp.bfloat16)] * 4
    return chain_call(
        functools.partial(mlp_kernel, tok, chunks),
        "mlp_share",
        (1,),
        index,
        inputs,
        outputs,
        scratch,
        11.0,
    )


def inner_out_kernel(index_ref, own_ref, far_ref, weight_ref, gain_ref, out_ref, sum_ref):
    half = own_ref.shape[0]
    upper = index_ref[1] % 2
    own = own_ref[...].astype(jnp.float32)
    far = far_ref[...].astype(jnp.float32)
    out_ref[pl.ds(pl.multiple_of(upper * half, 8), half), :] = own
    out_ref[pl.ds(pl.multiple_of((1 - upper) * half, 8), half), :] = far
    part = jnp.sum(weight_ref[...].astype(jnp.float32) * out_ref[...], axis=1, keepdims=True)
    part = part / gain_ref[...]

    @pl.when(pl.program_id(0) == 0)
    def _():
        sum_ref[...] = part

    @pl.when(pl.program_id(0) > 0)
    def _():
        sum_ref[...] = sum_ref[...] + part


def inner_out(index, halves, weight, gain):
    own, far = halves
    rows, full = weight.shape
    depth = full // len(WHOLE)
    block = pl.BlockSpec((rows // 2, depth), lambda t, index_ref: (0, t ^ index_ref[0]))
    column = gain.astype(jnp.float32).reshape(rows, 1)
    inputs = [(own, block), (far, block)]
    inputs += [(weight, pl.BlockSpec((rows, depth), lambda t, _: (0, t))), (column, whole(column))]
    outputs = [
        ((rows, full), jnp.float32, pl.BlockSpec((rows, depth), lambda t, _: (0, t))),
        ((rows, 1), jnp.float32, const((rows, 1))),
    ]
    total, sums = chain_call(
        inner_out_kernel, "inner_out", (len(WHOLE),), index, inputs, outputs, [], 3.0
    )
    return total, sums.reshape(rows)


def cross_backward_kernel(head_size, stretches, index_ref, *refs):
    q_ref, kv_ref, cot_ref, cross_ref, wout_ref, keep_ref, w_ref, rows_ref, gain_ref = refs[:9]
    terms = refs[9:13]
    dq_ref, dkv_ref, out_ref, branch_ref, attended_ref, first_ref, grad_ref, do_ref = refs[13:]
    score_scale = head_size ** (-0.5)
    pair = pl.program_id(0)
    wide = q_ref.shape[1]
    keys = kv_ref.shape[1] // stretches
    columns = pl.ds(pl.multiple_of(pair * wide, wide), wide)

    @pl.when(pair == 0)
    def _():
        values = cross_ref[...]
        grad_norm = sum(term[...].astype(jnp.float32) for term in terms)
        grad = cot_ref[...].astype(jnp.float32) + rms_back(
            values, inverse_rms(values), gain_ref[2:3, :], grad_norm
        )
        grad_ref[...] = grad
        branch = to_low(keep_ref[...] * grad)
        first_ref[...] = branch
        do_ref[...] = to_low(right_product(branch, wout_ref[...]))

    parts = []
    for s in range(stretches):
        rows = pl.ds(s * STRETCH, STRETCH)
        span = pl.ds(s * keys, keys)
        query = head_rows(q_ref[rows, :], head_size)
        grad = head_rows(do_ref[rows, columns], head_size)
        scores = right_product(kv_ref[0, span, :], query) * score_scale
        weights = jnp.exp(scores - jnp.max(scores, axis=0, keepdims=True))
        probs = weights / jnp.sum(weights, axis=0, keepdims=True)
        dprobs = right_product(kv_ref[1, span, :], grad)
        delta = jnp.sum(probs * dprobs, axis=0, keepdims=True)
        dscores = to_low(probs * (dprobs - delta))
        dkv_ref[0, span, :] = to_low(score_scale * matmul(dscores, query))
        dkv_ref[1, span, :] = to_low(matmul(to_low(probs), grad))
        parts.append(join_heads(left_product(kv_ref[0, span, :], dscores), head_size))
    dq_ref[:, columns] = to_low(score_scale * jnp.concatenate(parts, axis=0))

    @pl.when(pair == pl.num_programs(0) - 1)
    def _():
        width = rows_ref.shape[1]
        values = rows_ref[...]
        grad_norm = right_product(dq_ref[...], w_ref[:, width:])
        total = grad_ref[...] + rms_back(
            values, inverse_rms(values), gain_ref[1:2, :], grad_norm
        )
        out_ref[...] = total
        branch = to_low(total)
        branch_ref[...] = branch
        attended_ref[...] = to_low(right_product(branch, w_ref[:, :width]))


def cross_backward(
    index, query, key_value, cotangent, terms, after_cross, w_cout, keep_rows, w_pair, after_attn,
    gain_rows, stretches,
):
    tok, width = query.shape
    keys = key_value.shape[1]
    block = pl.BlockSpec((tok, 128), lambda i, _: (0, i))
    planes = pl.BlockSpec((2, keys, 128), lambda i, _: (0, 0, i))
    inputs = [(query, block), (key_value, planes), (cotangent, whole(cotangent))]
    inputs += [
        (value, whole(value))
        for value in (after_cross, w_cout, keep_rows, w_pair, after_attn, gain_rows, *terms)
    ]
    low = ((tok, width), jnp.bfloat16, const((tok, width)))
    outputs = [
        low,
        ((2, keys, width), jnp.bfloat16, planes),
        ((tok, width), jnp.float32, const((tok, width))),
        low,
        low,
        low,
    ]
    return chain_call(
        functools.partial(cross_backward_kernel, width // H, stretches),
        "cross_backward",
        (H // 2,),
        index,
        inputs,
        outputs,
        [pltpu.VMEM((tok, width), jnp.float32), pltpu.VMEM((tok, width), jnp.bfloat16)],
        13.0,
    )


def swap(values, axis, bit):
    count = lax.axis_size(axis)
    return lax.ppermute(values, axis, [(i, i ^ bit) for i in range(count)])


def after(value, *earlier):
    return lax.optimization_barrier((value,) + earlier)[0]


def mirrored(position, count):
    out = 0
    for _ in range(count.bit_length() - 1):
        out, position = 2 * out + position % 2, position // 2
    return out


def positions_kernel(
    stretches, index_ref, deal_ref, lengths_ref, pos_ref, low_ref, high_ref, keep_ref
):
    ctx_index = index_ref[1]
    held = pos_ref.shape[0] // STRETCH
    offset = lax.broadcasted_iota(jnp.int32, (STRETCH, 1), 0)
    for s in range(held):
        device = ctx_index ^ mirrored(s // stretches, held // stretches)
        given = deal_ref[device * stretches + s % stretches]
        pos_ref[pl.ds(s * STRETCH, STRETCH), :] = given * STRETCH + offset
    lane = lax.broadcasted_iota(jnp.int32, low_ref.shape, 1) % (stretches * STRETCH)
    low_pos = jnp.zeros(low_ref.shape, jnp.int32)
    high_pos = jnp.zeros(low_ref.shape, jnp.int32)
    for s in range(stretches):
        given = deal_ref[ctx_index * stretches + s]
        start, end = 0, 0
        for q in range(lengths_ref.shape[0]):
            start = jnp.where(end <= given, end, start)
            end = end + lengths_ref[q]
        here = lane // STRETCH == s
        low_pos = jnp.where(here, start * STRETCH, low_pos)
        high_pos = jnp.where(here, given * STRETCH + lane % STRETCH, high_pos)
        kept = jnp.where(given != start, 1.0, 0.0).astype(jnp.float32)
        keep_ref[pl.ds(s * STRETCH, STRETCH), :] = jnp.full((STRETCH, 1), kept, jnp.float32)
    low_ref[...] = low_pos
    high_ref[...] = high_pos


def positions(index, deal_row, lengths_row, stretches):
    tok_count = stretches * STRETCH
    smem = pl.BlockSpec(memory_space=pltpu.SMEM)
    vmem = pl.BlockSpec(memory_space=pltpu.VMEM)
    return pl.pallas_call(
        functools.partial(positions_kernel, stretches),
        in_specs=[smem] * 3,
        out_specs=[vmem] * 4,
        out_shape=[
            jax.ShapeDtypeStruct((deal_row.shape[0] * STRETCH, 1), jnp.int32),
            jax.ShapeDtypeStruct((1, 2 * tok_count), jnp.int32),
            jax.ShapeDtypeStruct((1, 2 * tok_count), jnp.int32),
            jax.ShapeDtypeStruct((tok_count, 1), jnp.float32),
        ],
        cost_estimate=lasting(1.5),
        name="positions",
    )(index, deal_row, lengths_row)


def chunk_count(rows):
    count = lax.axis_size("ctx")
    return count if count & (count - 1) == 0 and rows % (8 * count) == 0 else 1


def store_chunks(out_ref, start, held_ref, base, rows, own_chunk, chunks):
    size = rows // chunks
    for p in range(chunks):
        place = base + (own_chunk ^ p) * size
        part = held_ref[pl.ds(pl.multiple_of(place, 8), size), :]
        out_ref[pl.ds(start + p * size, size), :] = part.astype(out_ref.dtype)


def products_kernel(tiles, rows, chunks, index_ref, *refs):
    count = len(tiles)
    inputs, (keep_ref, send_ref, held_ref) = refs[:-3], refs[-3:]
    fsdp_index, own_chunk = index_ref[0], index_ref[2]
    width = held_ref.shape[1]
    for t, (left, right, column) in enumerate(tiles):

        @pl.when(pl.program_id(0) == t)
        def _(left=left, right=right, column=column):
            grads = inputs[right][:, pl.ds(column * width, width)]
            held_ref[...] = left_product(inputs[left][...], grads)

    for out_ref, order in ((keep_ref, (0, 2)), (send_ref, (1, 3))):
        for k, j in enumerate(order):
            store_chunks(
                out_ref, k * rows, held_ref, (fsdp_index ^ j) * rows, rows, own_chunk, chunks
            )


def wide_products(index, terms, microseconds):
    shares = lax.axis_size("fsdp")
    inputs, tiles = [], []
    width = terms[0][0].shape[1]
    for left, right, plane in terms:
        count = right.shape[-2]
        if not any(left is value and count == held for value, held in inputs):
            inputs.append((left, count))
        first = next(i for i, (v, held) in enumerate(inputs) if v is left and held == count)
        inputs.append((right, plane))
        for column in range(right.shape[-1] // width):
            tiles.append((first, len(inputs) - 1, column))
    rows = width // shares
    chunks = chunk_count(rows)
    specs = []
    for value, plane in inputs:
        if value.ndim == 2:
            specs.append(pl.BlockSpec((plane or value.shape[0], value.shape[1]), lambda i, _: (0, 0)))
        else:
            specs.append(
                pl.BlockSpec((None,) + value.shape[1:], lambda i, _, plane=plane: (plane, 0, 0))
            )
    total = len(tiles) * width
    out = jax.ShapeDtypeStruct((2 * rows, total), jnp.bfloat16)
    out_spec = pl.BlockSpec((2 * rows, width), lambda i, _: (0, i))
    return pl.pallas_call(
        functools.partial(products_kernel, tiles, rows, chunks),
        grid_spec=pltpu.PrefetchScalarGridSpec(
            num_scalar_prefetch=1,
            grid=(len(tiles),),
            in_specs=specs,
            out_specs=[out_spec, out_spec],
            scratch_shapes=[pltpu.VMEM((width, width), jnp.float32)],
        ),
        out_shape=[out, out],
        cost_estimate=lasting(microseconds),
        name="wide_products",
    )(index, *[value for value, _ in inputs])


def add_low(*parts):
    return to_low(sum(part.astype(jnp.float32) for part in parts))


def reduction(keep, send):
    rows = keep.shape[0] // 2
    received = swap(send, "fsdp", 1)
    received = yield send, received
    sent = add_low(keep[rows:], received[rows:])
    across = swap(sent, "fsdp", 2)
    across = yield sent, across
    return (yield from ctx_reduction((keep[:rows], received[:rows], across)))


def in_order(index, bit, own, far):
    upper = (index & bit) != 0
    return jnp.concatenate([jnp.where(upper, far, own), jnp.where(upper, own, far)], axis=0)


def ctx_reduction(parts):
    index = lax.axis_index("ctx")
    half = parts[0].shape[0] // 2
    chunks = chunk_count(2 * half)
    if chunks == 1:
        share = lax.psum(add_low(*parts), "ctx")
        upper = (index & 1) != 0
        first, second = share[:half], share[half:]
        return jnp.where(upper, second, first), jnp.where(upper, first, second)
    bit = 1
    while bit < chunks:
        sent = add_low(*[part[half:] for part in parts])
        held = add_low(*[part[:half] for part in parts])
        far = swap(sent, "ctx", bit)
        parts = (held, (yield sent, far))
        half, bit = half // 2, 2 * bit
    gathered = add_low(*parts)
    while bit > 2:
        bit = bit // 2
        far = swap(gathered, "ctx", bit)
        far = yield gathered, far
        gathered = in_order(index, bit, gathered, far)
    far = swap(gathered, "ctx", 1)
    far = yield gathered, far
    return gathered, far


def finished(halves, offset, width):
    own, far = (half[:, offset : offset + width] for half in halves)
    return in_order(lax.axis_index("ctx"), 1, own, far).astype(jnp.float32)


def sum_to_owner(total):
    bit = 1
    while bit < lax.axis_size("ctx"):
        half = total.shape[0] // 2
        sent = total[half:]
        far = swap(sent, "ctx", bit)
        far = yield sent, far
        total = add_low(total[:half], far)
        bit = 2 * bit
    return total


class Steps:
    def __init__(self, steps):
        self.steps = steps
        self.result = None
        self.advance(None)

    def advance(self, arrived):
        try:
            sent, self.arriving = self.steps.send(arrived)
            return sent
        except StopIteration as stop:
            self.result = stop.value
            return stop.value[1] if isinstance(stop.value, tuple) else stop.value

    def hold(self, *token):
        if self.result is not None:
            return token[0]
        self.arriving = after(self.arriving, *token)
        return self.arriving

    def move(self, *token):
        return token[0] if self.result is not None else self.advance(self.hold(*token))

    def finish(self, *token):
        sent = token[0]
        while self.result is None:
            sent = self.move(sent)
        return sent


def gain_gradient(weight, grad, gain):
    return jnp.sum(weight.astype(jnp.float32) * grad, axis=1) / gain.astype(jnp.float32)


def local(
    hidden,
    neighbours,
    cotangent,
    stretch_deal,
    seq_lengths,
    norm_gains,
    attn_qkv,
    attn_out,
    cross_q,
    cross_kv,
    cross_out,
    mlp_in,
    mlp_out,
):
    shares = lax.axis_size("fsdp")
    fsdp_index = lax.axis_index("fsdp")
    ctx_index = lax.axis_index("ctx")
    ctx_count = lax.axis_size("ctx")
    own_chunk, bit = 0 * ctx_index, 1
    while bit < ctx_count:
        own_chunk = 2 * own_chunk + (ctx_index & bit) // bit
        bit = 2 * bit
    place = jnp.stack([fsdp_index, ctx_index, own_chunk]).astype(jnp.int32)
    feature_width = hidden.shape[2]
    own = hidden[0]
    tok = own.shape[0]
    stretch_count = tok // STRETCH
    enc_rows = neighbours[0].reshape(-1, feature_width)
    cot = cotangent[0]

    key_pos, low_pos, high_pos, keep_rows = positions(
        place, stretch_deal[0], seq_lengths[0], stretch_count
    )

    first_share = jnp.concatenate(
        [attn_qkv, jnp.pad(norm_gains.T, ((0, 0), (0, 128 - norm_gains.shape[0])))], axis=1
    )
    across_qkv = swap(first_share, "fsdp", 2)
    if ctx_count == 8:
        far, last, near = swap(own, "ctx", 4), swap(own, "ctx", 6), swap(own, "ctx", 2)
        beside = swap(own, "ctx", 1)
        beside_near = swap(near, "ctx", 1)
        second = after(jnp.concatenate([far, last], axis=0), near)
        row_pieces = [own, near, second, beside, beside_near, swap(second, "ctx", 1)]
        layout = [[k * tok for k in ks] for ks in ((0,), (2,), (1, 3), (4,), (6,), (5, 7))]
        second = after(second, beside)
    else:
        first = own
        bit = ctx_count
        while bit > 2:
            bit = bit // 2
            first = jnp.concatenate([first, swap(first, "ctx", bit)], axis=0)
        row_pieces = [first, swap(first, "ctx", 1)]
        layout = [[k * first.shape[0]] for k in range(2)]
        second = first
    sibling_qkv = swap(after(first_share, second), "fsdp", 1)
    across_qkv = after(across_qkv, second)
    diagonal_qkv = swap(across_qkv, "fsdp", 1)
    pair_share = jnp.concatenate([attn_out, cross_q], axis=1)
    across_pair = swap(after(pair_share, second), "fsdp", 2)
    cross_share = jnp.concatenate([cross_kv, cross_out], axis=1)
    across_cross = swap(after(cross_share, second), "fsdp", 2)
    depth = mlp_out.shape[0]
    rows_in = mlp_in.shape[0]

    def block_of(j):
        return lax.dynamic_slice_in_dim(mlp_in, (fsdp_index ^ j) * depth, depth, axis=1)

    block_own = block_of(0)
    exchange_sibling = jnp.concatenate([block_of(1), cot], axis=0)
    exchange_across = jnp.concatenate([block_of(2), block_of(3), cot], axis=0)

    rows_all, scale_all = held_rows(row_pieces, layout)
    query, key_value, norm_all, w_qkv, gain_rows = project(
        place,
        rows_all,
        scale_all,
        [first_share, sibling_qkv, across_qkv, after(diagonal_qkv, scale_all)],
        tok,
    )
    across_pair = after(across_pair, query)
    diagonal_pair = swap(across_pair, "fsdp", 1)
    sibling_pair = swap(after(pair_share, query), "fsdp", 1)
    from_across = swap(after(exchange_across, across_pair), "fsdp", 2)
    attended, log_total = self_forward(query, key_value, key_pos, low_pos, high_pos)
    sibling_cross = swap(after(cross_share, attended), "fsdp", 1)
    across_cross = after(across_cross, attended)
    after_attn, norm_two, cross_query, w_pair = attend_out(
        place, attended, own, gain_rows, [pair_share, sibling_pair, across_pair, diagonal_pair]
    )
    diagonal_cross = swap(across_cross, "fsdp", 1)
    cross_key_value, cross_rows, after_cross, norm_three, w_ckv, w_cout = cross_forward(
        place,
        cross_query,
        enc_rows,
        after_attn,
        keep_rows,
        gain_rows,
        [cross_share, sibling_cross, across_cross, diagonal_cross],
        stretch_count,
    )
    from_sibling = swap(after(exchange_sibling, cross_query), "fsdp", 1)
    norm_across, norm_sibling = swap(norm_three, "fsdp", 2), swap(norm_three, "fsdp", 1)
    from_across = after(from_across, norm_three)
    from_diagonal = swap(from_across, "fsdp", 1)
    norm_diagonal = swap(norm_across, "fsdp", 1)
    (
        grad_own, grad_sibling, grad_across, grad_diagonal, out_own, out_across, out_send, share_down,
        keep_in, send_in,
    ) = mlp_share(
        place,
        [norm_three, norm_sibling, norm_across, norm_diagonal],
        cot,
        block_own,
        [from_sibling, from_across, from_diagonal],
        mlp_out,
    )

    terms = (
        grad_own,
        swap(grad_sibling, "fsdp", 1),
        swap(grad_across, "fsdp", 2),
        swap(grad_diagonal, "fsdp", 3),
    )
    received_in = swap(send_in, "fsdp", 1)
    across_in = swap(
        jnp.concatenate([keep_in[rows_in:], received_in[rows_in:]], axis=1), "fsdp", 2
    )
    down = Steps(ctx_reduction((share_down,)))
    (
        grad_cross_query, grad_cross_pair, grad_after_attn, grad_attn_branch, grad_attended,
        grad_cross_branch,
    ) = cross_backward(
        place,
        cross_query,
        cross_key_value,
        cot,
        terms,
        after_cross,
        w_cout,
        keep_rows,
        w_pair,
        after_attn,
        gain_rows,
        stretch_count,
    )
    across_in = after(across_in, grad_attended)
    arrived = down.hold(grad_attended)
    keep_cross, send_cross = wide_products(
        place,
        [
            (cross_rows, grad_cross_branch, None),
            (norm_two, grad_cross_query, None),
            (enc_rows, after(grad_cross_pair, across_in, arrived), 0),
            (enc_rows, grad_cross_pair, 1),
            (attended, grad_attn_branch, None),
        ],
        8.2,
    )
    cross = Steps(reduction(keep_cross, send_cross))
    ready = down.move(keep_cross)
    share_in = jnp.concatenate(
        [keep_in[:rows_in], received_in[:rows_in], after(across_in, ready)], axis=1
    )
    inner = Steps(ctx_reduction((share_in,)))
    ready = cross.move(share_in)
    grad_query, grad_pair = self_backward(
        query,
        key_value,
        after(grad_attended, ready),
        key_pos,
        low_pos,
        high_pos,
        log_total,
    )
    ready = inner.move(down.move(grad_query))
    keep_attn, send_attn = wide_products(
        place,
        [
            (norm_all, after(grad_query, ready), None),
            (norm_all, grad_pair, 0),
            (norm_all, grad_pair, 1),
        ],
        0.01,
    )
    attn = Steps(reduction(keep_attn, send_attn))
    norm1_all, norm1_query = norm_terms(place, after(grad_pair, keep_attn), grad_query, w_qkv)
    ready = cross.move(norm1_all)
    norm1 = Steps(sum_to_owner(after(norm1_all, ready)))
    grad_enc = enc_terms(place, after(grad_cross_pair, ready), w_ckv)
    out_sibling = swap(after(out_send, grad_enc), "fsdp", 1)
    ready = grad_enc
    for step in (attn, down, inner, cross, down, inner, attn, norm1):
        ready = step.move(ready)
    out_sibling = after(out_sibling, ready)
    out_far = swap(add_low(out_across, out_sibling[1]), "fsdp", 2)
    for step in (cross, attn, norm1, inner, down):
        ready = step.move(ready)
    layer_out = after_cross + (
        out_own + out_sibling[0].astype(jnp.float32) + after(out_far, ready).astype(jnp.float32)
    )
    for step in (cross, attn, inner):
        ready = step.move(ready)
    ready = down.finish(norm1.finish(ready))
    input_rows = own.astype(jnp.float32)
    grad_norm1 = norm1.result.astype(jnp.float32) + norm1_query
    grad_input = grad_after_attn + rms_back(
        input_rows, inverse_rms(input_rows), after(gain_rows, ready)[0:1], grad_norm1
    )
    total_down = finished(down.result, 0, feature_width)
    ready = after(ready, total_down, grad_input, layer_out)
    for step in (cross, attn):
        ready = step.move(ready)
    ready = inner.finish(ready)
    total_in, gain_three = inner_out(place, inner.result, mlp_in, norm_gains[2])
    ready = after(ready, total_in)
    while attn.result is None or cross.result is None:
        for step in (cross, attn):
            ready = step.move(ready)
    halves_cross, halves_attn = cross.result, attn.result
    d = feature_width
    total_cout = finished(halves_cross, 0, d)
    total_cq = finished(halves_cross, d, d)
    total_ckv = finished(halves_cross, 2 * d, 2 * d)
    total_out = finished(halves_cross, 4 * d, d)
    total_qkv = finished(halves_attn, 0, 3 * d)
    grad_gains = jnp.stack(
        [
            gain_gradient(attn_qkv, total_qkv, norm_gains[0]),
            gain_gradient(cross_q, total_cq, norm_gains[1]),
            gain_three,
        ]
    )
    return (
        layer_out[None],
        grad_input[None],
        grad_enc.reshape(neighbours.shape),
        grad_gains,
        total_qkv,
        total_out,
        total_cq,
        total_ckv,
        total_cout,
        total_in,
        total_down,
    )


def solution(mesh):
    return jax.shard_map(
        local,
        mesh=mesh,
        in_specs=(
            P("fsdp", "ctx", None),
            P("fsdp", "ctx", None, None),
            P("fsdp", "ctx", None),
            P("fsdp", None),
            P("fsdp", None),
            P(None, "fsdp"),
            P("fsdp", None),
            P("fsdp", None),
            P("fsdp", None),
            P("fsdp", None),
            P("fsdp", None),
            P("fsdp", None),
            P("fsdp", None),
        ),
        out_specs=(
            P("fsdp", "ctx", None),
            P("fsdp", "ctx", None),
            P("fsdp", "ctx", None, None),
            P(None, "fsdp"),
            P("fsdp", None),
            P("fsdp", None),
            P("fsdp", None),
            P("fsdp", None),
            P("fsdp", None),
            P("fsdp", None),
            P("fsdp", None),
        ),
        check_vma=False,
    )
```

```python
import functools

import jax
import jax.numpy as jnp
from jax import lax
from jax.experimental import pallas as pl
from jax.experimental.pallas import tpu as pltpu
from jax.sharding import PartitionSpec as P

H = 12
STRETCH = 64


NORM_EPS = 1e-06
MASKED_SCORE = -1e30
KEY_BLOCK = 1024


def lasting(microseconds):
    return pl.CostEstimate(
        flops=int(microseconds * 1.15e10), bytes_accessed=int(microseconds * 1e6), transcendentals=0
    )


def to_low(values):
    return values.astype(jnp.bfloat16)


def matmul(left, right):
    return jnp.dot(left, right, preferred_element_type=jnp.float32)


def left_product(left, right):
    return lax.dot_general(left, right, (((0,), (0,)), ((), ())), preferred_element_type=jnp.float32)


def right_product(left, right):
    return lax.dot_general(left, right, (((1,), (1,)), ((), ())), preferred_element_type=jnp.float32)


def inverse_rms(values):
    return lax.rsqrt(jnp.mean(values * values, axis=-1, keepdims=True) + NORM_EPS)


def rms_back(values, scale, gain, grad):
    gained = gain * grad
    along = jnp.mean(gained * values, axis=-1, keepdims=True)
    return scale * gained - values * (scale * scale * scale) * along


PAIR = 128
STEP = 256


def head_rows(rows, head_size, scale=1.0):
    wide = rows.astype(jnp.float32) * scale
    lane = lax.broadcasted_iota(jnp.int32, wide.shape, 1)
    first = jnp.where(lane < head_size, wide, 0.0)
    second = jnp.where(lane >= head_size, wide, 0.0)
    return to_low(jnp.concatenate([first, second], axis=0))


def join_heads(columns, head_size):
    tok_count = columns.shape[1] // 2
    return jnp.concatenate(
        [columns[:head_size, :tok_count], columns[head_size:, tok_count:]], axis=0
    ).T


def self_forward_kernel(
    head_size, blocks, q_ref, k_ref, v_ref, pos_ref, low_ref, high_ref, o_ref, lse_ref
):
    score_scale = head_size ** (-0.5)
    low_pos, high_pos = low_ref[...], high_ref[...]
    rows = k_ref.shape[0] // blocks

    def span_of(index):
        return pl.ds(pl.multiple_of(index * rows, rows), rows)

    def visible(index):
        key_pos = pos_ref[span_of(index), :]
        return (key_pos >= low_pos) & (key_pos <= high_pos)

    once = visible(0) if blocks == 1 else None
    for p in range(q_ref.shape[1] // PAIR):
        columns = pl.ds(p * PAIR, PAIR)
        query = head_rows(q_ref[:, columns], head_size, score_scale)

        def scores_of(index, query=query, columns=columns):
            seen = visible(index) if once is None else once
            scores = right_product(k_ref[span_of(index), columns], query)
            return jnp.where(seen, scores, MASKED_SCORE)

        if blocks == 1:
            scores = scores_of(0)
            peak = jnp.max(scores, axis=0, keepdims=True)
            weights = jnp.exp(scores - peak)
            total = jnp.sum(weights, axis=0, keepdims=True)
            running = left_product(v_ref[:, columns], to_low(weights))
        else:
            peak = lax.fori_loop(
                0,
                blocks,
                lambda i, top: jnp.maximum(top, jnp.max(scores_of(i), axis=0, keepdims=True)),
                jnp.full((1, query.shape[0]), MASKED_SCORE, jnp.float32),
            )

            def add(index, state, peak=peak, columns=columns, scores_of=scores_of):
                total, running = state
                weights = jnp.exp(scores_of(index) - peak)
                return (
                    total + jnp.sum(weights, axis=0, keepdims=True),
                    running + left_product(v_ref[span_of(index), columns], to_low(weights)),
                )

            total, running = lax.fori_loop(
                0,
                blocks,
                add,
                (
                    jnp.zeros((1, query.shape[0]), jnp.float32),
                    jnp.zeros((2 * head_size, query.shape[0]), jnp.float32),
                ),
            )
        o_ref[:, columns] = to_low(join_heads(running / total, head_size))
        lse_ref[p] = peak + jnp.log(total)


def self_backward_kernel(
    head_size,
    blocks,
    q_ref,
    k_ref,
    v_ref,
    do_ref,
    pos_ref,
    low_ref,
    high_ref,
    lse_ref,
    dq_ref,
    dkv_ref,
):
    score_scale = head_size ** (-0.5)
    low_pos, high_pos = low_ref[...], high_ref[...]
    rows = k_ref.shape[0] // blocks

    def span_of(index):
        return pl.ds(pl.multiple_of(index * rows, rows), rows)

    def visible(index):
        key_pos = pos_ref[span_of(index), :]
        return (key_pos >= low_pos) & (key_pos <= high_pos)

    once = visible(0) if blocks == 1 else None
    for p in range(q_ref.shape[1] // PAIR):
        columns = pl.ds(p * PAIR, PAIR)
        query = head_rows(q_ref[:, columns], head_size, score_scale)
        grad = head_rows(do_ref[:, columns], head_size)
        log_total = lse_ref[p]

        def pair_of(index, query=query, grad=grad, log_total=log_total, columns=columns):
            span = span_of(index)
            seen = visible(index) if once is None else once
            scores = jnp.where(seen, right_product(k_ref[span, columns], query), MASKED_SCORE)
            return jnp.exp(scores - log_total), right_product(v_ref[span, columns], grad)

        def finish(index, probs, dprobs, delta, query=query, grad=grad, columns=columns):
            span = span_of(index)
            dscores = to_low(probs * (dprobs - delta))
            dkv_ref[0, span, columns] = to_low(matmul(dscores, query))
            dkv_ref[1, span, columns] = to_low(matmul(to_low(probs), grad))
            return left_product(k_ref[span, columns], dscores)

        if blocks == 1:
            probs, dprobs = pair_of(0)
            delta = jnp.sum(probs * dprobs, axis=0, keepdims=True)
            turned = finish(0, probs, dprobs, delta)
        else:

            def add_delta(index, delta, pair_of=pair_of):
                probs, dprobs = pair_of(index)
                return delta + jnp.sum(probs * dprobs, axis=0, keepdims=True)

            delta = lax.fori_loop(
                0, blocks, add_delta, jnp.zeros((1, query.shape[0]), jnp.float32)
            )

            def add_query(index, turned, delta=delta, pair_of=pair_of, finish=finish):
                probs, dprobs = pair_of(index)
                return turned + finish(index, probs, dprobs, delta)

            turned = lax.fori_loop(
                0, blocks, add_query, jnp.zeros((2 * head_size, query.shape[0]), jnp.float32)
            )
        dq_ref[:, columns] = to_low(score_scale * join_heads(turned, head_size))


def self_specs(tok_count, key_count, steps):
    return (
        pl.BlockSpec((tok_count, STEP), lambda i: (0, i)),
        pl.BlockSpec((key_count, STEP), lambda i: (0, i)),
        pl.BlockSpec((key_count, STEP), lambda i: (0, steps + i)),
        pl.BlockSpec((key_count, 1), lambda i: (0, 0)),
        pl.BlockSpec((1, 2 * tok_count), lambda i: (0, 0)),
        pl.BlockSpec((STEP // PAIR, 1, 2 * tok_count), lambda i: (i, 0, 0)),
    )


def self_forward(query, key_value, key_pos, low_pos, high_pos):
    tok_count, feature_width = query.shape
    key_count = key_value.shape[0]
    head_size = feature_width // H
    steps = feature_width // STEP
    blocks = max(1, key_count // KEY_BLOCK)
    rows, keys, values, pos, edge, lse = self_specs(tok_count, key_count, steps)
    return pl.pallas_call(
        functools.partial(self_forward_kernel, head_size, blocks),
        grid=(steps,),
        in_specs=[rows, keys, values, pos, edge, edge],
        out_specs=[rows, lse],
        out_shape=[
            jax.ShapeDtypeStruct((tok_count, feature_width), jnp.bfloat16),
            jax.ShapeDtypeStruct((H // 2, 1, 2 * tok_count), jnp.float32),
        ],
        cost_estimate=lasting(7.6),
        name="self_forward",
    )(query, key_value, key_value, key_pos, low_pos, high_pos)


def self_backward(query, key_value, grad, key_pos, low_pos, high_pos, log_total):
    tok_count, feature_width = query.shape
    key_count = key_value.shape[0]
    head_size = feature_width // H
    steps = feature_width // STEP
    blocks = max(1, key_count // KEY_BLOCK)
    rows, keys, values, pos, edge, lse = self_specs(tok_count, key_count, steps)
    return pl.pallas_call(
        functools.partial(self_backward_kernel, head_size, blocks),
        grid=(steps,),
        in_specs=[rows, keys, values, rows, pos, edge, edge, lse],
        out_specs=[rows, pl.BlockSpec((2, key_count, STEP), lambda i: (0, 0, i))],
        out_shape=[
            jax.ShapeDtypeStruct((tok_count, feature_width), jnp.bfloat16),
            jax.ShapeDtypeStruct((2, key_count, feature_width), jnp.bfloat16),
        ],
        cost_estimate=lasting(10.2),
        name="self_backward",
    )(query, key_value, key_value, grad, key_pos, low_pos, high_pos, log_total)


WHOLE = ((0, None), (1, None), (2, None), (3, None))
HALVES = ((0, None), (1, None), (2, 0), (2, 1), (3, 0), (3, 1))


def bases_of(pieces):
    return WHOLE if len(pieces) == len(WHOLE) else HALVES


def fill(out_ref, pieces, index_ref, columns=slice(None)):
    rows = pieces[0].shape[0]
    for piece, (j, half) in zip(pieces, bases_of(pieces)):
        place = (index_ref[0] ^ j) * rows
        if half is not None:
            place = place + ((index_ref[1] % 2) ^ half) * (rows // 2)
        part = piece[:, columns].astype(out_ref.dtype)
        out_ref[pl.ds(pl.multiple_of(place, 16), piece.shape[0]), :] = part


def whole(value):
    zeros = (0,) * value.ndim
    return pl.BlockSpec(value.shape, lambda *_: zeros)


def chain_call(kernel, name, grid, index, inputs, outputs, scratch, microseconds):
    return pl.pallas_call(
        kernel,
        grid_spec=pltpu.PrefetchScalarGridSpec(
            num_scalar_prefetch=1,
            grid=grid,
            in_specs=[spec for _, spec in inputs],
            out_specs=[spec for _, _, spec in outputs],
            scratch_shapes=scratch,
        ),
        out_shape=[jax.ShapeDtypeStruct(shape, dtype) for shape, dtype, _ in outputs],
        cost_estimate=lasting(microseconds),
        name=name,
    )(index, *[value for value, _ in inputs])


def const(shape):
    zeros = (0,) * len(shape)
    return pl.BlockSpec(shape, lambda *_: zeros)


def rows_kernel(layout, *refs):
    row_refs, (rows_ref, scale_ref) = refs[: len(layout)], refs[len(layout) :]
    for row_ref, places in zip(row_refs, layout):
        count = row_ref.shape[0] // len(places)
        for k, place in enumerate(places):
            rows = row_ref[pl.ds(k * count, count), :]
            rows_ref[pl.ds(place, count), :] = rows
            scale_ref[pl.ds(place, count), :] = inverse_rms(rows.astype(jnp.float32))


def held_rows(row_pieces, layout):
    total = sum(piece.shape[0] for piece in row_pieces)
    width = row_pieces[0].shape[1]
    return pl.pallas_call(
        functools.partial(rows_kernel, layout),
        out_shape=[
            jax.ShapeDtypeStruct((total, width), jnp.bfloat16),
            jax.ShapeDtypeStruct((total, 1), jnp.float32),
        ],
        cost_estimate=lasting(2.0),
        name="held_rows",
    )(*row_pieces)


def project_kernel(tok, pieces, index_ref, rows_ref, scale_ref, *refs):
    piece_refs, (q_ref, kv_ref, norm_ref, w_ref, gain_ref, column_ref) = (
        refs[:pieces],
        refs[pieces:],
    )
    width = q_ref.shape[1]
    step = pl.program_id(0)

    @pl.when(step == 0)
    def _():
        fill(w_ref, piece_refs, index_ref, slice(0, 3 * width))
        fill(column_ref, piece_refs, index_ref, slice(3 * width, 3 * width + 128))
        gain_ref[...] = column_ref[...].T[: gain_ref.shape[0], :]

    norm = to_low(rows_ref[...].astype(jnp.float32) * scale_ref[...] * gain_ref[0:1, :])
    norm_ref[...] = norm
    kv_ref[...] = to_low(matmul(norm, w_ref[:, width:]))

    @pl.when(step == 0)
    def _():
        q_ref[...] = to_low(matmul(norm_ref[pl.ds(0, tok), :], w_ref[:, :width]))


def project(index, rows, scale, pieces, tok):
    total, width = rows.shape
    block = min(512, total)

    def rows_of(columns):
        return pl.BlockSpec((block, columns), lambda i, _: (i, 0))

    inputs = [(rows, rows_of(width)), (scale, rows_of(1))]
    inputs += [(value, whole(value)) for value in pieces]
    outputs = [
        ((tok, width), jnp.bfloat16, const((tok, width))),
        ((total, 2 * width), jnp.bfloat16, rows_of(2 * width)),
        ((total, width), jnp.bfloat16, rows_of(width)),
        ((width, 3 * width), jnp.bfloat16, const((width, 3 * width))),
        ((8, width), jnp.float32, const((8, width))),
    ]
    return chain_call(
        functools.partial(project_kernel, tok, len(pieces)),
        "project",
        (total // block,),
        index,
        inputs,
        outputs,
        [pltpu.VMEM((width, 128), jnp.float32)],
        9.0,
    )


def enc_terms_kernel(index_ref, pair_ref, w_ref, out_ref):
    out_ref[...] = right_product(pair_ref[0], w_ref[0]) + right_product(pair_ref[1], w_ref[1])


def enc_terms(index, grad_pair, w_pair):
    _, total, width = grad_pair.shape
    block = min(256, total)
    inputs = [
        (grad_pair, pl.BlockSpec((2, block, width), lambda i, _: (0, i, 0))),
        (w_pair, whole(w_pair)),
    ]
    outputs = [((total, width), jnp.float32, pl.BlockSpec((block, width), lambda i, _: (i, 0)))]
    return chain_call(
        enc_terms_kernel, "enc_terms", (total // block,), index, inputs, outputs, [], 4.0
    )[0]


def norm_terms_kernel(index_ref, pair_ref, query_ref, w_ref, out_ref, own_ref):
    width = out_ref.shape[1]
    out_ref[...] = to_low(
        right_product(pair_ref[0], w_ref[:, width : 2 * width])
        + right_product(pair_ref[1], w_ref[:, 2 * width :])
    )

    @pl.when(pl.program_id(0) == 0)
    def _():
        own_ref[...] = right_product(query_ref[...], w_ref[:, :width])


def norm_terms(index, grad_pair, grad_query, w_qkv):
    _, total, width = grad_pair.shape
    tok = grad_query.shape[0]
    block = min(512, total)
    inputs = [
        (grad_pair, pl.BlockSpec((2, block, width), lambda i, _: (0, i, 0))),
        (grad_query, whole(grad_query)),
        (w_qkv, whole(w_qkv)),
    ]
    outputs = [
        ((total, width), jnp.bfloat16, pl.BlockSpec((block, width), lambda i, _: (i, 0))),
        ((tok, width), jnp.float32, const((tok, width))),
    ]
    return chain_call(
        norm_terms_kernel, "norm_terms", (total // block,), index, inputs, outputs, [], 0.01
    )


def attend_out_kernel(pieces, index_ref, att_ref, own_ref, gain_ref, *refs):
    piece_refs, (after_ref, norm_ref, query_ref, w_ref) = refs[:pieces], refs[pieces:]
    width = att_ref.shape[1]
    fill(w_ref, piece_refs, index_ref)
    rows = own_ref[...].astype(jnp.float32) + matmul(att_ref[...], w_ref[:, :width])
    after_ref[...] = rows
    norm = to_low(rows * inverse_rms(rows) * gain_ref[1:2, :])
    norm_ref[...] = norm
    query_ref[...] = to_low(matmul(norm, w_ref[:, width:]))


def attend_out(index, attended, own, gain_rows, pieces):
    tok, width = attended.shape
    inputs = [(value, whole(value)) for value in (attended, own, gain_rows)]
    inputs += [
        (piece, pl.BlockSpec((piece.shape[0], 2 * width), lambda *_: (0, 0))) for piece in pieces
    ]
    outputs = [
        ((tok, width), jnp.float32, const((tok, width))),
        ((tok, width), jnp.bfloat16, const((tok, width))),
        ((tok, width), jnp.bfloat16, const((tok, width))),
        ((width, 2 * width), jnp.bfloat16, const((width, 2 * width))),
    ]
    return chain_call(
        functools.partial(attend_out_kernel, len(pieces)),
        "attend_out",
        (1,),
        index,
        inputs,
        outputs,
        [],
        4.4,
    )


def cross_forward_kernel(head_size, stretches, pieces, index_ref, *refs):
    q_ref, enc_ref, rows_ref, keep_ref, gain_ref = refs[:5]
    refs = refs[5:]
    key_refs, value_refs = refs[:pieces], refs[pieces : 2 * pieces]
    out_refs, refs = refs[2 * pieces : 3 * pieces], refs[3 * pieces :]
    kv_ref, cross_ref, after_ref, norm_ref, wkv_ref, wout_ref = refs
    score_scale = head_size ** (-0.5)
    pair = pl.program_id(0)
    wide = q_ref.shape[1]
    fill(wkv_ref.at[0], key_refs, index_ref)
    fill(wkv_ref.at[1], value_refs, index_ref)
    kv_ref[0] = to_low(matmul(enc_ref[...], wkv_ref[0]))
    kv_ref[1] = to_low(matmul(enc_ref[...], wkv_ref[1]))

    @pl.when(pair == 0)
    def _():
        fill(wout_ref, out_refs, index_ref)

    keys = enc_ref.shape[0] // stretches
    sides = []
    for p in range(wide // PAIR):
        part = pl.ds(p * PAIR, PAIR)
        parts = []
        for s in range(stretches):
            span = pl.ds(s * keys, keys)
            query = head_rows(q_ref[pl.ds(s * STRETCH, STRETCH), part], head_size, score_scale)
            scores = right_product(kv_ref[0, span, part], query)
            weights = jnp.exp(scores - jnp.max(scores, axis=0, keepdims=True))
            probs = to_low(weights / jnp.sum(weights, axis=0, keepdims=True))
            parts.append(join_heads(left_product(kv_ref[1, span, part], probs), head_size))
        sides.append(jnp.concatenate(parts, axis=0))
    columns = pl.ds(pl.multiple_of(pair * wide, wide), wide)
    cross_ref[:, columns] = to_low(jnp.concatenate(sides, axis=1))

    @pl.when(pair == pl.num_programs(0) - 1)
    def _():
        rows = rows_ref[...] + keep_ref[...] * matmul(cross_ref[...], wout_ref[...])
        after_ref[...] = rows
        norm_ref[...] = to_low(rows * inverse_rms(rows) * gain_ref[2:3, :])


def cross_forward(index, query, enc_rows, after_attn, keep_rows, gain_rows, pieces, stretches):
    tok, width = query.shape
    pairs = width // STEP
    keys = enc_rows.shape[0]
    inputs = [(query, pl.BlockSpec((tok, STEP), lambda i, _: (0, i)))]
    inputs += [(value, whole(value)) for value in (enc_rows, after_attn, keep_rows, gain_rows)]
    for first in (0, pairs):
        inputs += [
            (piece, pl.BlockSpec((piece.shape[0], STEP), lambda i, _, f=first: (0, f + i)))
            for piece in pieces
        ]
    inputs += [(piece, pl.BlockSpec((piece.shape[0], width), lambda i, _: (0, 2))) for piece in pieces]
    outputs = [
        ((2, keys, width), jnp.bfloat16, pl.BlockSpec((2, keys, STEP), lambda i, _: (0, 0, i))),
        ((tok, width), jnp.bfloat16, const((tok, width))),
        ((tok, width), jnp.float32, const((tok, width))),
        ((tok, width), jnp.bfloat16, const((tok, width))),
        ((2, width, width), jnp.bfloat16, pl.BlockSpec((2, width, STEP), lambda i, _: (0, 0, i))),
        ((width, width), jnp.bfloat16, const((width, width))),
    ]
    return chain_call(
        functools.partial(cross_forward_kernel, width // H, stretches, len(pieces)),
        "cross_forward",
        (pairs,),
        index,
        inputs,
        outputs,
        [],
        12.3,
    )


ERF_ABOVE = (
    -2.72614225801306e-10, 2.77068142495902e-08, -2.10102402082508e-06, -5.69250639462346e-05,
    -7.34990630326855e-04, -2.95459980854025e-03, -1.60960333262415e-02,
)
ERF_BELOW = (
    -1.45660718464996e-05, -2.13374055278905e-04, -1.68282697438203e-03, -7.37332916720468e-03,
    -1.42647390514189e-02,
)


def erf(values):
    values = jnp.clip(values, -4.0, 4.0)
    square = values * values
    above, below = ERF_ABOVE[0], ERF_BELOW[0]
    for factor in ERF_ABOVE[1:]:
        above = above * square + factor
    for factor in ERF_BELOW[1:]:
        below = below * square + factor
    return values * above / below


def mlp_kernel(tok, chunks, index_ref, *refs):
    norms, cot_ref, block_ref, exchanged, down_ref = refs[:4], refs[4], refs[5], refs[6:9], refs[9]
    grad_refs, out_own_ref, out_across_ref, out_send_ref = refs[10:14], refs[14], refs[15], refs[16]
    down_share_ref, keep_ref, send_ref, w_ref, held_ref, norm_all, cot_all, act_all, inner_all = refs[
        17:
    ]
    rows_in = block_ref.shape[0]
    starts = (0, 0, rows_in)
    blocks = [ref.at[pl.ds(start, rows_in), :] for ref, start in zip(exchanged, starts)]
    fill(w_ref, [block_ref, *blocks], index_ref)
    cot_all[pl.ds(0, tok), :] = cot_ref[...]
    for k, ref in enumerate(exchanged):
        start = ref.shape[0] - tok
        cot_all[pl.ds((k + 1) * tok, tok), :] = ref[pl.ds(start, tok), :]
    for k in range(4):
        norm_all[pl.ds(k * tok, tok), :] = norms[k][...]
    for k in range(2):
        rows = pl.ds(2 * k * tok, 2 * tok)
        inner = matmul(norm_all[rows, :], w_ref[...])
        share_below = 0.5 * (1.0 + erf(inner * (2.0**-0.5)))
        activation = to_low(inner * share_below)
        act_all[rows, :] = activation
        slope = share_below + inner * jnp.exp(-0.5 * inner * inner) * ((2.0 * jnp.pi) ** -0.5)
        grad_inner = to_low(right_product(cot_all[rows, :], down_ref[...]) * slope)
        inner_all[rows, :] = grad_inner
        grad = right_product(grad_inner, w_ref[...])
        out = matmul(activation, down_ref[...])
        grad_refs[2 * k][...] = grad[:tok].astype(grad_refs[2 * k].dtype)
        grad_refs[2 * k + 1][...] = to_low(grad[tok:])
        if k == 0:
            out_own_ref[...] = out[:tok]
        else:
            out_across_ref[...] = out[:tok]
        out_send_ref[k] = to_low(out[tok:])
    depth = down_ref.shape[0]
    held_ref[...] = left_product(act_all[...], cot_all[...])
    store_chunks(down_share_ref, 0, held_ref, 0, depth, index_ref[2], chunks[1])
    held_ref[...] = left_product(norm_all[...], inner_all[...])
    rows = depth // 4
    for out_ref, order in ((keep_ref, (0, 2)), (send_ref, (1, 3))):
        for k, j in enumerate(order):
            store_chunks(
                out_ref, k * rows, held_ref, (index_ref[0] ^ j) * rows, rows, index_ref[2], chunks[0]
            )


def mlp_share(index, norms, cot, block_own, exchanged, w_down):
    depth, width = w_down.shape
    tok = cot.shape[0]
    chunks = (chunk_count(width // len(WHOLE)), chunk_count(depth))
    inputs = [(value, whole(value)) for value in (*norms, cot, block_own, *exchanged, w_down)]
    token_f32 = ((tok, width), jnp.float32, const((tok, width)))
    token_low = ((tok, width), jnp.bfloat16, const((tok, width)))
    token_send = ((2, tok, width), jnp.bfloat16, const((2, tok, width)))
    rows = ((width // 2, depth), jnp.bfloat16, const((width // 2, depth)))
    outputs = [token_f32, token_low, token_low, token_low, token_f32, token_f32, token_send]
    outputs += [((depth, width), jnp.bfloat16, const((depth, width))), rows, rows]
    scratch = [pltpu.VMEM((width, depth), jnp.bfloat16), pltpu.VMEM((depth, depth), jnp.float32)]
    scratch += [pltpu.VMEM((4 * tok, depth), jnp.bfloat16)] * 4
    return chain_call(
        functools.partial(mlp_kernel, tok, chunks),
        "mlp_share",
        (1,),
        index,
        inputs,
        outputs,
        scratch,
        11.0,
    )


def inner_out_kernel(index_ref, own_ref, far_ref, weight_ref, gain_ref, out_ref, sum_ref):
    half = own_ref.shape[0]
    upper = index_ref[1] % 2
    own = own_ref[...].astype(jnp.float32)
    far = far_ref[...].astype(jnp.float32)
    out_ref[pl.ds(pl.multiple_of(upper * half, 8), half), :] = own
    out_ref[pl.ds(pl.multiple_of((1 - upper) * half, 8), half), :] = far
    part = jnp.sum(weight_ref[...].astype(jnp.float32) * out_ref[...], axis=1, keepdims=True)
    part = part / gain_ref[...]

    @pl.when(pl.program_id(0) == 0)
    def _():
        sum_ref[...] = part

    @pl.when(pl.program_id(0) > 0)
    def _():
        sum_ref[...] = sum_ref[...] + part


def inner_out(index, halves, weight, gain):
    own, far = halves
    rows, full = weight.shape
    depth = full // len(WHOLE)
    block = pl.BlockSpec((rows // 2, depth), lambda t, index_ref: (0, t ^ index_ref[0]))
    column = gain.astype(jnp.float32).reshape(rows, 1)
    inputs = [(own, block), (far, block)]
    inputs += [(weight, pl.BlockSpec((rows, depth), lambda t, _: (0, t))), (column, whole(column))]
    outputs = [
        ((rows, full), jnp.float32, pl.BlockSpec((rows, depth), lambda t, _: (0, t))),
        ((rows, 1), jnp.float32, const((rows, 1))),
    ]
    total, sums = chain_call(
        inner_out_kernel, "inner_out", (len(WHOLE),), index, inputs, outputs, [], 3.0
    )
    return total, sums.reshape(rows)


def cross_backward_kernel(head_size, stretches, index_ref, *refs):
    q_ref, kv_ref, cot_ref, cross_ref, wout_ref, keep_ref, w_ref, rows_ref, gain_ref = refs[:9]
    terms = refs[9:13]
    dq_ref, dkv_ref, out_ref, branch_ref, attended_ref, first_ref, grad_ref, do_ref = refs[13:]
    score_scale = head_size ** (-0.5)
    pair = pl.program_id(0)
    wide = q_ref.shape[1]
    keys = kv_ref.shape[1] // stretches

    @pl.when(pair == 0)
    def _():
        values = cross_ref[...]
        grad_norm = sum(term[...].astype(jnp.float32) for term in terms)
        grad = cot_ref[...].astype(jnp.float32) + rms_back(
            values, inverse_rms(values), gain_ref[2:3, :], grad_norm
        )
        grad_ref[...] = grad
        branch = to_low(keep_ref[...] * grad)
        first_ref[...] = branch
        do_ref[...] = to_low(right_product(branch, wout_ref[...]))

    sides = []
    for p in range(wide // PAIR):
        part = pl.ds(p * PAIR, PAIR)
        place = pl.ds(pl.multiple_of(pair * wide + p * PAIR, PAIR), PAIR)
        parts = []
        for s in range(stretches):
            rows = pl.ds(s * STRETCH, STRETCH)
            span = pl.ds(s * keys, keys)
            query = head_rows(q_ref[rows, part], head_size, score_scale)
            grad = head_rows(do_ref[rows, place], head_size)
            scores = right_product(kv_ref[0, span, part], query)
            weights = jnp.exp(scores - jnp.max(scores, axis=0, keepdims=True))
            probs = weights / jnp.sum(weights, axis=0, keepdims=True)
            dprobs = right_product(kv_ref[1, span, part], grad)
            delta = jnp.sum(probs * dprobs, axis=0, keepdims=True)
            dscores = to_low(probs * (dprobs - delta))
            dkv_ref[0, span, part] = to_low(matmul(dscores, query))
            dkv_ref[1, span, part] = to_low(matmul(to_low(probs), grad))
            parts.append(join_heads(left_product(kv_ref[0, span, part], dscores), head_size))
        sides.append(jnp.concatenate(parts, axis=0))
    columns = pl.ds(pl.multiple_of(pair * wide, wide), wide)
    dq_ref[:, columns] = to_low(score_scale * jnp.concatenate(sides, axis=1))

    @pl.when(pair == pl.num_programs(0) - 1)
    def _():
        width = rows_ref.shape[1]
        values = rows_ref[...]
        grad_norm = right_product(dq_ref[...], w_ref[:, width:])
        total = grad_ref[...] + rms_back(
            values, inverse_rms(values), gain_ref[1:2, :], grad_norm
        )
        out_ref[...] = total
        branch = to_low(total)
        branch_ref[...] = branch
        attended_ref[...] = to_low(right_product(branch, w_ref[:, :width]))


def cross_backward(
    index, query, key_value, cotangent, terms, after_cross, w_cout, keep_rows, w_pair, after_attn,
    gain_rows, stretches,
):
    tok, width = query.shape
    keys = key_value.shape[1]
    block = pl.BlockSpec((tok, STEP), lambda i, _: (0, i))
    planes = pl.BlockSpec((2, keys, STEP), lambda i, _: (0, 0, i))
    inputs = [(query, block), (key_value, planes), (cotangent, whole(cotangent))]
    inputs += [
        (value, whole(value))
        for value in (after_cross, w_cout, keep_rows, w_pair, after_attn, gain_rows, *terms)
    ]
    low = ((tok, width), jnp.bfloat16, const((tok, width)))
    outputs = [
        low,
        ((2, keys, width), jnp.bfloat16, planes),
        ((tok, width), jnp.float32, const((tok, width))),
        low,
        low,
        low,
    ]
    return chain_call(
        functools.partial(cross_backward_kernel, width // H, stretches),
        "cross_backward",
        (width // STEP,),
        index,
        inputs,
        outputs,
        [pltpu.VMEM((tok, width), jnp.float32), pltpu.VMEM((tok, width), jnp.bfloat16)],
        13.0,
    )


def swap(values, axis, bit):
    count = lax.axis_size(axis)
    return lax.ppermute(values, axis, [(i, i ^ bit) for i in range(count)])


def after(value, *earlier):
    return lax.optimization_barrier((value,) + earlier)[0]


def mirrored(position, count):
    out = 0
    for _ in range(count.bit_length() - 1):
        out, position = 2 * out + position % 2, position // 2
    return out


def positions_kernel(
    stretches, index_ref, deal_ref, lengths_ref, pos_ref, low_ref, high_ref, keep_ref
):
    ctx_index = index_ref[1]
    held = pos_ref.shape[0] // STRETCH
    offset = lax.broadcasted_iota(jnp.int32, (STRETCH, 1), 0)
    for s in range(held):
        device = ctx_index ^ mirrored(s // stretches, held // stretches)
        given = deal_ref[device * stretches + s % stretches]
        pos_ref[pl.ds(s * STRETCH, STRETCH), :] = given * STRETCH + offset
    lane = lax.broadcasted_iota(jnp.int32, low_ref.shape, 1) % (stretches * STRETCH)
    low_pos = jnp.zeros(low_ref.shape, jnp.int32)
    high_pos = jnp.zeros(low_ref.shape, jnp.int32)
    for s in range(stretches):
        given = deal_ref[ctx_index * stretches + s]
        start, end = 0, 0
        for q in range(lengths_ref.shape[0]):
            start = jnp.where(end <= given, end, start)
            end = end + lengths_ref[q]
        here = lane // STRETCH == s
        low_pos = jnp.where(here, start * STRETCH, low_pos)
        high_pos = jnp.where(here, given * STRETCH + lane % STRETCH, high_pos)
        kept = jnp.where(given != start, 1.0, 0.0).astype(jnp.float32)
        keep_ref[pl.ds(s * STRETCH, STRETCH), :] = jnp.full((STRETCH, 1), kept, jnp.float32)
    low_ref[...] = low_pos
    high_ref[...] = high_pos


def positions(index, deal_row, lengths_row, stretches):
    tok_count = stretches * STRETCH
    smem = pl.BlockSpec(memory_space=pltpu.SMEM)
    vmem = pl.BlockSpec(memory_space=pltpu.VMEM)
    return pl.pallas_call(
        functools.partial(positions_kernel, stretches),
        in_specs=[smem] * 3,
        out_specs=[vmem] * 4,
        out_shape=[
            jax.ShapeDtypeStruct((deal_row.shape[0] * STRETCH, 1), jnp.int32),
            jax.ShapeDtypeStruct((1, 2 * tok_count), jnp.int32),
            jax.ShapeDtypeStruct((1, 2 * tok_count), jnp.int32),
            jax.ShapeDtypeStruct((tok_count, 1), jnp.float32),
        ],
        cost_estimate=lasting(0.01),
        name="positions",
    )(index, deal_row, lengths_row)


def chunk_count(rows):
    count = lax.axis_size("ctx")
    return count if count & (count - 1) == 0 and rows % (8 * count) == 0 else 1


def store_chunks(out_ref, start, held_ref, base, rows, own_chunk, chunks):
    size = rows // chunks
    for p in range(chunks):
        place = base + (own_chunk ^ p) * size
        part = held_ref[pl.ds(pl.multiple_of(place, 8), size), :]
        out_ref[pl.ds(start + p * size, size), :] = part.astype(out_ref.dtype)


def products_kernel(tiles, rows, chunks, index_ref, *refs):
    count = len(tiles)
    inputs, (keep_ref, send_ref, held_ref) = refs[:-3], refs[-3:]
    fsdp_index, own_chunk = index_ref[0], index_ref[2]
    width = held_ref.shape[1]
    for t, (left, right, column) in enumerate(tiles):

        @pl.when(pl.program_id(0) == t)
        def _(left=left, right=right, column=column):
            grads = inputs[right][:, pl.ds(column * width, width)]
            held_ref[...] = left_product(inputs[left][...], grads)

    for out_ref, order in ((keep_ref, (0, 2)), (send_ref, (1, 3))):
        for k, j in enumerate(order):
            store_chunks(
                out_ref, k * rows, held_ref, (fsdp_index ^ j) * rows, rows, own_chunk, chunks
            )


def wide_products(index, terms, microseconds):
    shares = lax.axis_size("fsdp")
    inputs, tiles = [], []
    width = terms[0][0].shape[1]
    for left, right, plane in terms:
        count = right.shape[-2]
        if not any(left is value and count == held for value, held in inputs):
            inputs.append((left, count))
        first = next(i for i, (v, held) in enumerate(inputs) if v is left and held == count)
        inputs.append((right, plane))
        for column in range(right.shape[-1] // width):
            tiles.append((first, len(inputs) - 1, column))
    rows = width // shares
    chunks = chunk_count(rows)
    specs = []
    for value, plane in inputs:
        if value.ndim == 2:
            specs.append(pl.BlockSpec((plane or value.shape[0], value.shape[1]), lambda i, _: (0, 0)))
        else:
            specs.append(
                pl.BlockSpec((None,) + value.shape[1:], lambda i, _, plane=plane: (plane, 0, 0))
            )
    total = len(tiles) * width
    out = jax.ShapeDtypeStruct((2 * rows, total), jnp.bfloat16)
    out_spec = pl.BlockSpec((2 * rows, width), lambda i, _: (0, i))
    return pl.pallas_call(
        functools.partial(products_kernel, tiles, rows, chunks),
        grid_spec=pltpu.PrefetchScalarGridSpec(
            num_scalar_prefetch=1,
            grid=(len(tiles),),
            in_specs=specs,
            out_specs=[out_spec, out_spec],
            scratch_shapes=[pltpu.VMEM((width, width), jnp.float32)],
        ),
        out_shape=[out, out],
        cost_estimate=lasting(microseconds),
        name="wide_products",
    )(index, *[value for value, _ in inputs])


def add_low(*parts):
    return to_low(sum(part.astype(jnp.float32) for part in parts))


def reduction(keep, send):
    rows = keep.shape[0] // 2
    received = swap(send, "fsdp", 1)
    received = yield send, received
    sent = add_low(keep[rows:], received[rows:])
    across = swap(sent, "fsdp", 2)
    across = yield sent, across
    return (yield from ctx_reduction((keep[:rows], received[:rows], across)))


def in_order(index, bit, own, far):
    upper = (index & bit) != 0
    return jnp.concatenate([jnp.where(upper, far, own), jnp.where(upper, own, far)], axis=0)


def ctx_reduction(parts):
    index = lax.axis_index("ctx")
    half = parts[0].shape[0] // 2
    chunks = chunk_count(2 * half)
    if chunks == 1:
        share = lax.psum(add_low(*parts), "ctx")
        upper = (index & 1) != 0
        first, second = share[:half], share[half:]
        return jnp.where(upper, second, first), jnp.where(upper, first, second)
    bit = 1
    while bit < chunks:
        sent = add_low(*[part[half:] for part in parts])
        held = add_low(*[part[:half] for part in parts])
        far = swap(sent, "ctx", bit)
        parts = (held, (yield sent, far))
        half, bit = half // 2, 2 * bit
    gathered = add_low(*parts)
    while bit > 2:
        bit = bit // 2
        far = swap(gathered, "ctx", bit)
        far = yield gathered, far
        gathered = in_order(index, bit, gathered, far)
    far = swap(gathered, "ctx", 1)
    far = yield gathered, far
    return gathered, far


def finished(halves, offset, width):
    own, far = (half[:, offset : offset + width] for half in halves)
    return in_order(lax.axis_index("ctx"), 1, own, far).astype(jnp.float32)


def sum_to_owner(total):
    bit = 1
    while bit < lax.axis_size("ctx"):
        half = total.shape[0] // 2
        sent = total[half:]
        far = swap(sent, "ctx", bit)
        far = yield sent, far
        total = add_low(total[:half], far)
        bit = 2 * bit
    return total


class Steps:
    def __init__(self, steps):
        self.steps = steps
        self.result = None
        self.advance(None)

    def advance(self, arrived):
        try:
            sent, self.arriving = self.steps.send(arrived)
            return sent
        except StopIteration as stop:
            self.result = stop.value
            return stop.value[1] if isinstance(stop.value, tuple) else stop.value

    def hold(self, *token):
        if self.result is not None:
            return token[0]
        self.arriving = after(self.arriving, *token)
        return self.arriving

    def move(self, *token):
        return token[0] if self.result is not None else self.advance(self.hold(*token))

    def finish(self, *token):
        sent = token[0]
        while self.result is None:
            sent = self.move(sent)
        return sent


def gain_gradient(weight, grad, gain):
    return jnp.sum(weight.astype(jnp.float32) * grad, axis=1) / gain.astype(jnp.float32)


def local(
    hidden,
    neighbours,
    cotangent,
    stretch_deal,
    seq_lengths,
    norm_gains,
    attn_qkv,
    attn_out,
    cross_q,
    cross_kv,
    cross_out,
    mlp_in,
    mlp_out,
):
    shares = lax.axis_size("fsdp")
    fsdp_index = lax.axis_index("fsdp")
    ctx_index = lax.axis_index("ctx")
    ctx_count = lax.axis_size("ctx")
    own_chunk, bit = 0 * ctx_index, 1
    while bit < ctx_count:
        own_chunk = 2 * own_chunk + (ctx_index & bit) // bit
        bit = 2 * bit
    place = jnp.stack([fsdp_index, ctx_index, own_chunk]).astype(jnp.int32)
    feature_width = hidden.shape[2]
    own = hidden[0]
    tok = own.shape[0]
    stretch_count = tok // STRETCH
    enc_rows = neighbours[0].reshape(-1, feature_width)
    cot = cotangent[0]

    key_pos, low_pos, high_pos, keep_rows = positions(
        place, stretch_deal[0], seq_lengths[0], stretch_count
    )

    first_share = jnp.concatenate(
        [attn_qkv, jnp.pad(norm_gains.T, ((0, 0), (0, 128 - norm_gains.shape[0])))], axis=1
    )
    across_qkv = swap(first_share, "fsdp", 2)
    if ctx_count == 8:
        far, last, near = swap(own, "ctx", 4), swap(own, "ctx", 6), swap(own, "ctx", 2)
        beside = swap(own, "ctx", 1)
        beside_near = swap(near, "ctx", 1)
        second = after(jnp.concatenate([far, last], axis=0), near)
        row_pieces = [own, near, second, beside, beside_near, swap(second, "ctx", 1)]
        layout = [[k * tok for k in ks] for ks in ((0,), (2,), (1, 3), (4,), (6,), (5, 7))]
        second = after(second, beside)
    else:
        first = own
        bit = ctx_count
        while bit > 2:
            bit = bit // 2
            first = jnp.concatenate([first, swap(first, "ctx", bit)], axis=0)
        row_pieces = [first, swap(first, "ctx", 1)]
        layout = [[k * first.shape[0]] for k in range(2)]
        second = first
    sibling_qkv = swap(after(first_share, second), "fsdp", 1)
    across_qkv = after(across_qkv, second)
    diagonal_qkv = swap(across_qkv, "fsdp", 1)
    pair_share = jnp.concatenate([attn_out, cross_q], axis=1)
    across_pair = swap(after(pair_share, second), "fsdp", 2)
    cross_share = jnp.concatenate([cross_kv, cross_out], axis=1)
    across_cross = swap(after(cross_share, second), "fsdp", 2)
    depth = mlp_out.shape[0]
    rows_in = mlp_in.shape[0]

    def block_of(j):
        return lax.dynamic_slice_in_dim(mlp_in, (fsdp_index ^ j) * depth, depth, axis=1)

    block_own = block_of(0)
    exchange_sibling = jnp.concatenate([block_of(1), cot], axis=0)
    exchange_across = jnp.concatenate([block_of(2), block_of(3), cot], axis=0)

    rows_all, scale_all = held_rows(row_pieces, layout)
    query, key_value, norm_all, w_qkv, gain_rows = project(
        place,
        rows_all,
        scale_all,
        [first_share, sibling_qkv, across_qkv, after(diagonal_qkv, scale_all)],
        tok,
    )
    across_pair = after(across_pair, query)
    diagonal_pair = swap(across_pair, "fsdp", 1)
    sibling_pair = swap(after(pair_share, query), "fsdp", 1)
    from_across = swap(after(exchange_across, across_pair), "fsdp", 2)
    attended, log_total = self_forward(query, key_value, key_pos, low_pos, high_pos)
    sibling_cross = swap(after(cross_share, attended), "fsdp", 1)
    across_cross = after(across_cross, attended)
    after_attn, norm_two, cross_query, w_pair = attend_out(
        place, attended, own, gain_rows, [pair_share, sibling_pair, across_pair, diagonal_pair]
    )
    diagonal_cross = swap(across_cross, "fsdp", 1)
    cross_key_value, cross_rows, after_cross, norm_three, w_ckv, w_cout = cross_forward(
        place,
        cross_query,
        enc_rows,
        after_attn,
        keep_rows,
        gain_rows,
        [cross_share, sibling_cross, across_cross, diagonal_cross],
        stretch_count,
    )
    from_sibling = swap(after(exchange_sibling, cross_query), "fsdp", 1)
    norm_across, norm_sibling = swap(norm_three, "fsdp", 2), swap(norm_three, "fsdp", 1)
    from_across = after(from_across, norm_three)
    from_diagonal = swap(from_across, "fsdp", 1)
    norm_diagonal = swap(norm_across, "fsdp", 1)
    (
        grad_own, grad_sibling, grad_across, grad_diagonal, out_own, out_across, out_send, share_down,
        keep_in, send_in,
    ) = mlp_share(
        place,
        [norm_three, norm_sibling, norm_across, norm_diagonal],
        cot,
        block_own,
        [from_sibling, from_across, from_diagonal],
        mlp_out,
    )

    terms = (
        grad_own,
        swap(grad_sibling, "fsdp", 1),
        swap(grad_across, "fsdp", 2),
        swap(grad_diagonal, "fsdp", 3),
    )
    received_in = swap(send_in, "fsdp", 1)
    across_in = swap(
        jnp.concatenate([keep_in[rows_in:], received_in[rows_in:]], axis=1), "fsdp", 2
    )
    down = Steps(ctx_reduction((share_down,)))
    (
        grad_cross_query, grad_cross_pair, grad_after_attn, grad_attn_branch, grad_attended,
        grad_cross_branch,
    ) = cross_backward(
        place,
        cross_query,
        cross_key_value,
        cot,
        terms,
        after_cross,
        w_cout,
        keep_rows,
        w_pair,
        after_attn,
        gain_rows,
        stretch_count,
    )
    across_in = after(across_in, grad_attended)
    out_sibling = swap(after(out_send, grad_attended), "fsdp", 1)
    arrived = down.hold(grad_attended)
    keep_cross, send_cross = wide_products(
        place,
        [
            (cross_rows, grad_cross_branch, None),
            (norm_two, grad_cross_query, None),
            (enc_rows, after(grad_cross_pair, across_in, arrived), 0),
            (enc_rows, grad_cross_pair, 1),
            (attended, grad_attn_branch, None),
        ],
        8.2,
    )
    cross = Steps(reduction(keep_cross, send_cross))
    ready = down.move(keep_cross)
    share_in = jnp.concatenate(
        [keep_in[:rows_in], received_in[:rows_in], after(across_in, ready)], axis=1
    )
    inner = Steps(ctx_reduction((share_in,)))
    ready = cross.move(share_in)
    grad_query, grad_pair = self_backward(
        query,
        key_value,
        after(grad_attended, ready),
        key_pos,
        low_pos,
        high_pos,
        log_total,
    )
    out_sibling = after(out_sibling, grad_query)
    out_far = swap(add_low(out_across, out_sibling[1]), "fsdp", 2)
    ready = inner.move(down.move(grad_query))
    keep_attn, send_attn = wide_products(
        place,
        [
            (norm_all, after(grad_query, ready), None),
            (norm_all, grad_pair, 0),
            (norm_all, grad_pair, 1),
        ],
        0.01,
    )
    attn = Steps(reduction(keep_attn, send_attn))
    norm1_all, norm1_query = norm_terms(place, after(grad_pair, keep_attn), grad_query, w_qkv)
    ready = cross.move(norm1_all)
    norm1 = Steps(sum_to_owner(after(norm1_all, ready)))
    grad_enc = enc_terms(place, after(grad_cross_pair, ready), w_ckv)
    ready = attn.move(grad_enc)
    layer_out = after_cross + (
        out_own + out_sibling[0].astype(jnp.float32) + after(out_far, ready).astype(jnp.float32)
    )
    ready = down.move(ready, layer_out)
    for step in (inner, cross, down, inner, attn, norm1, cross, attn, down, inner, norm1):
        ready = step.move(ready)
    for step in (cross, attn, inner):
        ready = step.move(ready)
    ready = down.finish(norm1.finish(ready))
    input_rows = own.astype(jnp.float32)
    grad_norm1 = norm1.result.astype(jnp.float32) + norm1_query
    grad_input = grad_after_attn + rms_back(
        input_rows, inverse_rms(input_rows), after(gain_rows, ready)[0:1], grad_norm1
    )
    total_down = finished(down.result, 0, feature_width)
    ready = cross.move(ready, total_down, grad_input)
    ready = attn.move(ready)
    ready = cross.move(ready)
    ready = attn.move(ready)
    ready = inner.finish(ready)
    total_in, gain_three = inner_out(place, inner.result, mlp_in, norm_gains[2])
    cross.move(ready, total_in)
    ready = cross.finish(ready)
    d = feature_width
    total_cout = finished(cross.result, 0, d)
    total_cq = finished(cross.result, d, d)
    total_ckv = finished(cross.result, 2 * d, 2 * d)
    total_out = finished(cross.result, 4 * d, d)
    gain_two = gain_gradient(cross_q, total_cq, norm_gains[1])
    attn.move(ready, total_cout, total_ckv, total_out, gain_two)
    attn.finish(ready)
    total_qkv = finished(attn.result, 0, 3 * d)
    gain_one = gain_gradient(attn_qkv, total_qkv, norm_gains[0])
    grad_gains = jnp.stack([gain_one, gain_two, gain_three])
    return (
        layer_out[None],
        grad_input[None],
        grad_enc.reshape(neighbours.shape),
        grad_gains,
        total_qkv,
        total_out,
        total_cq,
        total_ckv,
        total_cout,
        total_in,
        total_down,
    )


def solution(mesh):
    return jax.shard_map(
        local,
        mesh=mesh,
        in_specs=(
            P("fsdp", "ctx", None),
            P("fsdp", "ctx", None, None),
            P("fsdp", "ctx", None),
            P("fsdp", None),
            P("fsdp", None),
            P(None, "fsdp"),
            P("fsdp", None),
            P("fsdp", None),
            P("fsdp", None),
            P("fsdp", None),
            P("fsdp", None),
            P("fsdp", None),
            P("fsdp", None),
        ),
        out_specs=(
            P("fsdp", "ctx", None),
            P("fsdp", "ctx", None),
            P("fsdp", "ctx", None, None),
            P(None, "fsdp"),
            P("fsdp", None),
            P("fsdp", None),
            P("fsdp", None),
            P("fsdp", None),
            P("fsdp", None),
            P("fsdp", None),
            P("fsdp", None),
        ),
        check_vma=False,
    )
```

```python
import functools

import jax
import jax.numpy as jnp
from jax import lax
from jax.experimental import pallas as pl
from jax.experimental.pallas import tpu as pltpu
from jax.sharding import PartitionSpec as P

H = 12
STRETCH = 64


NORM_EPS = 1e-06
MASKED_SCORE = -1e30
KEY_BLOCK = 1024


def lasting(microseconds):
    return pl.CostEstimate(
        flops=int(microseconds * 1.15e10), bytes_accessed=int(microseconds * 1e6), transcendentals=0
    )


def to_low(values):
    return values.astype(jnp.bfloat16)


def matmul(left, right):
    return jnp.dot(left, right, preferred_element_type=jnp.float32)


def left_product(left, right):
    return lax.dot_general(left, right, (((0,), (0,)), ((), ())), preferred_element_type=jnp.float32)


def right_product(left, right):
    return lax.dot_general(left, right, (((1,), (1,)), ((), ())), preferred_element_type=jnp.float32)


def inverse_rms(values):
    return lax.rsqrt(jnp.mean(values * values, axis=-1, keepdims=True) + NORM_EPS)


def rms_back(values, scale, gain, grad):
    gained = gain * grad
    along = jnp.mean(gained * values, axis=-1, keepdims=True)
    return scale * gained - values * (scale * scale * scale) * along


PAIR = 128
STEP = 256


def head_rows(rows, head_size, scale=1.0):
    wide = rows.astype(jnp.float32) * scale
    lane = lax.broadcasted_iota(jnp.int32, wide.shape, 1)
    first = jnp.where(lane < head_size, wide, 0.0)
    second = jnp.where(lane >= head_size, wide, 0.0)
    return to_low(jnp.concatenate([first, second], axis=0))


def join_heads(columns, head_size):
    tok_count = columns.shape[1] // 2
    return jnp.concatenate(
        [columns[:head_size, :tok_count], columns[head_size:, tok_count:]], axis=0
    ).T


def self_forward_kernel(
    head_size, blocks, q_ref, k_ref, v_ref, pos_ref, low_ref, high_ref, o_ref, lse_ref
):
    score_scale = head_size ** (-0.5)
    low_pos, high_pos = low_ref[...], high_ref[...]
    rows = k_ref.shape[0] // blocks

    def span_of(index):
        return pl.ds(pl.multiple_of(index * rows, rows), rows)

    def visible(index):
        key_pos = pos_ref[span_of(index), :]
        return (key_pos >= low_pos) & (key_pos <= high_pos)

    once = visible(0) if blocks == 1 else None
    for p in range(q_ref.shape[1] // PAIR):
        columns = pl.ds(p * PAIR, PAIR)
        query = head_rows(q_ref[:, columns], head_size, score_scale)

        def scores_of(index, query=query, columns=columns):
            seen = visible(index) if once is None else once
            scores = right_product(k_ref[span_of(index), columns], query)
            return jnp.where(seen, scores, MASKED_SCORE)

        if blocks == 1:
            scores = scores_of(0)
            peak = jnp.max(scores, axis=0, keepdims=True)
            weights = jnp.exp(scores - peak)
            total = jnp.sum(weights, axis=0, keepdims=True)
            running = left_product(v_ref[:, columns], to_low(weights))
        else:
            peak = lax.fori_loop(
                0,
                blocks,
                lambda i, top: jnp.maximum(top, jnp.max(scores_of(i), axis=0, keepdims=True)),
                jnp.full((1, query.shape[0]), MASKED_SCORE, jnp.float32),
            )

            def add(index, state, peak=peak, columns=columns, scores_of=scores_of):
                total, running = state
                weights = jnp.exp(scores_of(index) - peak)
                return (
                    total + jnp.sum(weights, axis=0, keepdims=True),
                    running + left_product(v_ref[span_of(index), columns], to_low(weights)),
                )

            total, running = lax.fori_loop(
                0,
                blocks,
                add,
                (
                    jnp.zeros((1, query.shape[0]), jnp.float32),
                    jnp.zeros((2 * head_size, query.shape[0]), jnp.float32),
                ),
            )
        o_ref[:, columns] = to_low(join_heads(running / total, head_size))
        lse_ref[p] = peak + jnp.log(total)


def self_backward_kernel(
    head_size,
    blocks,
    q_ref,
    k_ref,
    v_ref,
    do_ref,
    pos_ref,
    low_ref,
    high_ref,
    lse_ref,
    dq_ref,
    dkv_ref,
):
    score_scale = head_size ** (-0.5)
    low_pos, high_pos = low_ref[...], high_ref[...]
    rows = k_ref.shape[0] // blocks

    def span_of(index):
        return pl.ds(pl.multiple_of(index * rows, rows), rows)

    def visible(index):
        key_pos = pos_ref[span_of(index), :]
        return (key_pos >= low_pos) & (key_pos <= high_pos)

    once = visible(0) if blocks == 1 else None
    for p in range(q_ref.shape[1] // PAIR):
        columns = pl.ds(p * PAIR, PAIR)
        query = head_rows(q_ref[:, columns], head_size, score_scale)
        grad = head_rows(do_ref[:, columns], head_size)
        log_total = lse_ref[p]

        def pair_of(index, query=query, grad=grad, log_total=log_total, columns=columns):
            span = span_of(index)
            seen = visible(index) if once is None else once
            scores = jnp.where(seen, right_product(k_ref[span, columns], query), MASKED_SCORE)
            return jnp.exp(scores - log_total), right_product(v_ref[span, columns], grad)

        def finish(index, probs, dprobs, delta, query=query, grad=grad, columns=columns):
            span = span_of(index)
            dscores = to_low(probs * (dprobs - delta))
            dkv_ref[0, span, columns] = to_low(matmul(dscores, query))
            dkv_ref[1, span, columns] = to_low(matmul(to_low(probs), grad))
            return left_product(k_ref[span, columns], dscores)

        if blocks == 1:
            probs, dprobs = pair_of(0)
            delta = jnp.sum(probs * dprobs, axis=0, keepdims=True)
            turned = finish(0, probs, dprobs, delta)
        else:

            def add_delta(index, delta, pair_of=pair_of):
                probs, dprobs = pair_of(index)
                return delta + jnp.sum(probs * dprobs, axis=0, keepdims=True)

            delta = lax.fori_loop(
                0, blocks, add_delta, jnp.zeros((1, query.shape[0]), jnp.float32)
            )

            def add_query(index, turned, delta=delta, pair_of=pair_of, finish=finish):
                probs, dprobs = pair_of(index)
                return turned + finish(index, probs, dprobs, delta)

            turned = lax.fori_loop(
                0, blocks, add_query, jnp.zeros((2 * head_size, query.shape[0]), jnp.float32)
            )
        dq_ref[:, columns] = to_low(score_scale * join_heads(turned, head_size))


def self_specs(tok_count, key_count, steps):
    return (
        pl.BlockSpec((tok_count, STEP), lambda i: (0, i)),
        pl.BlockSpec((key_count, STEP), lambda i: (0, i)),
        pl.BlockSpec((key_count, STEP), lambda i: (0, steps + i)),
        pl.BlockSpec((key_count, 1), lambda i: (0, 0)),
        pl.BlockSpec((1, 2 * tok_count), lambda i: (0, 0)),
        pl.BlockSpec((STEP // PAIR, 1, 2 * tok_count), lambda i: (i, 0, 0)),
    )


def self_forward(query, key_value, key_pos, low_pos, high_pos):
    tok_count, feature_width = query.shape
    key_count = key_value.shape[0]
    head_size = feature_width // H
    steps = feature_width // STEP
    blocks = max(1, key_count // KEY_BLOCK)
    rows, keys, values, pos, edge, lse = self_specs(tok_count, key_count, steps)
    return pl.pallas_call(
        functools.partial(self_forward_kernel, head_size, blocks),
        grid=(steps,),
        in_specs=[rows, keys, values, pos, edge, edge],
        out_specs=[rows, lse],
        out_shape=[
            jax.ShapeDtypeStruct((tok_count, feature_width), jnp.bfloat16),
            jax.ShapeDtypeStruct((H // 2, 1, 2 * tok_count), jnp.float32),
        ],
        cost_estimate=lasting(7.6),
        name="self_forward",
    )(query, key_value, key_value, key_pos, low_pos, high_pos)


def self_backward(query, key_value, grad, key_pos, low_pos, high_pos, log_total):
    tok_count, feature_width = query.shape
    key_count = key_value.shape[0]
    head_size = feature_width // H
    steps = feature_width // STEP
    blocks = max(1, key_count // KEY_BLOCK)
    rows, keys, values, pos, edge, lse = self_specs(tok_count, key_count, steps)
    return pl.pallas_call(
        functools.partial(self_backward_kernel, head_size, blocks),
        grid=(steps,),
        in_specs=[rows, keys, values, rows, pos, edge, edge, lse],
        out_specs=[rows, pl.BlockSpec((2, key_count, STEP), lambda i: (0, 0, i))],
        out_shape=[
            jax.ShapeDtypeStruct((tok_count, feature_width), jnp.bfloat16),
            jax.ShapeDtypeStruct((2, key_count, feature_width), jnp.bfloat16),
        ],
        cost_estimate=lasting(10.2),
        name="self_backward",
    )(query, key_value, key_value, grad, key_pos, low_pos, high_pos, log_total)


WHOLE = ((0, None), (1, None), (2, None), (3, None))
HALVES = ((0, None), (1, None), (2, 0), (2, 1), (3, 0), (3, 1))


def bases_of(pieces):
    return WHOLE if len(pieces) == len(WHOLE) else HALVES


def fill(out_ref, pieces, index_ref, columns=slice(None)):
    rows = pieces[0].shape[0]
    for piece, (j, half) in zip(pieces, bases_of(pieces)):
        place = (index_ref[0] ^ j) * rows
        if half is not None:
            place = place + ((index_ref[1] % 2) ^ half) * (rows // 2)
        part = piece[:, columns].astype(out_ref.dtype)
        out_ref[pl.ds(pl.multiple_of(place, 16), piece.shape[0]), :] = part


def whole(value):
    zeros = (0,) * value.ndim
    return pl.BlockSpec(value.shape, lambda *_: zeros)


def chain_call(kernel, name, grid, index, inputs, outputs, scratch, microseconds):
    return pl.pallas_call(
        kernel,
        grid_spec=pltpu.PrefetchScalarGridSpec(
            num_scalar_prefetch=1,
            grid=grid,
            in_specs=[spec for _, spec in inputs],
            out_specs=[spec for _, _, spec in outputs],
            scratch_shapes=scratch,
        ),
        out_shape=[jax.ShapeDtypeStruct(shape, dtype) for shape, dtype, _ in outputs],
        cost_estimate=lasting(microseconds),
        name=name,
    )(index, *[value for value, _ in inputs])


def const(shape):
    zeros = (0,) * len(shape)
    return pl.BlockSpec(shape, lambda *_: zeros)


def rows_kernel(layout, *refs):
    row_refs, (rows_ref, scale_ref) = refs[: len(layout)], refs[len(layout) :]
    for row_ref, places in zip(row_refs, layout):
        count = row_ref.shape[0] // len(places)
        for k, place in enumerate(places):
            rows = row_ref[pl.ds(k * count, count), :]
            rows_ref[pl.ds(place, count), :] = rows
            scale_ref[pl.ds(place, count), :] = inverse_rms(rows.astype(jnp.float32))


def held_rows(row_pieces, layout):
    total = sum(piece.shape[0] for piece in row_pieces)
    width = row_pieces[0].shape[1]
    return pl.pallas_call(
        functools.partial(rows_kernel, layout),
        out_shape=[
            jax.ShapeDtypeStruct((total, width), jnp.bfloat16),
            jax.ShapeDtypeStruct((total, 1), jnp.float32),
        ],
        cost_estimate=lasting(2.0),
        name="held_rows",
    )(*row_pieces)


def project_kernel(tok, pieces, index_ref, rows_ref, scale_ref, *refs):
    piece_refs, (q_ref, kv_ref, norm_ref, w_ref, gain_ref, column_ref) = (
        refs[:pieces],
        refs[pieces:],
    )
    width = q_ref.shape[1]
    step = pl.program_id(0)

    @pl.when(step == 0)
    def _():
        fill(w_ref, piece_refs, index_ref, slice(0, 3 * width))
        fill(column_ref, piece_refs, index_ref, slice(3 * width, 3 * width + 128))
        gain_ref[...] = column_ref[...].T[: gain_ref.shape[0], :]

    norm = to_low(rows_ref[...].astype(jnp.float32) * scale_ref[...] * gain_ref[0:1, :])
    norm_ref[...] = norm
    kv_ref[...] = to_low(matmul(norm, w_ref[:, width:]))

    @pl.when(step == 0)
    def _():
        q_ref[...] = to_low(matmul(norm_ref[pl.ds(0, tok), :], w_ref[:, :width]))


def project(index, rows, scale, pieces, tok):
    total, width = rows.shape
    block = min(512, total)

    def rows_of(columns):
        return pl.BlockSpec((block, columns), lambda i, _: (i, 0))

    inputs = [(rows, rows_of(width)), (scale, rows_of(1))]
    inputs += [(value, whole(value)) for value in pieces]
    outputs = [
        ((tok, width), jnp.bfloat16, const((tok, width))),
        ((total, 2 * width), jnp.bfloat16, rows_of(2 * width)),
        ((total, width), jnp.bfloat16, rows_of(width)),
        ((width, 3 * width), jnp.bfloat16, const((width, 3 * width))),
        ((8, width), jnp.float32, const((8, width))),
    ]
    return chain_call(
        functools.partial(project_kernel, tok, len(pieces)),
        "project",
        (total // block,),
        index,
        inputs,
        outputs,
        [pltpu.VMEM((width, 128), jnp.float32)],
        9.0,
    )


def enc_terms_kernel(index_ref, pair_ref, w_ref, out_ref):
    out_ref[...] = right_product(pair_ref[0], w_ref[0]) + right_product(pair_ref[1], w_ref[1])


def enc_terms(index, grad_pair, w_pair):
    _, total, width = grad_pair.shape
    block = min(256, total)
    inputs = [
        (grad_pair, pl.BlockSpec((2, block, width), lambda i, _: (0, i, 0))),
        (w_pair, whole(w_pair)),
    ]
    outputs = [((total, width), jnp.float32, pl.BlockSpec((block, width), lambda i, _: (i, 0)))]
    return chain_call(
        enc_terms_kernel, "enc_terms", (total // block,), index, inputs, outputs, [], 4.0
    )[0]


def norm_terms_kernel(index_ref, pair_ref, query_ref, w_ref, out_ref, own_ref):
    width = out_ref.shape[1]
    out_ref[...] = to_low(
        right_product(pair_ref[0], w_ref[:, width : 2 * width])
        + right_product(pair_ref[1], w_ref[:, 2 * width :])
    )

    @pl.when(pl.program_id(0) == 0)
    def _():
        own_ref[...] = right_product(query_ref[...], w_ref[:, :width])


def norm_terms(index, grad_pair, grad_query, w_qkv):
    _, total, width = grad_pair.shape
    tok = grad_query.shape[0]
    block = min(512, total)
    inputs = [
        (grad_pair, pl.BlockSpec((2, block, width), lambda i, _: (0, i, 0))),
        (grad_query, whole(grad_query)),
        (w_qkv, whole(w_qkv)),
    ]
    outputs = [
        ((total, width), jnp.bfloat16, pl.BlockSpec((block, width), lambda i, _: (i, 0))),
        ((tok, width), jnp.float32, const((tok, width))),
    ]
    return chain_call(
        norm_terms_kernel, "norm_terms", (total // block,), index, inputs, outputs, [], 0.01
    )


def attend_out_kernel(pieces, index_ref, att_ref, own_ref, gain_ref, *refs):
    piece_refs, (after_ref, norm_ref, query_ref, w_ref) = refs[:pieces], refs[pieces:]
    width = att_ref.shape[1]
    fill(w_ref, piece_refs, index_ref)
    rows = own_ref[...].astype(jnp.float32) + matmul(att_ref[...], w_ref[:, :width])
    after_ref[...] = rows
    norm = to_low(rows * inverse_rms(rows) * gain_ref[1:2, :])
    norm_ref[...] = norm
    query_ref[...] = to_low(matmul(norm, w_ref[:, width:]))


def attend_out(index, attended, own, gain_rows, pieces):
    tok, width = attended.shape
    inputs = [(value, whole(value)) for value in (attended, own, gain_rows)]
    inputs += [
        (piece, pl.BlockSpec((piece.shape[0], 2 * width), lambda *_: (0, 0))) for piece in pieces
    ]
    outputs = [
        ((tok, width), jnp.float32, const((tok, width))),
        ((tok, width), jnp.bfloat16, const((tok, width))),
        ((tok, width), jnp.bfloat16, const((tok, width))),
        ((width, 2 * width), jnp.bfloat16, const((width, 2 * width))),
    ]
    return chain_call(
        functools.partial(attend_out_kernel, len(pieces)),
        "attend_out",
        (1,),
        index,
        inputs,
        outputs,
        [],
        4.4,
    )


def cross_forward_kernel(head_size, stretches, pieces, index_ref, *refs):
    q_ref, enc_ref, rows_ref, keep_ref, gain_ref = refs[:5]
    refs = refs[5:]
    key_refs, value_refs = refs[:pieces], refs[pieces : 2 * pieces]
    out_refs, refs = refs[2 * pieces : 3 * pieces], refs[3 * pieces :]
    kv_ref, cross_ref, after_ref, norm_ref, wkv_ref, wout_ref = refs
    score_scale = head_size ** (-0.5)
    pair = pl.program_id(0)
    wide = q_ref.shape[1]
    fill(wkv_ref.at[0], key_refs, index_ref)
    fill(wkv_ref.at[1], value_refs, index_ref)
    kv_ref[0] = to_low(matmul(enc_ref[...], wkv_ref[0]))
    kv_ref[1] = to_low(matmul(enc_ref[...], wkv_ref[1]))

    @pl.when(pair == 0)
    def _():
        fill(wout_ref, out_refs, index_ref)

    keys = enc_ref.shape[0] // stretches
    sides = []
    for p in range(wide // PAIR):
        part = pl.ds(p * PAIR, PAIR)
        parts = []
        for s in range(stretches):
            span = pl.ds(s * keys, keys)
            query = head_rows(q_ref[pl.ds(s * STRETCH, STRETCH), part], head_size, score_scale)
            scores = right_product(kv_ref[0, span, part], query)
            weights = jnp.exp(scores - jnp.max(scores, axis=0, keepdims=True))
            probs = to_low(weights / jnp.sum(weights, axis=0, keepdims=True))
            parts.append(join_heads(left_product(kv_ref[1, span, part], probs), head_size))
        sides.append(jnp.concatenate(parts, axis=0))
    columns = pl.ds(pl.multiple_of(pair * wide, wide), wide)
    cross_ref[:, columns] = to_low(jnp.concatenate(sides, axis=1))

    @pl.when(pair == pl.num_programs(0) - 1)
    def _():
        rows = rows_ref[...] + keep_ref[...] * matmul(cross_ref[...], wout_ref[...])
        after_ref[...] = rows
        norm_ref[...] = to_low(rows * inverse_rms(rows) * gain_ref[2:3, :])


def cross_forward(index, query, enc_rows, after_attn, keep_rows, gain_rows, pieces, stretches):
    tok, width = query.shape
    pairs = width // STEP
    keys = enc_rows.shape[0]
    inputs = [(query, pl.BlockSpec((tok, STEP), lambda i, _: (0, i)))]
    inputs += [(value, whole(value)) for value in (enc_rows, after_attn, keep_rows, gain_rows)]
    for first in (0, pairs):
        inputs += [
            (piece, pl.BlockSpec((piece.shape[0], STEP), lambda i, _, f=first: (0, f + i)))
            for piece in pieces
        ]
    inputs += [(piece, pl.BlockSpec((piece.shape[0], width), lambda i, _: (0, 2))) for piece in pieces]
    outputs = [
        ((2, keys, width), jnp.bfloat16, pl.BlockSpec((2, keys, STEP), lambda i, _: (0, 0, i))),
        ((tok, width), jnp.bfloat16, const((tok, width))),
        ((tok, width), jnp.float32, const((tok, width))),
        ((tok, width), jnp.bfloat16, const((tok, width))),
        ((2, width, width), jnp.bfloat16, pl.BlockSpec((2, width, STEP), lambda i, _: (0, 0, i))),
        ((width, width), jnp.bfloat16, const((width, width))),
    ]
    return chain_call(
        functools.partial(cross_forward_kernel, width // H, stretches, len(pieces)),
        "cross_forward",
        (pairs,),
        index,
        inputs,
        outputs,
        [],
        12.3,
    )


ERF_ABOVE = (
    -2.72614225801306e-10, 2.77068142495902e-08, -2.10102402082508e-06, -5.69250639462346e-05,
    -7.34990630326855e-04, -2.95459980854025e-03, -1.60960333262415e-02,
)
ERF_BELOW = (
    -1.45660718464996e-05, -2.13374055278905e-04, -1.68282697438203e-03, -7.37332916720468e-03,
    -1.42647390514189e-02,
)


def erf(values):
    values = jnp.clip(values, -4.0, 4.0)
    square = values * values
    above, below = ERF_ABOVE[0], ERF_BELOW[0]
    for factor in ERF_ABOVE[1:]:
        above = above * square + factor
    for factor in ERF_BELOW[1:]:
        below = below * square + factor
    return values * above / below


def mlp_kernel(tok, chunks, index_ref, *refs):
    norms, cot_ref, block_ref, exchanged, down_ref = refs[:4], refs[4], refs[5], refs[6:9], refs[9]
    grad_refs, out_own_ref, out_across_ref, out_send_ref = refs[10:14], refs[14], refs[15], refs[16]
    down_share_ref, keep_ref, send_ref, w_ref, held_ref, norm_all, cot_all, act_all, inner_all = refs[
        17:
    ]
    rows_in = block_ref.shape[0]
    starts = (0, 0, rows_in)
    blocks = [ref.at[pl.ds(start, rows_in), :] for ref, start in zip(exchanged, starts)]
    fill(w_ref, [block_ref, *blocks], index_ref)
    cot_all[pl.ds(0, tok), :] = cot_ref[...]
    for k, ref in enumerate(exchanged):
        start = ref.shape[0] - tok
        cot_all[pl.ds((k + 1) * tok, tok), :] = ref[pl.ds(start, tok), :]
    for k in range(4):
        norm_all[pl.ds(k * tok, tok), :] = norms[k][...]
    for k in range(2):
        rows = pl.ds(2 * k * tok, 2 * tok)
        inner = matmul(norm_all[rows, :], w_ref[...])
        share_below = 0.5 * (1.0 + erf(inner * (2.0**-0.5)))
        activation = to_low(inner * share_below)
        act_all[rows, :] = activation
        slope = share_below + inner * jnp.exp(-0.5 * inner * inner) * ((2.0 * jnp.pi) ** -0.5)
        grad_inner = to_low(right_product(cot_all[rows, :], down_ref[...]) * slope)
        inner_all[rows, :] = grad_inner
        grad = right_product(grad_inner, w_ref[...])
        out = matmul(activation, down_ref[...])
        grad_refs[2 * k][...] = grad[:tok].astype(grad_refs[2 * k].dtype)
        grad_refs[2 * k + 1][...] = to_low(grad[tok:])
        if k == 0:
            out_own_ref[...] = out[:tok]
        else:
            out_across_ref[...] = out[:tok]
        out_send_ref[k] = to_low(out[tok:])
    depth = down_ref.shape[0]
    held_ref[...] = left_product(act_all[...], cot_all[...])
    store_chunks(down_share_ref, 0, held_ref, 0, depth, index_ref[2], chunks[1])
    held_ref[...] = left_product(norm_all[...], inner_all[...])
    rows = depth // 4
    for out_ref, order in ((keep_ref, (0, 2)), (send_ref, (1, 3))):
        for k, j in enumerate(order):
            store_chunks(
                out_ref, k * rows, held_ref, (index_ref[0] ^ j) * rows, rows, index_ref[2], chunks[0]
            )


def mlp_share(index, norms, cot, block_own, exchanged, w_down):
    depth, width = w_down.shape
    tok = cot.shape[0]
    chunks = (chunk_count(width // len(WHOLE)), chunk_count(depth))
    inputs = [(value, whole(value)) for value in (*norms, cot, block_own, *exchanged, w_down)]
    token_f32 = ((tok, width), jnp.float32, const((tok, width)))
    token_low = ((tok, width), jnp.bfloat16, const((tok, width)))
    token_send = ((2, tok, width), jnp.bfloat16, const((2, tok, width)))
    rows = ((width // 2, depth), jnp.bfloat16, const((width // 2, depth)))
    outputs = [token_f32, token_low, token_low, token_low, token_f32, token_f32, token_send]
    outputs += [((depth, width), jnp.bfloat16, const((depth, width))), rows, rows]
    scratch = [pltpu.VMEM((width, depth), jnp.bfloat16), pltpu.VMEM((depth, depth), jnp.float32)]
    scratch += [pltpu.VMEM((4 * tok, depth), jnp.bfloat16)] * 4
    return chain_call(
        functools.partial(mlp_kernel, tok, chunks),
        "mlp_share",
        (1,),
        index,
        inputs,
        outputs,
        scratch,
        11.0,
    )


def inner_out_kernel(index_ref, own_ref, far_ref, weight_ref, gain_ref, out_ref, sum_ref):
    half = own_ref.shape[0]
    upper = index_ref[1] % 2
    own = own_ref[...].astype(jnp.float32)
    far = far_ref[...].astype(jnp.float32)
    out_ref[pl.ds(pl.multiple_of(upper * half, 8), half), :] = own
    out_ref[pl.ds(pl.multiple_of((1 - upper) * half, 8), half), :] = far
    part = jnp.sum(weight_ref[...].astype(jnp.float32) * out_ref[...], axis=1, keepdims=True)
    part = part / gain_ref[...]

    @pl.when(pl.program_id(0) == 0)
    def _():
        sum_ref[...] = part

    @pl.when(pl.program_id(0) > 0)
    def _():
        sum_ref[...] = sum_ref[...] + part


def inner_out(index, halves, weight, gain):
    own, far = halves
    rows, full = weight.shape
    depth = full // len(WHOLE)
    block = pl.BlockSpec((rows // 2, depth), lambda t, index_ref: (0, t ^ index_ref[0]))
    column = gain.astype(jnp.float32).reshape(rows, 1)
    inputs = [(own, block), (far, block)]
    inputs += [(weight, pl.BlockSpec((rows, depth), lambda t, _: (0, t))), (column, whole(column))]
    outputs = [
        ((rows, full), jnp.float32, pl.BlockSpec((rows, depth), lambda t, _: (0, t))),
        ((rows, 1), jnp.float32, const((rows, 1))),
    ]
    total, sums = chain_call(
        inner_out_kernel, "inner_out", (len(WHOLE),), index, inputs, outputs, [], 3.0
    )
    return total, sums.reshape(rows)


def cross_backward_kernel(head_size, stretches, index_ref, *refs):
    q_ref, kv_ref, cot_ref, cross_ref, wout_ref, keep_ref, w_ref, rows_ref, gain_ref = refs[:9]
    terms = refs[9:13]
    dq_ref, dkv_ref, out_ref, branch_ref, attended_ref, first_ref, grad_ref, do_ref = refs[13:]
    score_scale = head_size ** (-0.5)
    pair = pl.program_id(0)
    wide = q_ref.shape[1]
    keys = kv_ref.shape[1] // stretches

    @pl.when(pair == 0)
    def _():
        values = cross_ref[...]
        grad_norm = sum(term[...].astype(jnp.float32) for term in terms)
        grad = cot_ref[...].astype(jnp.float32) + rms_back(
            values, inverse_rms(values), gain_ref[2:3, :], grad_norm
        )
        grad_ref[...] = grad
        branch = to_low(keep_ref[...] * grad)
        first_ref[...] = branch
        do_ref[...] = to_low(right_product(branch, wout_ref[...]))

    sides = []
    for p in range(wide // PAIR):
        part = pl.ds(p * PAIR, PAIR)
        place = pl.ds(pl.multiple_of(pair * wide + p * PAIR, PAIR), PAIR)
        parts = []
        for s in range(stretches):
            rows = pl.ds(s * STRETCH, STRETCH)
            span = pl.ds(s * keys, keys)
            query = head_rows(q_ref[rows, part], head_size, score_scale)
            grad = head_rows(do_ref[rows, place], head_size)
            scores = right_product(kv_ref[0, span, part], query)
            weights = jnp.exp(scores - jnp.max(scores, axis=0, keepdims=True))
            probs = weights / jnp.sum(weights, axis=0, keepdims=True)
            dprobs = right_product(kv_ref[1, span, part], grad)
            delta = jnp.sum(probs * dprobs, axis=0, keepdims=True)
            dscores = to_low(probs * (dprobs - delta))
            dkv_ref[0, span, part] = to_low(matmul(dscores, query))
            dkv_ref[1, span, part] = to_low(matmul(to_low(probs), grad))
            parts.append(join_heads(left_product(kv_ref[0, span, part], dscores), head_size))
        sides.append(jnp.concatenate(parts, axis=0))
    columns = pl.ds(pl.multiple_of(pair * wide, wide), wide)
    dq_ref[:, columns] = to_low(score_scale * jnp.concatenate(sides, axis=1))

    @pl.when(pair == pl.num_programs(0) - 1)
    def _():
        width = rows_ref.shape[1]
        values = rows_ref[...]
        grad_norm = right_product(dq_ref[...], w_ref[:, width:])
        total = grad_ref[...] + rms_back(
            values, inverse_rms(values), gain_ref[1:2, :], grad_norm
        )
        out_ref[...] = total
        branch = to_low(total)
        branch_ref[...] = branch
        attended_ref[...] = to_low(right_product(branch, w_ref[:, :width]))


def cross_backward(
    index, query, key_value, cotangent, terms, after_cross, w_cout, keep_rows, w_pair, after_attn,
    gain_rows, stretches,
):
    tok, width = query.shape
    keys = key_value.shape[1]
    block = pl.BlockSpec((tok, STEP), lambda i, _: (0, i))
    planes = pl.BlockSpec((2, keys, STEP), lambda i, _: (0, 0, i))
    inputs = [(query, block), (key_value, planes), (cotangent, whole(cotangent))]
    inputs += [
        (value, whole(value))
        for value in (after_cross, w_cout, keep_rows, w_pair, after_attn, gain_rows, *terms)
    ]
    low = ((tok, width), jnp.bfloat16, const((tok, width)))
    outputs = [
        low,
        ((2, keys, width), jnp.bfloat16, planes),
        ((tok, width), jnp.float32, const((tok, width))),
        low,
        low,
        low,
    ]
    return chain_call(
        functools.partial(cross_backward_kernel, width // H, stretches),
        "cross_backward",
        (width // STEP,),
        index,
        inputs,
        outputs,
        [pltpu.VMEM((tok, width), jnp.float32), pltpu.VMEM((tok, width), jnp.bfloat16)],
        13.0,
    )


def swap(values, axis, bit):
    count = lax.axis_size(axis)
    return lax.ppermute(values, axis, [(i, i ^ bit) for i in range(count)])


def after(value, *earlier):
    return lax.optimization_barrier((value,) + earlier)[0]


def mirrored(position, count):
    out = 0
    for _ in range(count.bit_length() - 1):
        out, position = 2 * out + position % 2, position // 2
    return out


def positions_kernel(
    stretches, index_ref, deal_ref, lengths_ref, pos_ref, low_ref, high_ref, keep_ref
):
    ctx_index = index_ref[1]
    held = pos_ref.shape[0] // STRETCH
    offset = lax.broadcasted_iota(jnp.int32, (STRETCH, 1), 0)
    for s in range(held):
        device = ctx_index ^ mirrored(s // stretches, held // stretches)
        given = deal_ref[device * stretches + s % stretches]
        pos_ref[pl.ds(s * STRETCH, STRETCH), :] = given * STRETCH + offset
    lane = lax.broadcasted_iota(jnp.int32, low_ref.shape, 1) % (stretches * STRETCH)
    low_pos = jnp.zeros(low_ref.shape, jnp.int32)
    high_pos = jnp.zeros(low_ref.shape, jnp.int32)
    for s in range(stretches):
        given = deal_ref[ctx_index * stretches + s]
        start, end = 0, 0
        for q in range(lengths_ref.shape[0]):
            start = jnp.where(end <= given, end, start)
            end = end + lengths_ref[q]
        here = lane // STRETCH == s
        low_pos = jnp.where(here, start * STRETCH, low_pos)
        high_pos = jnp.where(here, given * STRETCH + lane % STRETCH, high_pos)
        kept = jnp.where(given != start, 1.0, 0.0).astype(jnp.float32)
        keep_ref[pl.ds(s * STRETCH, STRETCH), :] = jnp.full((STRETCH, 1), kept, jnp.float32)
    low_ref[...] = low_pos
    high_ref[...] = high_pos


def positions(index, deal_row, lengths_row, stretches):
    tok_count = stretches * STRETCH
    smem = pl.BlockSpec(memory_space=pltpu.SMEM)
    vmem = pl.BlockSpec(memory_space=pltpu.VMEM)
    return pl.pallas_call(
        functools.partial(positions_kernel, stretches),
        in_specs=[smem] * 3,
        out_specs=[vmem] * 4,
        out_shape=[
            jax.ShapeDtypeStruct((deal_row.shape[0] * STRETCH, 1), jnp.int32),
            jax.ShapeDtypeStruct((1, 2 * tok_count), jnp.int32),
            jax.ShapeDtypeStruct((1, 2 * tok_count), jnp.int32),
            jax.ShapeDtypeStruct((tok_count, 1), jnp.float32),
        ],
        cost_estimate=lasting(0.01),
        name="positions",
    )(index, deal_row, lengths_row)


def chunk_count(rows):
    count = lax.axis_size("ctx")
    return count if count & (count - 1) == 0 and rows % (8 * count) == 0 else 1


def store_chunks(out_ref, start, held_ref, base, rows, own_chunk, chunks):
    size = rows // chunks
    for p in range(chunks):
        place = base + (own_chunk ^ p) * size
        part = held_ref[pl.ds(pl.multiple_of(place, 8), size), :]
        out_ref[pl.ds(start + p * size, size), :] = part.astype(out_ref.dtype)


def products_kernel(tiles, rows, chunks, index_ref, *refs):
    count = len(tiles)
    inputs, (keep_ref, send_ref, held_ref) = refs[:-3], refs[-3:]
    fsdp_index, own_chunk = index_ref[0], index_ref[2]
    width = held_ref.shape[1]
    for t, (left, right, column) in enumerate(tiles):

        @pl.when(pl.program_id(0) == t)
        def _(left=left, right=right, column=column):
            grads = inputs[right][:, pl.ds(column * width, width)]
            held_ref[...] = left_product(inputs[left][...], grads)

    for out_ref, order in ((keep_ref, (0, 2)), (send_ref, (1, 3))):
        for k, j in enumerate(order):
            store_chunks(
                out_ref, k * rows, held_ref, (fsdp_index ^ j) * rows, rows, own_chunk, chunks
            )


def wide_products(index, terms, microseconds):
    shares = lax.axis_size("fsdp")
    inputs, tiles = [], []
    width = terms[0][0].shape[1]
    for left, right, plane in terms:
        count = right.shape[-2]
        if not any(left is value and count == held for value, held in inputs):
            inputs.append((left, count))
        first = next(i for i, (v, held) in enumerate(inputs) if v is left and held == count)
        inputs.append((right, plane))
        for column in range(right.shape[-1] // width):
            tiles.append((first, len(inputs) - 1, column))
    rows = width // shares
    chunks = chunk_count(rows)
    specs = []
    for value, plane in inputs:
        if value.ndim == 2:
            specs.append(pl.BlockSpec((plane or value.shape[0], value.shape[1]), lambda i, _: (0, 0)))
        else:
            specs.append(
                pl.BlockSpec((None,) + value.shape[1:], lambda i, _, plane=plane: (plane, 0, 0))
            )
    total = len(tiles) * width
    out = jax.ShapeDtypeStruct((2 * rows, total), jnp.bfloat16)
    out_spec = pl.BlockSpec((2 * rows, width), lambda i, _: (0, i))
    return pl.pallas_call(
        functools.partial(products_kernel, tiles, rows, chunks),
        grid_spec=pltpu.PrefetchScalarGridSpec(
            num_scalar_prefetch=1,
            grid=(len(tiles),),
            in_specs=specs,
            out_specs=[out_spec, out_spec],
            scratch_shapes=[pltpu.VMEM((width, width), jnp.float32)],
        ),
        out_shape=[out, out],
        cost_estimate=lasting(microseconds),
        name="wide_products",
    )(index, *[value for value, _ in inputs])


def add_low(*parts):
    return to_low(sum(part.astype(jnp.float32) for part in parts))


def reduction(keep, send):
    rows = keep.shape[0] // 2
    received = swap(send, "fsdp", 1)
    received = yield send, received
    sent = add_low(keep[rows:], received[rows:])
    across = swap(sent, "fsdp", 2)
    across = yield sent, across
    return (yield from ctx_reduction((keep[:rows], received[:rows], across)))


def in_order(index, bit, own, far):
    upper = (index & bit) != 0
    return jnp.concatenate([jnp.where(upper, far, own), jnp.where(upper, own, far)], axis=0)


def ctx_reduction(parts):
    index = lax.axis_index("ctx")
    half = parts[0].shape[0] // 2
    chunks = chunk_count(2 * half)
    if chunks == 1:
        share = lax.psum(add_low(*parts), "ctx")
        upper = (index & 1) != 0
        first, second = share[:half], share[half:]
        return jnp.where(upper, second, first), jnp.where(upper, first, second)
    bit = 1
    while bit < chunks:
        sent = add_low(*[part[half:] for part in parts])
        held = add_low(*[part[:half] for part in parts])
        far = swap(sent, "ctx", bit)
        parts = (held, (yield sent, far))
        half, bit = half // 2, 2 * bit
    gathered = add_low(*parts)
    while bit > 2:
        bit = bit // 2
        far = swap(gathered, "ctx", bit)
        far = yield gathered, far
        gathered = in_order(index, bit, gathered, far)
    far = swap(gathered, "ctx", 1)
    far = yield gathered, far
    return gathered, far


def finished(halves, offset, width):
    own, far = (half[:, offset : offset + width] for half in halves)
    return in_order(lax.axis_index("ctx"), 1, own, far).astype(jnp.float32)


def sum_to_owner(total):
    bit = 1
    while bit < lax.axis_size("ctx"):
        half = total.shape[0] // 2
        sent = total[half:]
        far = swap(sent, "ctx", bit)
        far = yield sent, far
        total = add_low(total[:half], far)
        bit = 2 * bit
    return total


class Steps:
    def __init__(self, steps):
        self.steps = steps
        self.result = None
        self.advance(None)

    def advance(self, arrived):
        try:
            sent, self.arriving = self.steps.send(arrived)
            return sent
        except StopIteration as stop:
            self.result = stop.value
            return stop.value[1] if isinstance(stop.value, tuple) else stop.value

    def hold(self, *token):
        if self.result is not None:
            return token[0]
        self.arriving = after(self.arriving, *token)
        return self.arriving

    def move(self, *token):
        return token[0] if self.result is not None else self.advance(self.hold(*token))

    def finish(self, *token):
        sent = token[0]
        while self.result is None:
            sent = self.move(sent)
        return sent


def gain_gradient(weight, grad, gain):
    return jnp.sum(weight.astype(jnp.float32) * grad, axis=1) / gain.astype(jnp.float32)


def local(
    hidden,
    neighbours,
    cotangent,
    stretch_deal,
    seq_lengths,
    norm_gains,
    attn_qkv,
    attn_out,
    cross_q,
    cross_kv,
    cross_out,
    mlp_in,
    mlp_out,
):
    shares = lax.axis_size("fsdp")
    fsdp_index = lax.axis_index("fsdp")
    ctx_index = lax.axis_index("ctx")
    ctx_count = lax.axis_size("ctx")
    own_chunk, bit = 0 * ctx_index, 1
    while bit < ctx_count:
        own_chunk = 2 * own_chunk + (ctx_index & bit) // bit
        bit = 2 * bit
    place = jnp.stack([fsdp_index, ctx_index, own_chunk]).astype(jnp.int32)
    feature_width = hidden.shape[2]
    own = hidden[0]
    tok = own.shape[0]
    stretch_count = tok // STRETCH
    enc_rows = neighbours[0].reshape(-1, feature_width)
    cot = cotangent[0]

    key_pos, low_pos, high_pos, keep_rows = positions(
        place, stretch_deal[0], seq_lengths[0], stretch_count
    )

    first_share = jnp.concatenate(
        [attn_qkv, jnp.pad(norm_gains.T, ((0, 0), (0, 128 - norm_gains.shape[0])))], axis=1
    )
    across_qkv = swap(first_share, "fsdp", 2)
    if ctx_count == 8:
        far, last, near = swap(own, "ctx", 4), swap(own, "ctx", 6), swap(own, "ctx", 2)
        beside = swap(own, "ctx", 1)
        beside_near = swap(near, "ctx", 1)
        second = after(jnp.concatenate([far, last], axis=0), near)
        row_pieces = [own, near, second, beside, beside_near, swap(second, "ctx", 1)]
        layout = [[k * tok for k in ks] for ks in ((0,), (2,), (1, 3), (4,), (6,), (5, 7))]
        second = after(second, beside)
    else:
        first = own
        bit = ctx_count
        while bit > 2:
            bit = bit // 2
            first = jnp.concatenate([first, swap(first, "ctx", bit)], axis=0)
        row_pieces = [first, swap(first, "ctx", 1)]
        layout = [[k * first.shape[0]] for k in range(2)]
        second = first
    sibling_qkv = swap(after(first_share, second), "fsdp", 1)
    across_qkv = after(across_qkv, second)
    diagonal_qkv = swap(across_qkv, "fsdp", 1)
    pair_share = jnp.concatenate([attn_out, cross_q], axis=1)
    across_pair = swap(after(pair_share, second), "fsdp", 2)
    cross_share = jnp.concatenate([cross_kv, cross_out], axis=1)
    across_cross = swap(after(cross_share, second), "fsdp", 2)
    depth = mlp_out.shape[0]
    rows_in = mlp_in.shape[0]

    def block_of(j):
        return lax.dynamic_slice_in_dim(mlp_in, (fsdp_index ^ j) * depth, depth, axis=1)

    block_own = block_of(0)
    exchange_sibling = jnp.concatenate([block_of(1), cot], axis=0)
    exchange_across = jnp.concatenate([block_of(2), block_of(3), cot], axis=0)

    rows_all, scale_all = held_rows(row_pieces, layout)
    query, key_value, norm_all, w_qkv, gain_rows = project(
        place,
        rows_all,
        scale_all,
        [first_share, sibling_qkv, across_qkv, after(diagonal_qkv, scale_all)],
        tok,
    )
    across_pair = after(across_pair, query)
    diagonal_pair = swap(across_pair, "fsdp", 1)
    sibling_pair = swap(after(pair_share, query), "fsdp", 1)
    from_across = swap(after(exchange_across, across_pair), "fsdp", 2)
    attended, log_total = self_forward(query, key_value, key_pos, low_pos, high_pos)
    sibling_cross = swap(after(cross_share, attended), "fsdp", 1)
    across_cross = after(across_cross, attended)
    after_attn, norm_two, cross_query, w_pair = attend_out(
        place, attended, own, gain_rows, [pair_share, sibling_pair, across_pair, diagonal_pair]
    )
    diagonal_cross = swap(across_cross, "fsdp", 1)
    cross_key_value, cross_rows, after_cross, norm_three, w_ckv, w_cout = cross_forward(
        place,
        cross_query,
        enc_rows,
        after_attn,
        keep_rows,
        gain_rows,
        [cross_share, sibling_cross, across_cross, diagonal_cross],
        stretch_count,
    )
    from_sibling = swap(after(exchange_sibling, cross_query), "fsdp", 1)
    norm_across, norm_sibling = swap(norm_three, "fsdp", 2), swap(norm_three, "fsdp", 1)
    from_across = after(from_across, norm_three)
    from_diagonal = swap(from_across, "fsdp", 1)
    norm_diagonal = swap(norm_across, "fsdp", 1)
    (
        grad_own, grad_sibling, grad_across, grad_diagonal, out_own, out_across, out_send, share_down,
        keep_in, send_in,
    ) = mlp_share(
        place,
        [norm_three, norm_sibling, norm_across, norm_diagonal],
        cot,
        block_own,
        [from_sibling, from_across, from_diagonal],
        mlp_out,
    )

    terms = (
        grad_own,
        swap(grad_sibling, "fsdp", 1),
        swap(grad_across, "fsdp", 2),
        swap(grad_diagonal, "fsdp", 3),
    )
    received_in = swap(send_in, "fsdp", 1)
    across_in = swap(
        jnp.concatenate([keep_in[rows_in:], received_in[rows_in:]], axis=1), "fsdp", 2
    )
    down = Steps(ctx_reduction((share_down,)))
    (
        grad_cross_query, grad_cross_pair, grad_after_attn, grad_attn_branch, grad_attended,
        grad_cross_branch,
    ) = cross_backward(
        place,
        cross_query,
        cross_key_value,
        cot,
        terms,
        after_cross,
        w_cout,
        keep_rows,
        w_pair,
        after_attn,
        gain_rows,
        stretch_count,
    )
    across_in = after(across_in, grad_attended)
    out_sibling = swap(after(out_send, grad_attended), "fsdp", 1)
    arrived = down.hold(grad_attended)
    keep_cross, send_cross = wide_products(
        place,
        [
            (cross_rows, grad_cross_branch, None),
            (norm_two, grad_cross_query, None),
            (enc_rows, after(grad_cross_pair, across_in, arrived), 0),
            (enc_rows, grad_cross_pair, 1),
            (attended, grad_attn_branch, None),
        ],
        8.2,
    )
    cross = Steps(reduction(keep_cross, send_cross))
    ready = down.move(keep_cross)
    share_in = jnp.concatenate(
        [keep_in[:rows_in], received_in[:rows_in], after(across_in, ready)], axis=1
    )
    inner = Steps(ctx_reduction((share_in,)))
    ready = cross.move(share_in)
    grad_query, grad_pair = self_backward(
        query,
        key_value,
        after(grad_attended, ready),
        key_pos,
        low_pos,
        high_pos,
        log_total,
    )
    out_sibling = after(out_sibling, grad_query)
    out_far = swap(add_low(out_across, out_sibling[1]), "fsdp", 2)
    ready = inner.move(down.move(grad_query))
    keep_attn, send_attn = wide_products(
        place,
        [
            (norm_all, after(grad_query, ready), None),
            (norm_all, grad_pair, 0),
            (norm_all, grad_pair, 1),
        ],
        0.01,
    )
    attn = Steps(reduction(keep_attn, send_attn))
    norm1_all, norm1_query = norm_terms(place, after(grad_pair, keep_attn), grad_query, w_qkv)
    ready = cross.move(norm1_all)
    grad_enc = enc_terms(place, after(grad_cross_pair, ready), w_ckv)
    ready = attn.move(grad_enc)
    layer_out = after_cross + (
        out_own + out_sibling[0].astype(jnp.float32) + after(out_far, ready).astype(jnp.float32)
    )
    ready = down.move(ready, layer_out)
    for step in (inner, cross, down, inner, attn):
        ready = step.move(ready)
    norm1 = Steps(sum_to_owner(after(norm1_all, ready)))
    for step in (cross, attn, down, inner, cross, norm1, attn, inner, cross, norm1, attn):
        ready = step.move(ready)
    ready = norm1.finish(ready)
    input_rows = own.astype(jnp.float32)
    grad_norm1 = norm1.result.astype(jnp.float32) + norm1_query
    grad_input = grad_after_attn + rms_back(
        input_rows, inverse_rms(input_rows), after(gain_rows, ready)[0:1], grad_norm1
    )
    ready = cross.move(ready)
    ready = attn.move(down.finish(ready), grad_input)
    total_down = finished(down.result, 0, feature_width)
    ready = inner.finish(after(ready, total_down))
    ready = attn.move(ready)
    total_in, gain_three = inner_out(place, inner.result, mlp_in, norm_gains[2])
    cross.move(ready, total_in)
    ready = cross.finish(ready)
    d = feature_width
    total_cout = finished(cross.result, 0, d)
    total_cq = finished(cross.result, d, d)
    total_ckv = finished(cross.result, 2 * d, 2 * d)
    total_out = finished(cross.result, 4 * d, d)
    gain_two = gain_gradient(cross_q, total_cq, norm_gains[1])
    attn.move(ready, total_cout, total_ckv, total_out, gain_two)
    attn.finish(ready)
    total_qkv = finished(attn.result, 0, 3 * d)
    gain_one = gain_gradient(attn_qkv, total_qkv, norm_gains[0])
    grad_gains = jnp.stack([gain_one, gain_two, gain_three])
    return (
        layer_out[None],
        grad_input[None],
        grad_enc.reshape(neighbours.shape),
        grad_gains,
        total_qkv,
        total_out,
        total_cq,
        total_ckv,
        total_cout,
        total_in,
        total_down,
    )


def solution(mesh):
    return jax.shard_map(
        local,
        mesh=mesh,
        in_specs=(
            P("fsdp", "ctx", None),
            P("fsdp", "ctx", None, None),
            P("fsdp", "ctx", None),
            P("fsdp", None),
            P("fsdp", None),
            P(None, "fsdp"),
            P("fsdp", None),
            P("fsdp", None),
            P("fsdp", None),
            P("fsdp", None),
            P("fsdp", None),
            P("fsdp", None),
            P("fsdp", None),
        ),
        out_specs=(
            P("fsdp", "ctx", None),
            P("fsdp", "ctx", None),
            P("fsdp", "ctx", None, None),
            P(None, "fsdp"),
            P("fsdp", None),
            P("fsdp", None),
            P("fsdp", None),
            P("fsdp", None),
            P("fsdp", None),
            P("fsdp", None),
            P("fsdp", None),
        ),
        check_vma=False,
    )
```

```python
import functools

import jax
import jax.numpy as jnp
from jax import lax
from jax.experimental import pallas as pl
from jax.experimental.pallas import tpu as pltpu
from jax.sharding import PartitionSpec as P

H = 12
STRETCH = 64


NORM_EPS = 1e-06
MASKED_SCORE = -1e30
KEY_BLOCK = 1024


def lasting(microseconds):
    return pl.CostEstimate(
        flops=int(microseconds * 1.15e10), bytes_accessed=int(microseconds * 1e6), transcendentals=0
    )


def to_low(values):
    return values.astype(jnp.bfloat16)


def matmul(left, right):
    return jnp.dot(left, right, preferred_element_type=jnp.float32)


def left_product(left, right):
    return lax.dot_general(left, right, (((0,), (0,)), ((), ())), preferred_element_type=jnp.float32)


def right_product(left, right):
    return lax.dot_general(left, right, (((1,), (1,)), ((), ())), preferred_element_type=jnp.float32)


def inverse_rms(values):
    return lax.rsqrt(jnp.mean(values * values, axis=-1, keepdims=True) + NORM_EPS)


def rms_back(values, scale, gain, grad):
    gained = gain * grad
    along = jnp.mean(gained * values, axis=-1, keepdims=True)
    return scale * gained - values * (scale * scale * scale) * along


PAIR = 128
STEP = 256


def head_rows(rows, head_size, scale=1.0):
    wide = rows.astype(jnp.float32) * scale
    lane = lax.broadcasted_iota(jnp.int32, wide.shape, 1)
    first = jnp.where(lane < head_size, wide, 0.0)
    second = jnp.where(lane >= head_size, wide, 0.0)
    return to_low(jnp.concatenate([first, second], axis=0))


def join_heads(columns, head_size):
    tok_count = columns.shape[1] // 2
    return jnp.concatenate(
        [columns[:head_size, :tok_count], columns[head_size:, tok_count:]], axis=0
    ).T


def self_forward_kernel(
    head_size, blocks, q_ref, k_ref, v_ref, pos_ref, low_ref, high_ref, o_ref, lse_ref
):
    score_scale = head_size ** (-0.5)
    low_pos, high_pos = low_ref[...], high_ref[...]
    rows = k_ref.shape[0] // blocks

    def span_of(index):
        return pl.ds(pl.multiple_of(index * rows, rows), rows)

    def visible(index):
        key_pos = pos_ref[span_of(index), :]
        return (key_pos >= low_pos) & (key_pos <= high_pos)

    once = visible(0) if blocks == 1 else None
    for p in range(q_ref.shape[1] // PAIR):
        columns = pl.ds(p * PAIR, PAIR)
        query = head_rows(q_ref[:, columns], head_size, score_scale)

        def scores_of(index, query=query, columns=columns):
            seen = visible(index) if once is None else once
            scores = right_product(k_ref[span_of(index), columns], query)
            return jnp.where(seen, scores, MASKED_SCORE)

        if blocks == 1:
            scores = scores_of(0)
            peak = jnp.max(scores, axis=0, keepdims=True)
            weights = jnp.exp(scores - peak)
            total = jnp.sum(weights, axis=0, keepdims=True)
            running = left_product(v_ref[:, columns], to_low(weights))
        else:
            peak = lax.fori_loop(
                0,
                blocks,
                lambda i, top: jnp.maximum(top, jnp.max(scores_of(i), axis=0, keepdims=True)),
                jnp.full((1, query.shape[0]), MASKED_SCORE, jnp.float32),
            )

            def add(index, state, peak=peak, columns=columns, scores_of=scores_of):
                total, running = state
                weights = jnp.exp(scores_of(index) - peak)
                return (
                    total + jnp.sum(weights, axis=0, keepdims=True),
                    running + left_product(v_ref[span_of(index), columns], to_low(weights)),
                )

            total, running = lax.fori_loop(
                0,
                blocks,
                add,
                (
                    jnp.zeros((1, query.shape[0]), jnp.float32),
                    jnp.zeros((2 * head_size, query.shape[0]), jnp.float32),
                ),
            )
        o_ref[:, columns] = to_low(join_heads(running / total, head_size))
        lse_ref[p] = peak + jnp.log(total)


def self_backward_kernel(
    head_size,
    blocks,
    q_ref,
    k_ref,
    v_ref,
    do_ref,
    pos_ref,
    low_ref,
    high_ref,
    lse_ref,
    dq_ref,
    dkv_ref,
):
    score_scale = head_size ** (-0.5)
    low_pos, high_pos = low_ref[...], high_ref[...]
    rows = k_ref.shape[0] // blocks

    def span_of(index):
        return pl.ds(pl.multiple_of(index * rows, rows), rows)

    def visible(index):
        key_pos = pos_ref[span_of(index), :]
        return (key_pos >= low_pos) & (key_pos <= high_pos)

    once = visible(0) if blocks == 1 else None
    for p in range(q_ref.shape[1] // PAIR):
        columns = pl.ds(p * PAIR, PAIR)
        query = head_rows(q_ref[:, columns], head_size, score_scale)
        grad = head_rows(do_ref[:, columns], head_size)
        log_total = lse_ref[p]

        def pair_of(index, query=query, grad=grad, log_total=log_total, columns=columns):
            span = span_of(index)
            seen = visible(index) if once is None else once
            scores = jnp.where(seen, right_product(k_ref[span, columns], query), MASKED_SCORE)
            return jnp.exp(scores - log_total), right_product(v_ref[span, columns], grad)

        def finish(index, probs, dprobs, delta, query=query, grad=grad, columns=columns):
            span = span_of(index)
            dscores = to_low(probs * (dprobs - delta))
            dkv_ref[0, span, columns] = to_low(matmul(dscores, query))
            dkv_ref[1, span, columns] = to_low(matmul(to_low(probs), grad))
            return left_product(k_ref[span, columns], dscores)

        if blocks == 1:
            probs, dprobs = pair_of(0)
            delta = jnp.sum(probs * dprobs, axis=0, keepdims=True)
            turned = finish(0, probs, dprobs, delta)
        else:

            def add_delta(index, delta, pair_of=pair_of):
                probs, dprobs = pair_of(index)
                return delta + jnp.sum(probs * dprobs, axis=0, keepdims=True)

            delta = lax.fori_loop(
                0, blocks, add_delta, jnp.zeros((1, query.shape[0]), jnp.float32)
            )

            def add_query(index, turned, delta=delta, pair_of=pair_of, finish=finish):
                probs, dprobs = pair_of(index)
                return turned + finish(index, probs, dprobs, delta)

            turned = lax.fori_loop(
                0, blocks, add_query, jnp.zeros((2 * head_size, query.shape[0]), jnp.float32)
            )
        dq_ref[:, columns] = to_low(score_scale * join_heads(turned, head_size))


def self_specs(tok_count, key_count, steps):
    return (
        pl.BlockSpec((tok_count, STEP), lambda i: (0, i)),
        pl.BlockSpec((key_count, STEP), lambda i: (0, i)),
        pl.BlockSpec((key_count, STEP), lambda i: (0, steps + i)),
        pl.BlockSpec((key_count, 1), lambda i: (0, 0)),
        pl.BlockSpec((1, 2 * tok_count), lambda i: (0, 0)),
        pl.BlockSpec((STEP // PAIR, 1, 2 * tok_count), lambda i: (i, 0, 0)),
    )


def self_forward(query, key_value, key_pos, low_pos, high_pos):
    tok_count, feature_width = query.shape
    key_count = key_value.shape[0]
    head_size = feature_width // H
    steps = feature_width // STEP
    blocks = max(1, key_count // KEY_BLOCK)
    rows, keys, values, pos, edge, lse = self_specs(tok_count, key_count, steps)
    return pl.pallas_call(
        functools.partial(self_forward_kernel, head_size, blocks),
        grid=(steps,),
        in_specs=[rows, keys, values, pos, edge, edge],
        out_specs=[rows, lse],
        out_shape=[
            jax.ShapeDtypeStruct((tok_count, feature_width), jnp.bfloat16),
            jax.ShapeDtypeStruct((H // 2, 1, 2 * tok_count), jnp.float32),
        ],
        cost_estimate=lasting(7.6),
        name="self_forward",
    )(query, key_value, key_value, key_pos, low_pos, high_pos)


def self_backward(query, key_value, grad, key_pos, low_pos, high_pos, log_total):
    tok_count, feature_width = query.shape
    key_count = key_value.shape[0]
    head_size = feature_width // H
    steps = feature_width // STEP
    blocks = max(1, key_count // KEY_BLOCK)
    rows, keys, values, pos, edge, lse = self_specs(tok_count, key_count, steps)
    return pl.pallas_call(
        functools.partial(self_backward_kernel, head_size, blocks),
        grid=(steps,),
        in_specs=[rows, keys, values, rows, pos, edge, edge, lse],
        out_specs=[rows, pl.BlockSpec((2, key_count, STEP), lambda i: (0, 0, i))],
        out_shape=[
            jax.ShapeDtypeStruct((tok_count, feature_width), jnp.bfloat16),
            jax.ShapeDtypeStruct((2, key_count, feature_width), jnp.bfloat16),
        ],
        cost_estimate=lasting(10.2),
        name="self_backward",
    )(query, key_value, key_value, grad, key_pos, low_pos, high_pos, log_total)


WHOLE = ((0, None), (1, None), (2, None), (3, None))
HALVES = ((0, None), (1, None), (2, 0), (2, 1), (3, 0), (3, 1))


def bases_of(pieces):
    return WHOLE if len(pieces) == len(WHOLE) else HALVES


def fill(out_ref, pieces, index_ref, columns=slice(None)):
    rows = pieces[0].shape[0]
    for piece, (j, half) in zip(pieces, bases_of(pieces)):
        place = (index_ref[0] ^ j) * rows
        if half is not None:
            place = place + ((index_ref[1] % 2) ^ half) * (rows // 2)
        part = piece[:, columns].astype(out_ref.dtype)
        out_ref[pl.ds(pl.multiple_of(place, 16), piece.shape[0]), :] = part


def whole(value):
    zeros = (0,) * value.ndim
    return pl.BlockSpec(value.shape, lambda *_: zeros)


def chain_call(kernel, name, grid, index, inputs, outputs, scratch, microseconds):
    return pl.pallas_call(
        kernel,
        grid_spec=pltpu.PrefetchScalarGridSpec(
            num_scalar_prefetch=1,
            grid=grid,
            in_specs=[spec for _, spec in inputs],
            out_specs=[spec for _, _, spec in outputs],
            scratch_shapes=scratch,
        ),
        out_shape=[jax.ShapeDtypeStruct(shape, dtype) for shape, dtype, _ in outputs],
        cost_estimate=lasting(microseconds),
        name=name,
    )(index, *[value for value, _ in inputs])


def const(shape):
    zeros = (0,) * len(shape)
    return pl.BlockSpec(shape, lambda *_: zeros)


def rows_kernel(layout, *refs):
    row_refs, (rows_ref, scale_ref) = refs[: len(layout)], refs[len(layout) :]
    for row_ref, places in zip(row_refs, layout):
        count = row_ref.shape[0] // len(places)
        for k, place in enumerate(places):
            rows = row_ref[pl.ds(k * count, count), :]
            rows_ref[pl.ds(place, count), :] = rows
            scale_ref[pl.ds(place, count), :] = inverse_rms(rows.astype(jnp.float32))


def held_rows(row_pieces, layout):
    total = sum(piece.shape[0] for piece in row_pieces)
    width = row_pieces[0].shape[1]
    return pl.pallas_call(
        functools.partial(rows_kernel, layout),
        out_shape=[
            jax.ShapeDtypeStruct((total, width), jnp.bfloat16),
            jax.ShapeDtypeStruct((total, 1), jnp.float32),
        ],
        cost_estimate=lasting(2.0),
        name="held_rows",
    )(*row_pieces)


def project_kernel(tok, pieces, index_ref, rows_ref, scale_ref, *refs):
    piece_refs, (q_ref, kv_ref, norm_ref, w_ref, gain_ref, column_ref) = (
        refs[:pieces],
        refs[pieces:],
    )
    width = q_ref.shape[1]
    step = pl.program_id(0)

    @pl.when(step == 0)
    def _():
        fill(w_ref, piece_refs, index_ref, slice(0, 3 * width))
        fill(column_ref, piece_refs, index_ref, slice(3 * width, 3 * width + 128))
        gain_ref[...] = column_ref[...].T[: gain_ref.shape[0], :]

    norm = to_low(rows_ref[...].astype(jnp.float32) * scale_ref[...] * gain_ref[0:1, :])
    norm_ref[...] = norm
    kv_ref[...] = to_low(matmul(norm, w_ref[:, width:]))

    @pl.when(step == 0)
    def _():
        q_ref[...] = to_low(matmul(norm_ref[pl.ds(0, tok), :], w_ref[:, :width]))


def project(index, rows, scale, pieces, tok):
    total, width = rows.shape
    block = min(512, total)

    def rows_of(columns):
        return pl.BlockSpec((block, columns), lambda i, _: (i, 0))

    inputs = [(rows, rows_of(width)), (scale, rows_of(1))]
    inputs += [(value, whole(value)) for value in pieces]
    outputs = [
        ((tok, width), jnp.bfloat16, const((tok, width))),
        ((total, 2 * width), jnp.bfloat16, rows_of(2 * width)),
        ((total, width), jnp.bfloat16, rows_of(width)),
        ((width, 3 * width), jnp.bfloat16, const((width, 3 * width))),
        ((8, width), jnp.float32, const((8, width))),
    ]
    return chain_call(
        functools.partial(project_kernel, tok, len(pieces)),
        "project",
        (total // block,),
        index,
        inputs,
        outputs,
        [pltpu.VMEM((width, 128), jnp.float32)],
        9.0,
    )


def enc_terms_kernel(index_ref, pair_ref, w_ref, out_ref):
    out_ref[...] = right_product(pair_ref[0], w_ref[0]) + right_product(pair_ref[1], w_ref[1])


def enc_terms(index, grad_pair, w_pair):
    _, total, width = grad_pair.shape
    block = min(256, total)
    inputs = [
        (grad_pair, pl.BlockSpec((2, block, width), lambda i, _: (0, i, 0))),
        (w_pair, whole(w_pair)),
    ]
    outputs = [((total, width), jnp.float32, pl.BlockSpec((block, width), lambda i, _: (i, 0)))]
    return chain_call(
        enc_terms_kernel, "enc_terms", (total // block,), index, inputs, outputs, [], 4.0
    )[0]


def norm_terms_kernel(index_ref, pair_ref, query_ref, w_ref, out_ref, own_ref):
    width = out_ref.shape[1]
    out_ref[...] = to_low(
        right_product(pair_ref[0], w_ref[:, width : 2 * width])
        + right_product(pair_ref[1], w_ref[:, 2 * width :])
    )

    @pl.when(pl.program_id(0) == 0)
    def _():
        own_ref[...] = right_product(query_ref[...], w_ref[:, :width])


def norm_terms(index, grad_pair, grad_query, w_qkv):
    _, total, width = grad_pair.shape
    tok = grad_query.shape[0]
    block = min(512, total)
    inputs = [
        (grad_pair, pl.BlockSpec((2, block, width), lambda i, _: (0, i, 0))),
        (grad_query, whole(grad_query)),
        (w_qkv, whole(w_qkv)),
    ]
    outputs = [
        ((total, width), jnp.bfloat16, pl.BlockSpec((block, width), lambda i, _: (i, 0))),
        ((tok, width), jnp.float32, const((tok, width))),
    ]
    return chain_call(
        norm_terms_kernel, "norm_terms", (total // block,), index, inputs, outputs, [], 0.01
    )


def attend_out_kernel(pieces, index_ref, att_ref, own_ref, gain_ref, *refs):
    piece_refs, (after_ref, norm_ref, query_ref, w_ref) = refs[:pieces], refs[pieces:]
    width = att_ref.shape[1]
    fill(w_ref, piece_refs, index_ref)
    rows = own_ref[...].astype(jnp.float32) + matmul(att_ref[...], w_ref[:, :width])
    after_ref[...] = rows
    norm = to_low(rows * inverse_rms(rows) * gain_ref[1:2, :])
    norm_ref[...] = norm
    query_ref[...] = to_low(matmul(norm, w_ref[:, width:]))


def attend_out(index, attended, own, gain_rows, pieces):
    tok, width = attended.shape
    inputs = [(value, whole(value)) for value in (attended, own, gain_rows)]
    inputs += [
        (piece, pl.BlockSpec((piece.shape[0], 2 * width), lambda *_: (0, 0))) for piece in pieces
    ]
    outputs = [
        ((tok, width), jnp.float32, const((tok, width))),
        ((tok, width), jnp.bfloat16, const((tok, width))),
        ((tok, width), jnp.bfloat16, const((tok, width))),
        ((width, 2 * width), jnp.bfloat16, const((width, 2 * width))),
    ]
    return chain_call(
        functools.partial(attend_out_kernel, len(pieces)),
        "attend_out",
        (1,),
        index,
        inputs,
        outputs,
        [],
        4.4,
    )


def cross_forward_kernel(head_size, stretches, pieces, index_ref, *refs):
    q_ref, enc_ref, rows_ref, keep_ref, gain_ref = refs[:5]
    refs = refs[5:]
    key_refs, value_refs = refs[:pieces], refs[pieces : 2 * pieces]
    out_refs, refs = refs[2 * pieces : 3 * pieces], refs[3 * pieces :]
    kv_ref, cross_ref, after_ref, norm_ref, wkv_ref, wout_ref = refs
    score_scale = head_size ** (-0.5)
    pair = pl.program_id(0)
    wide = q_ref.shape[1]
    fill(wkv_ref.at[0], key_refs, index_ref)
    fill(wkv_ref.at[1], value_refs, index_ref)
    kv_ref[0] = to_low(matmul(enc_ref[...], wkv_ref[0]))
    kv_ref[1] = to_low(matmul(enc_ref[...], wkv_ref[1]))

    @pl.when(pair == 0)
    def _():
        fill(wout_ref, out_refs, index_ref)

    keys = enc_ref.shape[0] // stretches
    sides = []
    for p in range(wide // PAIR):
        part = pl.ds(p * PAIR, PAIR)
        parts = []
        for s in range(stretches):
            span = pl.ds(s * keys, keys)
            query = head_rows(q_ref[pl.ds(s * STRETCH, STRETCH), part], head_size, score_scale)
            scores = right_product(kv_ref[0, span, part], query)
            weights = jnp.exp(scores - jnp.max(scores, axis=0, keepdims=True))
            probs = to_low(weights * (1.0 / jnp.sum(weights, axis=0, keepdims=True)))
            parts.append(join_heads(left_product(kv_ref[1, span, part], probs), head_size))
        sides.append(jnp.concatenate(parts, axis=0))
    columns = pl.ds(pl.multiple_of(pair * wide, wide), wide)
    cross_ref[:, columns] = to_low(jnp.concatenate(sides, axis=1))

    @pl.when(pair == pl.num_programs(0) - 1)
    def _():
        rows = rows_ref[...] + keep_ref[...] * matmul(cross_ref[...], wout_ref[...])
        after_ref[...] = rows
        norm_ref[...] = to_low(rows * inverse_rms(rows) * gain_ref[2:3, :])


def cross_forward(index, query, enc_rows, after_attn, keep_rows, gain_rows, pieces, stretches):
    tok, width = query.shape
    pairs = width // STEP
    keys = enc_rows.shape[0]
    inputs = [(query, pl.BlockSpec((tok, STEP), lambda i, _: (0, i)))]
    inputs += [(value, whole(value)) for value in (enc_rows, after_attn, keep_rows, gain_rows)]
    for first in (0, pairs):
        inputs += [
            (piece, pl.BlockSpec((piece.shape[0], STEP), lambda i, _, f=first: (0, f + i)))
            for piece in pieces
        ]
    inputs += [(piece, pl.BlockSpec((piece.shape[0], width), lambda i, _: (0, 2))) for piece in pieces]
    outputs = [
        ((2, keys, width), jnp.bfloat16, pl.BlockSpec((2, keys, STEP), lambda i, _: (0, 0, i))),
        ((tok, width), jnp.bfloat16, const((tok, width))),
        ((tok, width), jnp.float32, const((tok, width))),
        ((tok, width), jnp.bfloat16, const((tok, width))),
        ((2, width, width), jnp.bfloat16, pl.BlockSpec((2, width, STEP), lambda i, _: (0, 0, i))),
        ((width, width), jnp.bfloat16, const((width, width))),
    ]
    return chain_call(
        functools.partial(cross_forward_kernel, width // H, stretches, len(pieces)),
        "cross_forward",
        (pairs,),
        index,
        inputs,
        outputs,
        [],
        12.3,
    )


ERF_ABOVE = (
    -2.72614225801306e-10, 2.77068142495902e-08, -2.10102402082508e-06, -5.69250639462346e-05,
    -7.34990630326855e-04, -2.95459980854025e-03, -1.60960333262415e-02,
)
ERF_BELOW = (
    -1.45660718464996e-05, -2.13374055278905e-04, -1.68282697438203e-03, -7.37332916720468e-03,
    -1.42647390514189e-02,
)


def erf(values):
    values = jnp.clip(values, -4.0, 4.0)
    square = values * values
    above, below = ERF_ABOVE[0], ERF_BELOW[0]
    for factor in ERF_ABOVE[1:]:
        above = above * square + factor
    for factor in ERF_BELOW[1:]:
        below = below * square + factor
    return values * above / below


def mlp_kernel(tok, chunks, index_ref, *refs):
    norms, cot_ref, block_ref, exchanged, down_ref = refs[:4], refs[4], refs[5], refs[6:9], refs[9]
    grad_refs, out_own_ref, out_across_ref, out_send_ref = refs[10:14], refs[14], refs[15], refs[16]
    down_share_ref, keep_ref, send_ref, w_ref, held_ref, norm_all, cot_all, act_all, inner_all = refs[
        17:
    ]
    rows_in = block_ref.shape[0]
    starts = (0, 0, rows_in)
    blocks = [ref.at[pl.ds(start, rows_in), :] for ref, start in zip(exchanged, starts)]
    fill(w_ref, [block_ref, *blocks], index_ref)
    cot_all[pl.ds(0, tok), :] = cot_ref[...]
    for k, ref in enumerate(exchanged):
        start = ref.shape[0] - tok
        cot_all[pl.ds((k + 1) * tok, tok), :] = ref[pl.ds(start, tok), :]
    for k in range(4):
        norm_all[pl.ds(k * tok, tok), :] = norms[k][...]
    for k in range(2):
        rows = pl.ds(2 * k * tok, 2 * tok)
        inner = matmul(norm_all[rows, :], w_ref[...])
        share_below = 0.5 * (1.0 + erf(inner * (2.0**-0.5)))
        activation = to_low(inner * share_below)
        act_all[rows, :] = activation
        slope = share_below + inner * jnp.exp(-0.5 * inner * inner) * ((2.0 * jnp.pi) ** -0.5)
        grad_inner = to_low(right_product(cot_all[rows, :], down_ref[...]) * slope)
        inner_all[rows, :] = grad_inner
        grad = right_product(grad_inner, w_ref[...])
        out = matmul(activation, down_ref[...])
        grad_refs[2 * k][...] = grad[:tok].astype(grad_refs[2 * k].dtype)
        grad_refs[2 * k + 1][...] = to_low(grad[tok:])
        if k == 0:
            out_own_ref[...] = out[:tok]
        else:
            out_across_ref[...] = out[:tok]
        out_send_ref[k] = to_low(out[tok:])
    depth = down_ref.shape[0]
    held_ref[...] = left_product(act_all[...], cot_all[...])
    store_chunks(down_share_ref, 0, held_ref, 0, depth, index_ref[2], chunks[1])
    held_ref[...] = left_product(norm_all[...], inner_all[...])
    rows = depth // 4
    for out_ref, order in ((keep_ref, (0, 2)), (send_ref, (1, 3))):
        for k, j in enumerate(order):
            store_chunks(
                out_ref, k * rows, held_ref, (index_ref[0] ^ j) * rows, rows, index_ref[2], chunks[0]
            )


def mlp_share(index, norms, cot, block_own, exchanged, w_down):
    depth, width = w_down.shape
    tok = cot.shape[0]
    chunks = (chunk_count(width // len(WHOLE)), chunk_count(depth))
    inputs = [(value, whole(value)) for value in (*norms, cot, block_own, *exchanged, w_down)]
    token_f32 = ((tok, width), jnp.float32, const((tok, width)))
    token_low = ((tok, width), jnp.bfloat16, const((tok, width)))
    token_send = ((2, tok, width), jnp.bfloat16, const((2, tok, width)))
    rows = ((width // 2, depth), jnp.bfloat16, const((width // 2, depth)))
    outputs = [token_f32, token_low, token_low, token_low, token_f32, token_f32, token_send]
    outputs += [((depth, width), jnp.bfloat16, const((depth, width))), rows, rows]
    scratch = [pltpu.VMEM((width, depth), jnp.bfloat16), pltpu.VMEM((depth, depth), jnp.float32)]
    scratch += [pltpu.VMEM((4 * tok, depth), jnp.bfloat16)] * 4
    return chain_call(
        functools.partial(mlp_kernel, tok, chunks),
        "mlp_share",
        (1,),
        index,
        inputs,
        outputs,
        scratch,
        11.0,
    )


def inner_out_kernel(index_ref, own_ref, far_ref, weight_ref, gain_ref, out_ref, sum_ref):
    half = own_ref.shape[0]
    upper = index_ref[1] % 2
    own = own_ref[...].astype(jnp.float32)
    far = far_ref[...].astype(jnp.float32)
    out_ref[pl.ds(pl.multiple_of(upper * half, 8), half), :] = own
    out_ref[pl.ds(pl.multiple_of((1 - upper) * half, 8), half), :] = far
    part = jnp.sum(weight_ref[...].astype(jnp.float32) * out_ref[...], axis=1, keepdims=True)
    part = part / gain_ref[...]

    @pl.when(pl.program_id(0) == 0)
    def _():
        sum_ref[...] = part

    @pl.when(pl.program_id(0) > 0)
    def _():
        sum_ref[...] = sum_ref[...] + part


def inner_out(index, halves, weight, gain):
    own, far = halves
    rows, full = weight.shape
    depth = full // len(WHOLE)
    block = pl.BlockSpec((rows // 2, depth), lambda t, index_ref: (0, t ^ index_ref[0]))
    column = gain.astype(jnp.float32).reshape(rows, 1)
    inputs = [(own, block), (far, block)]
    inputs += [(weight, pl.BlockSpec((rows, depth), lambda t, _: (0, t))), (column, whole(column))]
    outputs = [
        ((rows, full), jnp.float32, pl.BlockSpec((rows, depth), lambda t, _: (0, t))),
        ((rows, 1), jnp.float32, const((rows, 1))),
    ]
    total, sums = chain_call(
        inner_out_kernel, "inner_out", (len(WHOLE),), index, inputs, outputs, [], 3.0
    )
    return total, sums.reshape(rows)


def cross_backward_kernel(head_size, stretches, index_ref, *refs):
    q_ref, kv_ref, cot_ref, cross_ref, wout_ref, keep_ref, w_ref, rows_ref, gain_ref = refs[:9]
    terms = refs[9:13]
    dq_ref, dkv_ref, out_ref, branch_ref, attended_ref, first_ref, grad_ref, do_ref = refs[13:]
    score_scale = head_size ** (-0.5)
    pair = pl.program_id(0)
    wide = q_ref.shape[1]
    keys = kv_ref.shape[1] // stretches

    @pl.when(pair == 0)
    def _():
        values = cross_ref[...]
        grad_norm = sum(term[...].astype(jnp.float32) for term in terms)
        grad = cot_ref[...].astype(jnp.float32) + rms_back(
            values, inverse_rms(values), gain_ref[2:3, :], grad_norm
        )
        grad_ref[...] = grad
        branch = to_low(keep_ref[...] * grad)
        first_ref[...] = branch
        do_ref[...] = to_low(right_product(branch, wout_ref[...]))

    sides = []
    for p in range(wide // PAIR):
        part = pl.ds(p * PAIR, PAIR)
        place = pl.ds(pl.multiple_of(pair * wide + p * PAIR, PAIR), PAIR)
        parts = []
        for s in range(stretches):
            rows = pl.ds(s * STRETCH, STRETCH)
            span = pl.ds(s * keys, keys)
            query = head_rows(q_ref[rows, part], head_size, score_scale)
            grad = head_rows(do_ref[rows, place], head_size)
            scores = right_product(kv_ref[0, span, part], query)
            weights = jnp.exp(scores - jnp.max(scores, axis=0, keepdims=True))
            probs = weights * (1.0 / jnp.sum(weights, axis=0, keepdims=True))
            dprobs = right_product(kv_ref[1, span, part], grad)
            delta = jnp.sum(probs * dprobs, axis=0, keepdims=True)
            dscores = to_low(probs * (dprobs - delta))
            dkv_ref[0, span, part] = to_low(matmul(dscores, query))
            dkv_ref[1, span, part] = to_low(matmul(to_low(probs), grad))
            parts.append(join_heads(left_product(kv_ref[0, span, part], dscores), head_size))
        sides.append(jnp.concatenate(parts, axis=0))
    columns = pl.ds(pl.multiple_of(pair * wide, wide), wide)
    dq_ref[:, columns] = to_low(score_scale * jnp.concatenate(sides, axis=1))

    @pl.when(pair == pl.num_programs(0) - 1)
    def _():
        width = rows_ref.shape[1]
        values = rows_ref[...]
        grad_norm = right_product(dq_ref[...], w_ref[:, width:])
        total = grad_ref[...] + rms_back(
            values, inverse_rms(values), gain_ref[1:2, :], grad_norm
        )
        out_ref[...] = total
        branch = to_low(total)
        branch_ref[...] = branch
        attended_ref[...] = to_low(right_product(branch, w_ref[:, :width]))


def cross_backward(
    index, query, key_value, cotangent, terms, after_cross, w_cout, keep_rows, w_pair, after_attn,
    gain_rows, stretches,
):
    tok, width = query.shape
    keys = key_value.shape[1]
    block = pl.BlockSpec((tok, STEP), lambda i, _: (0, i))
    planes = pl.BlockSpec((2, keys, STEP), lambda i, _: (0, 0, i))
    inputs = [(query, block), (key_value, planes), (cotangent, whole(cotangent))]
    inputs += [
        (value, whole(value))
        for value in (after_cross, w_cout, keep_rows, w_pair, after_attn, gain_rows, *terms)
    ]
    low = ((tok, width), jnp.bfloat16, const((tok, width)))
    outputs = [
        low,
        ((2, keys, width), jnp.bfloat16, planes),
        ((tok, width), jnp.float32, const((tok, width))),
        low,
        low,
        low,
    ]
    return chain_call(
        functools.partial(cross_backward_kernel, width // H, stretches),
        "cross_backward",
        (width // STEP,),
        index,
        inputs,
        outputs,
        [pltpu.VMEM((tok, width), jnp.float32), pltpu.VMEM((tok, width), jnp.bfloat16)],
        13.0,
    )


def swap(values, axis, bit):
    count = lax.axis_size(axis)
    return lax.ppermute(values, axis, [(i, i ^ bit) for i in range(count)])


def after(value, *earlier):
    return lax.optimization_barrier((value,) + earlier)[0]


def mirrored(position, count):
    out = 0
    for _ in range(count.bit_length() - 1):
        out, position = 2 * out + position % 2, position // 2
    return out


def positions_kernel(
    stretches, index_ref, deal_ref, lengths_ref, pos_ref, low_ref, high_ref, keep_ref
):
    ctx_index = index_ref[1]
    held = pos_ref.shape[0] // STRETCH
    offset = lax.broadcasted_iota(jnp.int32, (STRETCH, 1), 0)
    for s in range(held):
        device = ctx_index ^ mirrored(s // stretches, held // stretches)
        given = deal_ref[device * stretches + s % stretches]
        pos_ref[pl.ds(s * STRETCH, STRETCH), :] = given * STRETCH + offset
    lane = lax.broadcasted_iota(jnp.int32, low_ref.shape, 1) % (stretches * STRETCH)
    low_pos = jnp.zeros(low_ref.shape, jnp.int32)
    high_pos = jnp.zeros(low_ref.shape, jnp.int32)
    for s in range(stretches):
        given = deal_ref[ctx_index * stretches + s]
        start, end = 0, 0
        for q in range(lengths_ref.shape[0]):
            start = jnp.where(end <= given, end, start)
            end = end + lengths_ref[q]
        here = lane // STRETCH == s
        low_pos = jnp.where(here, start * STRETCH, low_pos)
        high_pos = jnp.where(here, given * STRETCH + lane % STRETCH, high_pos)
        kept = jnp.where(given != start, 1.0, 0.0).astype(jnp.float32)
        keep_ref[pl.ds(s * STRETCH, STRETCH), :] = jnp.full((STRETCH, 1), kept, jnp.float32)
    low_ref[...] = low_pos
    high_ref[...] = high_pos


def positions(index, deal_row, lengths_row, stretches):
    tok_count = stretches * STRETCH
    smem = pl.BlockSpec(memory_space=pltpu.SMEM)
    vmem = pl.BlockSpec(memory_space=pltpu.VMEM)
    return pl.pallas_call(
        functools.partial(positions_kernel, stretches),
        in_specs=[smem] * 3,
        out_specs=[vmem] * 4,
        out_shape=[
            jax.ShapeDtypeStruct((deal_row.shape[0] * STRETCH, 1), jnp.int32),
            jax.ShapeDtypeStruct((1, 2 * tok_count), jnp.int32),
            jax.ShapeDtypeStruct((1, 2 * tok_count), jnp.int32),
            jax.ShapeDtypeStruct((tok_count, 1), jnp.float32),
        ],
        cost_estimate=lasting(0.01),
        name="positions",
    )(index, deal_row, lengths_row)


def chunk_count(rows):
    count = lax.axis_size("ctx")
    return count if count & (count - 1) == 0 and rows % (8 * count) == 0 else 1


def store_chunks(out_ref, start, held_ref, base, rows, own_chunk, chunks):
    size = rows // chunks
    for p in range(chunks):
        place = base + (own_chunk ^ p) * size
        part = held_ref[pl.ds(pl.multiple_of(place, 8), size), :]
        out_ref[pl.ds(start + p * size, size), :] = part.astype(out_ref.dtype)


def products_kernel(tiles, rows, chunks, index_ref, *refs):
    count = len(tiles)
    inputs, (keep_ref, send_ref, held_ref) = refs[:-3], refs[-3:]
    fsdp_index, own_chunk = index_ref[0], index_ref[2]
    width = held_ref.shape[1]
    for t, (left, right, column) in enumerate(tiles):

        @pl.when(pl.program_id(0) == t)
        def _(left=left, right=right, column=column):
            grads = inputs[right][:, pl.ds(column * width, width)]
            held_ref[...] = left_product(inputs[left][...], grads)

    for out_ref, order in ((keep_ref, (0, 2)), (send_ref, (1, 3))):
        for k, j in enumerate(order):
            store_chunks(
                out_ref, k * rows, held_ref, (fsdp_index ^ j) * rows, rows, own_chunk, chunks
            )


def wide_products(index, terms, microseconds):
    shares = lax.axis_size("fsdp")
    inputs, tiles = [], []
    width = terms[0][0].shape[1]
    for left, right, plane in terms:
        count = right.shape[-2]
        if not any(left is value and count == held for value, held in inputs):
            inputs.append((left, count))
        first = next(i for i, (v, held) in enumerate(inputs) if v is left and held == count)
        inputs.append((right, plane))
        for column in range(right.shape[-1] // width):
            tiles.append((first, len(inputs) - 1, column))
    rows = width // shares
    chunks = chunk_count(rows)
    specs = []
    for value, plane in inputs:
        if value.ndim == 2:
            specs.append(pl.BlockSpec((plane or value.shape[0], value.shape[1]), lambda i, _: (0, 0)))
        else:
            specs.append(
                pl.BlockSpec((None,) + value.shape[1:], lambda i, _, plane=plane: (plane, 0, 0))
            )
    total = len(tiles) * width
    out = jax.ShapeDtypeStruct((2 * rows, total), jnp.bfloat16)
    out_spec = pl.BlockSpec((2 * rows, width), lambda i, _: (0, i))
    return pl.pallas_call(
        functools.partial(products_kernel, tiles, rows, chunks),
        grid_spec=pltpu.PrefetchScalarGridSpec(
            num_scalar_prefetch=1,
            grid=(len(tiles),),
            in_specs=specs,
            out_specs=[out_spec, out_spec],
            scratch_shapes=[pltpu.VMEM((width, width), jnp.float32)],
        ),
        out_shape=[out, out],
        cost_estimate=lasting(microseconds),
        name="wide_products",
    )(index, *[value for value, _ in inputs])


def add_low(*parts):
    return to_low(sum(part.astype(jnp.float32) for part in parts))


def reduction(keep, send):
    rows = keep.shape[0] // 2
    received = swap(send, "fsdp", 1)
    received = yield send, received
    sent = add_low(keep[rows:], received[rows:])
    across = swap(sent, "fsdp", 2)
    across = yield sent, across
    return (yield from ctx_reduction((keep[:rows], received[:rows], across)))


def in_order(index, bit, own, far):
    upper = (index & bit) != 0
    return jnp.concatenate([jnp.where(upper, far, own), jnp.where(upper, own, far)], axis=0)


def ctx_reduction(parts):
    index = lax.axis_index("ctx")
    half = parts[0].shape[0] // 2
    chunks = chunk_count(2 * half)
    if chunks == 1:
        share = lax.psum(add_low(*parts), "ctx")
        upper = (index & 1) != 0
        first, second = share[:half], share[half:]
        return jnp.where(upper, second, first), jnp.where(upper, first, second)
    bit = 1
    while bit < chunks:
        sent = add_low(*[part[half:] for part in parts])
        held = add_low(*[part[:half] for part in parts])
        far = swap(sent, "ctx", bit)
        parts = (held, (yield sent, far))
        half, bit = half // 2, 2 * bit
    gathered = add_low(*parts)
    while bit > 2:
        bit = bit // 2
        far = swap(gathered, "ctx", bit)
        far = yield gathered, far
        gathered = in_order(index, bit, gathered, far)
    far = swap(gathered, "ctx", 1)
    far = yield gathered, far
    return gathered, far


def finished(halves, offset, width):
    own, far = (half[:, offset : offset + width] for half in halves)
    return in_order(lax.axis_index("ctx"), 1, own, far).astype(jnp.float32)


def sum_to_owner(total):
    bit = 1
    while bit < lax.axis_size("ctx"):
        half = total.shape[0] // 2
        sent = total[half:]
        far = swap(sent, "ctx", bit)
        far = yield sent, far
        total = add_low(total[:half], far)
        bit = 2 * bit
    return total


class Steps:
    def __init__(self, steps):
        self.steps = steps
        self.result = None
        self.advance(None)

    def advance(self, arrived):
        try:
            sent, self.arriving = self.steps.send(arrived)
            return sent
        except StopIteration as stop:
            self.result = stop.value
            return stop.value[1] if isinstance(stop.value, tuple) else stop.value

    def hold(self, *token):
        if self.result is not None:
            return token[0]
        self.arriving = after(self.arriving, *token)
        return self.arriving

    def move(self, *token):
        return token[0] if self.result is not None else self.advance(self.hold(*token))

    def finish(self, *token):
        sent = token[0]
        while self.result is None:
            sent = self.move(sent)
        return sent


def gain_gradient(weight, grad, gain):
    return jnp.sum(weight.astype(jnp.float32) * grad, axis=1) / gain.astype(jnp.float32)


def local(
    hidden,
    neighbours,
    cotangent,
    stretch_deal,
    seq_lengths,
    norm_gains,
    attn_qkv,
    attn_out,
    cross_q,
    cross_kv,
    cross_out,
    mlp_in,
    mlp_out,
):
    shares = lax.axis_size("fsdp")
    fsdp_index = lax.axis_index("fsdp")
    ctx_index = lax.axis_index("ctx")
    ctx_count = lax.axis_size("ctx")
    own_chunk, bit = 0 * ctx_index, 1
    while bit < ctx_count:
        own_chunk = 2 * own_chunk + (ctx_index & bit) // bit
        bit = 2 * bit
    place = jnp.stack([fsdp_index, ctx_index, own_chunk]).astype(jnp.int32)
    feature_width = hidden.shape[2]
    own = hidden[0]
    tok = own.shape[0]
    stretch_count = tok // STRETCH
    enc_rows = neighbours[0].reshape(-1, feature_width)
    cot = cotangent[0]

    key_pos, low_pos, high_pos, keep_rows = positions(
        place, stretch_deal[0], seq_lengths[0], stretch_count
    )

    first_share = jnp.concatenate(
        [attn_qkv, jnp.pad(norm_gains.T, ((0, 0), (0, 128 - norm_gains.shape[0])))], axis=1
    )
    across_qkv = swap(first_share, "fsdp", 2)
    if ctx_count == 8:
        far, last, near = swap(own, "ctx", 4), swap(own, "ctx", 6), swap(own, "ctx", 2)
        beside = swap(own, "ctx", 1)
        beside_near = swap(near, "ctx", 1)
        second = after(jnp.concatenate([far, last], axis=0), near)
        row_pieces = [own, near, second, beside, beside_near, swap(second, "ctx", 1)]
        layout = [[k * tok for k in ks] for ks in ((0,), (2,), (1, 3), (4,), (6,), (5, 7))]
        second = after(second, beside)
    else:
        first = own
        bit = ctx_count
        while bit > 2:
            bit = bit // 2
            first = jnp.concatenate([first, swap(first, "ctx", bit)], axis=0)
        row_pieces = [first, swap(first, "ctx", 1)]
        layout = [[k * first.shape[0]] for k in range(2)]
        second = first
    sibling_qkv = swap(after(first_share, second), "fsdp", 1)
    across_qkv = after(across_qkv, second)
    diagonal_qkv = swap(across_qkv, "fsdp", 1)
    pair_share = jnp.concatenate([attn_out, cross_q], axis=1)
    across_pair = swap(after(pair_share, second), "fsdp", 2)
    cross_share = jnp.concatenate([cross_kv, cross_out], axis=1)
    across_cross = swap(after(cross_share, second), "fsdp", 2)
    depth = mlp_out.shape[0]
    rows_in = mlp_in.shape[0]

    def block_of(j):
        return lax.dynamic_slice_in_dim(mlp_in, (fsdp_index ^ j) * depth, depth, axis=1)

    block_own = block_of(0)
    exchange_sibling = jnp.concatenate([block_of(1), cot], axis=0)
    exchange_across = jnp.concatenate([block_of(2), block_of(3), cot], axis=0)

    rows_all, scale_all = held_rows(row_pieces, layout)
    query, key_value, norm_all, w_qkv, gain_rows = project(
        place,
        rows_all,
        scale_all,
        [first_share, sibling_qkv, across_qkv, after(diagonal_qkv, scale_all)],
        tok,
    )
    across_pair = after(across_pair, query)
    diagonal_pair = swap(across_pair, "fsdp", 1)
    sibling_pair = swap(after(pair_share, query), "fsdp", 1)
    from_across = swap(after(exchange_across, across_pair), "fsdp", 2)
    attended, log_total = self_forward(query, key_value, key_pos, low_pos, high_pos)
    sibling_cross = swap(after(cross_share, attended), "fsdp", 1)
    across_cross = after(across_cross, attended)
    after_attn, norm_two, cross_query, w_pair = attend_out(
        place, attended, own, gain_rows, [pair_share, sibling_pair, across_pair, diagonal_pair]
    )
    diagonal_cross = swap(across_cross, "fsdp", 1)
    cross_key_value, cross_rows, after_cross, norm_three, w_ckv, w_cout = cross_forward(
        place,
        cross_query,
        enc_rows,
        after_attn,
        keep_rows,
        gain_rows,
        [cross_share, sibling_cross, across_cross, diagonal_cross],
        stretch_count,
    )
    from_sibling = swap(after(exchange_sibling, cross_query), "fsdp", 1)
    norm_across, norm_sibling = swap(norm_three, "fsdp", 2), swap(norm_three, "fsdp", 1)
    from_across = after(from_across, norm_three)
    from_diagonal = swap(from_across, "fsdp", 1)
    norm_diagonal = swap(norm_across, "fsdp", 1)
    (
        grad_own, grad_sibling, grad_across, grad_diagonal, out_own, out_across, out_send, share_down,
        keep_in, send_in,
    ) = mlp_share(
        place,
        [norm_three, norm_sibling, norm_across, norm_diagonal],
        cot,
        block_own,
        [from_sibling, from_across, from_diagonal],
        mlp_out,
    )

    terms = (
        grad_own,
        swap(grad_sibling, "fsdp", 1),
        swap(grad_across, "fsdp", 2),
        swap(grad_diagonal, "fsdp", 3),
    )
    received_in = swap(send_in, "fsdp", 1)
    across_in = swap(
        jnp.concatenate([keep_in[rows_in:], received_in[rows_in:]], axis=1), "fsdp", 2
    )
    down = Steps(ctx_reduction((share_down,)))
    (
        grad_cross_query, grad_cross_pair, grad_after_attn, grad_attn_branch, grad_attended,
        grad_cross_branch,
    ) = cross_backward(
        place,
        cross_query,
        cross_key_value,
        cot,
        terms,
        after_cross,
        w_cout,
        keep_rows,
        w_pair,
        after_attn,
        gain_rows,
        stretch_count,
    )
    across_in = after(across_in, grad_attended)
    out_sibling = swap(after(out_send, grad_attended), "fsdp", 1)
    arrived = down.hold(grad_attended)
    keep_cross, send_cross = wide_products(
        place,
        [
            (cross_rows, grad_cross_branch, None),
            (norm_two, grad_cross_query, None),
            (enc_rows, after(grad_cross_pair, across_in, arrived), 0),
            (enc_rows, grad_cross_pair, 1),
            (attended, grad_attn_branch, None),
        ],
        8.2,
    )
    cross = Steps(reduction(keep_cross, send_cross))
    ready = down.move(keep_cross)
    share_in = jnp.concatenate(
        [keep_in[:rows_in], received_in[:rows_in], after(across_in, ready)], axis=1
    )
    inner = Steps(ctx_reduction((share_in,)))
    ready = cross.move(share_in)
    grad_query, grad_pair = self_backward(
        query,
        key_value,
        after(grad_attended, ready),
        key_pos,
        low_pos,
        high_pos,
        log_total,
    )
    out_sibling = after(out_sibling, grad_query)
    out_far = swap(add_low(out_across, out_sibling[1]), "fsdp", 2)
    ready = inner.move(down.move(grad_query))
    keep_attn, send_attn = wide_products(
        place,
        [
            (norm_all, after(grad_query, ready), None),
            (norm_all, grad_pair, 0),
            (norm_all, grad_pair, 1),
        ],
        0.01,
    )
    attn = Steps(reduction(keep_attn, send_attn))
    norm1_all, norm1_query = norm_terms(place, after(grad_pair, keep_attn), grad_query, w_qkv)
    ready = cross.move(norm1_all)
    grad_enc = enc_terms(place, after(grad_cross_pair, ready), w_ckv)
    ready = attn.move(grad_enc)
    layer_out = after_cross + (
        out_own + out_sibling[0].astype(jnp.float32) + after(out_far, ready).astype(jnp.float32)
    )
    ready = down.move(ready, layer_out)
    for step in (inner, cross, down, inner, attn):
        ready = step.move(ready)
    norm1 = Steps(sum_to_owner(after(norm1_all, ready)))
    for step in (cross, attn, down, inner, cross, norm1, attn, inner, cross, norm1, attn):
        ready = step.move(ready)
    ready = norm1.finish(ready)
    input_rows = own.astype(jnp.float32)
    grad_norm1 = norm1.result.astype(jnp.float32) + norm1_query
    grad_input = grad_after_attn + rms_back(
        input_rows, inverse_rms(input_rows), after(gain_rows, ready)[0:1], grad_norm1
    )
    ready = cross.move(ready)
    ready = attn.move(down.finish(ready), grad_input)
    total_down = finished(down.result, 0, feature_width)
    ready = inner.finish(after(ready, total_down))
    ready = attn.move(ready)
    total_in, gain_three = inner_out(place, inner.result, mlp_in, norm_gains[2])
    cross.move(ready, total_in)
    ready = cross.finish(ready)
    d = feature_width
    total_cout = finished(cross.result, 0, d)
    total_cq = finished(cross.result, d, d)
    total_ckv = finished(cross.result, 2 * d, 2 * d)
    total_out = finished(cross.result, 4 * d, d)
    gain_two = gain_gradient(cross_q, total_cq, norm_gains[1])
    attn.move(ready, total_cout, total_ckv, total_out, gain_two)
    attn.finish(ready)
    total_qkv = finished(attn.result, 0, 3 * d)
    gain_one = gain_gradient(attn_qkv, total_qkv, norm_gains[0])
    grad_gains = jnp.stack([gain_one, gain_two, gain_three])
    return (
        layer_out[None],
        grad_input[None],
        grad_enc.reshape(neighbours.shape),
        grad_gains,
        total_qkv,
        total_out,
        total_cq,
        total_ckv,
        total_cout,
        total_in,
        total_down,
    )


def solution(mesh):
    return jax.shard_map(
        local,
        mesh=mesh,
        in_specs=(
            P("fsdp", "ctx", None),
            P("fsdp", "ctx", None, None),
            P("fsdp", "ctx", None),
            P("fsdp", None),
            P("fsdp", None),
            P(None, "fsdp"),
            P("fsdp", None),
            P("fsdp", None),
            P("fsdp", None),
            P("fsdp", None),
            P("fsdp", None),
            P("fsdp", None),
            P("fsdp", None),
        ),
        out_specs=(
            P("fsdp", "ctx", None),
            P("fsdp", "ctx", None),
            P("fsdp", "ctx", None, None),
            P(None, "fsdp"),
            P("fsdp", None),
            P("fsdp", None),
            P("fsdp", None),
            P("fsdp", None),
            P("fsdp", None),
            P("fsdp", None),
            P("fsdp", None),
        ),
        check_vma=False,
    )
```
